32 devices in a mesh: dom: 8 (over z, x), feat: 4 (over y, core).
Axes of the slice: x: 2, y: 2, z: 4, core: 2. Of those that a mesh axis runs over, the one named last changes fastest.
Arguments:
- node_feats: bfloat16 [16384, 512], P('dom', 'feat'), may hold values from -6 to 6
- edge_tiles: bfloat16 [848, 128, 128], P('dom'), may hold values from -0.14941406 to 0.14941406
- tile_dst: int32 [848], P('dom'), may hold values from 0 to 15, as said below
- tile_src: int32 [848], P('dom'), may hold values from 0 to 25, as said below
- hub_ids: int32 [256], P('dom'), may hold values from 0 to 2047, as said below
- send_rows: int32 [8, 8, 128], P('dom'), may hold values from 0 to 2047
- send_count: int32 [8, 8], P('dom'), may hold values from 32 to 128, as said below
- w_self: bfloat16 [512, 512], P(None, 'feat'), may hold values from -0.25 to 0.25
- w_neigh: bfloat16 [512, 512], P(None, 'feat'), may hold values from -0.25 to 0.25
- out_bias: float32 [512], P('feat'), may hold values from -3 to 3
- grad_out: bfloat16 [16384, 512], P('dom', 'feat'), may hold values from -6 to 6
Outputs:
- output: bfloat16 [16384, 512], P('dom', 'feat')
- grad_feats: float32 [16384, 512], P('dom', 'feat')
- grad_self: float32 [512, 512], P(None, 'feat')
- grad_neigh: float32 [512, 512], P(None, 'feat')
- grad_bias: float32 [512], P('feat')
The draws below stay inside these ranges and needn't reach their ends.
Inputs may be any that keep to these rules, and one draw needn't show every extreme that they name: `tile_dst`: every one of the 16 blocks of a partition receives at least 5 of its tiles. `tile_src`: source blocks of a partition: its own rows, then all hub rows, then received rows in order of sender; every block is read by at least one tile of every partition. `hub_ids`: distinct within each partition. `send_count`: every partition sends exactly 128 rows to at least one partition, and some partition receives exactly 128 rows from every partition.
All inputs are finite; a program needn't handle non-finite values.
Results may differ from the reference program's by a relative error of at most 0.0055.
Values may be sent and summed in bfloat16 or wider, within the bound.
No kernel may reach another device: no remote copies, remote signals or barrier semaphores. Data moves between devices by JAX's collectives and lax.ppermute only.
A program may use at most 128 MiB of HBM per device.

```python
import jax
import jax.numpy as jnp
from jax import lax

F = 512
H = 512
TILE = 128
V_DEV = 2048
HUB_DEV = 32
CAP = 128
V = 16384
HUBS = 256
ROW_BLOCKS = 16
SRC_BLOCKS = 26
TILES = 106
N_DOM = 8


def draw_tile_src(key, part):
    key_list = jax.random.split(jax.random.fold_in(key, 11), N_DOM)

    def single(inner_key):
        first, second = jax.random.split(inner_key)
        extra_rows = jax.random.randint(first, (TILES - SRC_BLOCKS,), 0, SRC_BLOCKS).astype(jnp.int32)
        listed = jnp.concatenate([jnp.arange(SRC_BLOCKS, dtype=jnp.int32), extra_rows])
        return jax.random.permutation(second, listed)
    return jax.vmap(single)(key_list).reshape(-1).astype(jnp.int32)


def draw_tile_dst(key, part):
    key_list = jax.random.split(jax.random.fold_in(key, 23), N_DOM)

    def single(inner_key):
        first, second = jax.random.split(inner_key)
        random_part = jax.random.randint(first, (SRC_BLOCKS,), 0, ROW_BLOCKS).astype(jnp.int32)
        cyclic = (jnp.arange(TILES - SRC_BLOCKS, dtype=jnp.int32) % ROW_BLOCKS).astype(jnp.int32)
        listed = jnp.concatenate([random_part, cyclic])
        return jax.random.permutation(second, listed)
    return jax.vmap(single)(key_list).reshape(-1).astype(jnp.int32)


def draw_hub_ids(key, part):
    key_list = jax.random.split(jax.random.fold_in(key, 37), N_DOM)

    def single(inner_key):
        return jax.random.permutation(inner_key, V_DEV)[:HUB_DEV].astype(jnp.int32)
    return jax.vmap(single)(key_list).reshape(-1).astype(jnp.int32)


def draw_send_count(key, part):
    first, second, key_three, fourth = jax.random.split(jax.random.fold_in(key, 41), 4)
    base_count = jax.random.randint(first, (N_DOM, N_DOM), CAP // 4, CAP // 2 + 1)
    hot_pair = jax.random.randint(second, (N_DOM, N_DOM), 0, 4) == 0
    offsets = jax.random.randint(key_three, (N_DOM,), 1, N_DOM)
    column = jnp.arange(N_DOM, dtype=jnp.int32)
    target = (column + offsets) % N_DOM
    row_hot = column[None, :] == target[:, None]
    full_column = jax.random.randint(fourth, (), 0, N_DOM)
    column_hot = column[None, :] == full_column
    return jnp.where(hot_pair | row_hot | column_hot, CAP, base_count).astype(jnp.int32)


def plant(array, stream_key, least, largest):
    longest = array.shape.index(max(array.shape))
    spots = []
    for shift in (0, 1):
        where = [jax.random.randint(jax.random.fold_in(stream_key, axis), (), 0, length) for axis, length in enumerate(array.shape)]
        where[longest] = (where[longest] + shift) % array.shape[longest]
        spots.append(tuple(where))
    return array.at[spots[0]].set(least).at[spots[1]].set(largest)


def shard_levels(rng, dims, cuts, least, largest):
    def one(axis_at, parts):
        steps = jax.random.uniform(jax.random.fold_in(jax.random.fold_in(rng, 6), axis_at), (parts,), jnp.float32, least / len(cuts), largest / len(cuts))
        return jnp.repeat(jnp.exp(steps), dims[axis_at] // parts).reshape((-1,) + (1,) * (len(dims) - axis_at - 1))

    gain = one(*cuts[0])
    for cut in cuts[1:]:
        gain = gain * one(*cut)
    return gain


def centred(stream_key, extent, scale, most, pieces=(), held_as=jnp.bfloat16):
    array = scale * jax.random.normal(stream_key, extent, jnp.float32)
    if pieces:
        array = array * shard_levels(stream_key, extent, pieces, -0.22, 0.18)
    return jnp.clip(array, -most, most).astype(held_as)


def setup_inputs(seed: int = 0) -> dict:
    splits = jax.random.split(jax.random.key(seed), 12)
    node_feats = centred(splits[0], (V, F), 1.0, 6.0, ((0, 8), (1, 4)))
    edge_tiles = centred(splits[1], (N_DOM * TILES, TILE, TILE), 0.025, 0.14941406, ((0, 8),))
    tile_dst = draw_tile_dst(jax.random.fold_in(splits[11], 71), 0)
    tile_src = draw_tile_src(jax.random.fold_in(splits[11], 71), 0)
    hub_ids = draw_hub_ids(jax.random.fold_in(splits[11], 71), 0)
    send_rows = plant(jax.random.randint(splits[5], (N_DOM, N_DOM, CAP), 0, V_DEV), jax.random.fold_in(splits[5], 1), 0, V_DEV - 1).astype(jnp.int32)
    send_count = draw_send_count(jax.random.fold_in(splits[11], 71), 0)
    w_self = centred(splits[7], (F, H), F ** -0.5, 0.25, ((1, 4),))
    w_neigh = centred(splits[8], (F, H), F ** -0.5, 0.25, ((1, 4),))
    out_bias = centred(splits[9], (H,), 0.5, 3.0, ((0, 4),), jnp.float32)
    grad_out = centred(splits[10], (V, H), 1.0, 6.0, ((0, 8), (1, 4)))
    return {"node_feats": node_feats, "edge_tiles": edge_tiles, "tile_dst": tile_dst, "tile_src": tile_src, "hub_ids": hub_ids, "send_rows": send_rows, "send_count": send_count, "w_self": w_self, "w_neigh": w_neigh, "out_bias": out_bias, "grad_out": grad_out}


def reference(node_feats, edge_tiles, tile_dst, tile_src, hub_ids, send_rows, send_count, w_self, w_neigh, out_bias, grad_out):
    tile_size = edge_tiles.shape[1]
    width = node_feats.shape[1]
    owners = jnp.arange(N_DOM, dtype=jnp.int32)
    hub_vertex = (owners[:, None] * V_DEV + hub_ids.reshape(N_DOM, HUB_DEV)).reshape(-1).astype(jnp.int32)
    hub_table = node_feats[hub_vertex]
    slot_ids = jnp.arange(CAP, dtype=jnp.int32)
    tile_sets = edge_tiles.reshape(N_DOM, TILES, tile_size, tile_size)
    dst_sets = tile_dst.reshape(N_DOM, TILES)
    src_sets = tile_src.reshape(N_DOM, TILES)

    def boundary(partner):
        vertex = (owners[:, None] * V_DEV + send_rows[:, partner, :]).astype(jnp.int32)
        filled = slot_ids[None, :] < send_count[:, partner][:, None]
        return vertex, filled

    def forward(partner):
        vertex, filled = boundary(partner)
        received = jnp.where(filled[:, :, None], node_feats[vertex], jnp.zeros((), node_feats.dtype)).reshape(-1, width)
        own_rows = lax.dynamic_slice_in_dim(node_feats, (partner * V_DEV).astype(jnp.int32), V_DEV, 0)
        source = jnp.concatenate([own_rows, hub_table, received], axis=0).reshape(SRC_BLOCKS, tile_size, width)
        products = jnp.einsum("tij,tjf->tif", tile_sets[partner].astype(jnp.float32), source[src_sets[partner]].astype(jnp.float32))
        summed = jax.ops.segment_sum(products, dst_sets[partner], ROW_BLOCKS)
        return summed.reshape(V_DEV, width).astype(jnp.bfloat16)

    aggregated = lax.map(forward, owners).reshape(V, width)
    pre_act = jnp.dot(node_feats, w_self, preferred_element_type=jnp.float32) + jnp.dot(aggregated, w_neigh, preferred_element_type=jnp.float32) + out_bias
    gate_sig = jax.nn.sigmoid(pre_act)
    output = (pre_act * gate_sig).astype(jnp.bfloat16)
    grad_pre = (grad_out.astype(jnp.float32) * gate_sig * (1.0 + pre_act * (1.0 - gate_sig))).astype(jnp.bfloat16)
    grad_self = jnp.dot(node_feats.T, grad_pre, preferred_element_type=jnp.float32)
    grad_neigh = jnp.dot(aggregated.T, grad_pre, preferred_element_type=jnp.float32)
    grad_bias = jnp.sum(grad_pre.astype(jnp.float32), axis=0)
    direct = jnp.dot(grad_pre, w_self.T, preferred_element_type=jnp.float32)
    back_agg = jnp.dot(grad_pre, w_neigh.T, preferred_element_type=jnp.float32).astype(jnp.bfloat16)

    def backward(state, partner):
        grad_acc, hub_sum = state
        vertex, filled = boundary(partner)
        offset = (partner * V_DEV).astype(jnp.int32)
        local_rows = lax.dynamic_slice_in_dim(back_agg, offset, V_DEV, 0).reshape(ROW_BLOCKS, tile_size, width)
        spread = jnp.einsum("tji,tjf->tif", tile_sets[partner].astype(jnp.float32), local_rows[dst_sets[partner]].astype(jnp.float32))
        back_source = jax.ops.segment_sum(spread, src_sets[partner], SRC_BLOCKS).reshape(-1, width)
        own_part = back_source[:V_DEV]
        hub_part = back_source[V_DEV:V_DEV + HUBS]
        recv_part = back_source[V_DEV + HUBS:].reshape(N_DOM, CAP, width)
        updated = lax.dynamic_slice_in_dim(grad_acc, offset, V_DEV, 0) + own_part
        grad_acc = lax.dynamic_update_slice_in_dim(grad_acc, updated, offset, 0)
        returned = jnp.where(filled[:, :, None], recv_part, jnp.zeros((), recv_part.dtype)).reshape(-1, width)
        grad_acc = grad_acc.at[vertex.reshape(-1)].add(returned)
        return (grad_acc, hub_sum + hub_part), None

    start_state = (direct, jnp.zeros((HUBS, width), jnp.float32))
    (grad_feats, hub_sum), ignored = lax.scan(backward, start_state, owners)
    grad_feats = grad_feats.at[hub_vertex].add(hub_sum)
    return (output, grad_feats, grad_self, grad_neigh, grad_bias)
```

```python
import jax
import jax.numpy as jnp
from jax import lax
from jax.sharding import PartitionSpec as P

F32 = jnp.float32
BF16 = jnp.bfloat16


def body(
    node_feats,
    edge_tiles,
    tile_dst,
    tile_src,
    hub_ids,
    send_rows,
    send_count,
    w_self,
    w_neigh,
    out_bias,
    grad_out,
    *,
    n_feat,
):
    own_count, width = node_feats.shape
    tile_size = edge_tiles.shape[1]
    n_dom, capacity = send_rows.shape[1], send_rows.shape[2]
    hub_dev = hub_ids.shape[0]
    me = lax.axis_index("feat")
    order = me ^ jnp.arange(n_feat, dtype=jnp.int32)

    def swap(x, k):
        return lax.ppermute(x, "feat", [(j, j ^ k) for j in range(n_feat)])

    def gather_feat(x):
        shards = {0: x}
        bit = n_feat // 2
        while bit:
            for k in list(shards):
                shards[k ^ bit] = swap(shards[k], bit)
            bit //= 2
        return [shards[k] for k in range(n_feat)]

    whole_feats = jnp.concatenate(gather_feat(node_feats), axis=1)

    listed = send_rows[0]
    slots = jnp.arange(capacity, dtype=jnp.int32)
    filled = slots[None, :] < send_count[0][:, None]
    index = jnp.concatenate(
        [listed, jnp.broadcast_to(hub_ids[None, :], (n_dom, hub_dev))], axis=1
    )
    keep = jnp.concatenate([filled, jnp.ones((n_dom, hub_dev), bool)], axis=1)
    outgoing = jnp.where(keep[:, :, None], node_feats[index], jnp.zeros((), BF16))
    incoming = lax.all_to_all(outgoing, "dom", 0, 0, tiled=True)
    source = jnp.concatenate(
        [
            node_feats,
            incoming[:, capacity:].reshape(-1, width),
            incoming[:, :capacity].reshape(-1, width),
        ],
        axis=0,
    )
    source_blocks = source.shape[0] // tile_size
    row_blocks = own_count // tile_size
    blocks = source.reshape(source_blocks, tile_size, width)
    products = jnp.einsum("tij,tjf->tif", edge_tiles, blocks[tile_src], preferred_element_type=F32)
    summed = jax.ops.segment_sum(products, tile_dst, row_blocks)
    aggregated = summed.reshape(own_count, width).astype(BF16)

    whole_agg = jnp.concatenate(gather_feat(aggregated), axis=1)
    ws = w_self.reshape(n_feat, width, -1)[order].reshape(-1, w_self.shape[1])
    wn = w_neigh.reshape(n_feat, width, -1)[order].reshape(-1, w_self.shape[1])
    pre_act = (
        jnp.dot(whole_feats, ws, preferred_element_type=F32)
        + jnp.dot(whole_agg, wn, preferred_element_type=F32)
        + out_bias
    )
    gate_sig = jax.nn.sigmoid(pre_act)
    output = (pre_act * gate_sig).astype(BF16)
    grad_pre = (grad_out.astype(F32) * gate_sig * (1.0 + pre_act * (1.0 - gate_sig))).astype(BF16)

    whole_grad = jnp.concatenate(gather_feat(grad_pre), axis=1)

    contract_rows = (((0,), (0,)), ((), ()))
    part_self = lax.dot_general(whole_feats, grad_pre, contract_rows, preferred_element_type=F32)
    part_neigh = lax.dot_general(whole_agg, grad_pre, contract_rows, preferred_element_type=F32)
    part_bias = jnp.sum(grad_pre.astype(F32), axis=0, keepdims=True)
    parts = jnp.stack([part_self, part_neigh]).reshape(n_dom, -1, width)
    chunk = parts.shape[1]
    parts = jnp.concatenate([parts, jnp.broadcast_to(part_bias[None], (n_dom, 8, width))], axis=1)
    summed_w = jnp.sum(lax.all_to_all(parts, "dom", 0, 0, tiled=True), axis=0)
    grad_bias = summed_w[chunk]
    weights_out = summed_w[:chunk].astype(BF16)

    both = jnp.stack([w_self, w_neigh]).reshape(2, n_feat, width, -1)[:, order]
    rows = lax.concatenate(
        [both[:, 0:1]] + [swap(both[:, k : k + 1], k) for k in range(1, n_feat)], 1
    )
    contract_last = (((1,), (2,)), ((), ()))

    def back(w):
        return lax.dot_general(
            whole_grad,
            w.transpose(1, 0, 2).reshape(width, -1),
            (((1,), (1,)), ((), ())),
            preferred_element_type=F32,
        )

    direct = back(rows[0])
    back_agg = back(rows[1]).astype(BF16)
    back_blocks = back_agg.reshape(row_blocks, tile_size, width)[tile_dst]
    spread = jnp.einsum("tji,tjf->tif", edge_tiles, back_blocks, preferred_element_type=F32)
    back_source = jax.ops.segment_sum(spread, tile_src, source_blocks).reshape(-1, width)
    hub_total = n_dom * hub_dev
    hub_part = back_source[own_count : own_count + hub_total].reshape(n_dom, hub_dev, width)
    recv_part = back_source[own_count + hub_total :].reshape(n_dom, capacity, width)
    back_out = jnp.concatenate(
        [
            recv_part.astype(BF16),
            hub_part.astype(BF16),
            jnp.broadcast_to(weights_out[None], (n_dom, chunk, width)),
        ],
        axis=1,
    )
    back_in = lax.all_to_all(back_out, "dom", 0, 0, tiled=True)
    weights_in = back_in[:, capacity + hub_dev :].reshape(2, n_feat, width, -1)[:, order]
    grads = weights_in.astype(F32).reshape(2, n_feat * width, -1)
    rows_in = back_in[:, : capacity + hub_dev].astype(F32)
    rows_in = jnp.where(keep[:, :, None], rows_in, 0.0)
    grad_feats = direct + back_source[:own_count]
    grad_feats = grad_feats.at[index.reshape(-1)].add(rows_in.reshape(-1, width))
    return (output, grad_feats, grads[0], grads[1], grad_bias)


def solution(mesh):
    in_specs = (
        P("dom", "feat"),
        P("dom", None, None),
        P("dom"),
        P("dom"),
        P("dom"),
        P("dom", None, None),
        P("dom", None),
        P(None, "feat"),
        P(None, "feat"),
        P("feat"),
        P("dom", "feat"),
    )
    out_specs = (P("dom", "feat"), P("dom", "feat"), P(None, "feat"), P(None, "feat"), P("feat"))
    n_feat = mesh.shape["feat"]

    def run(*args):
        return body(*args, n_feat=n_feat)

    return jax.shard_map(run, mesh=mesh, in_specs=in_specs, out_specs=out_specs, check_vma=False)
```

```python
import functools

import jax
import jax.numpy as jnp
from jax import lax
from jax.experimental import pallas as pl
from jax.experimental.pallas import tpu as pltpu
from jax.sharding import PartitionSpec as P

F32 = jnp.float32
BF16 = jnp.bfloat16
VMEM = pl.BlockSpec(memory_space=pltpu.VMEM)
SMEM = pl.BlockSpec(memory_space=pltpu.SMEM)
UNROLL = 8
T_BITS, S_BITS = 10, 10


def params(mib):
    return pltpu.CompilerParams(vmem_limit_bytes=mib << 20)


def cost(flops, nbytes):
    return pl.CostEstimate(flops=flops, bytes_accessed=nbytes, transcendentals=0)


def pick_kernel(rows_s, count_s, hub_s, x, out, x32, stage):
    n_dom, capacity = rows_s.shape
    hub_dev = hub_s.shape[0]
    step = 16
    x32[...] = x[...].astype(F32)
    for j in range(hub_dev):
        stage[capacity + j : capacity + j + 1, :] = x32[pl.ds(hub_s[j], 1), :]
    hub = stage[capacity:, :].astype(BF16)
    slot = lax.broadcasted_iota(jnp.int32, (capacity, x.shape[1]), 0)

    def peer(q, carry):
        def some(g, carry):
            for u in range(step):
                c = g * step + u
                stage[pl.ds(c, 1), :] = x32[pl.ds(rows_s[q, c], 1), :]
            return carry

        lax.fori_loop(0, capacity // step, some, 0)
        kept = jnp.where(slot < count_s[0, q], stage[:capacity, :], 0.0)
        out[q, :capacity, :] = kept.astype(BF16)
        out[q, capacity:, :] = hub
        return carry

    lax.fori_loop(0, n_dom, peer, 0)


def pick(send_rows, send_count, hub_ids, x):
    n_dom, capacity = send_rows.shape
    rows = capacity + hub_ids.shape[0]
    return pl.pallas_call(
        pick_kernel,
        out_shape=jax.ShapeDtypeStruct((n_dom, rows, x.shape[1]), BF16),
        in_specs=[SMEM, SMEM, SMEM, VMEM],
        out_specs=VMEM,
        scratch_shapes=[pltpu.VMEM(x.shape, F32), pltpu.VMEM((rows, x.shape[1]), F32)],
        compiler_params=params(16),
        cost_estimate=cost(0, 1 << 21),
        name="pick_rows",
    )(send_rows, send_count, hub_ids, x)


def unpack(entry):
    t = entry & ((1 << T_BITS) - 1)
    s = (entry >> T_BITS) & ((1 << S_BITS) - 1)
    return t, s, entry >> (T_BITS + S_BITS)


def make_lists(dst_s, src_s, lists, own_blocks, far_blocks):
    length = lists.shape[1] - 1

    def step(t, n):
        s = src_s[t]
        d = dst_s[t]
        far = (s >= own_blocks).astype(jnp.int32)
        lists[0, n[0]] = t + (s << T_BITS) + (d << (T_BITS + S_BITS))
        lists[1, n[1]] = t + ((s - own_blocks) << T_BITS) + (d << (T_BITS + S_BITS))
        return n[0] + 1 - far, n[1] + far

    n = lax.fori_loop(0, dst_s.shape[0], step, (jnp.int32(0), jnp.int32(0)))
    for which, blocks in ((0, own_blocks), (1, far_blocks)):
        spare = (blocks << T_BITS) + (own_blocks << (T_BITS + S_BITS))
        for u in range(UNROLL - 1):
            lists[which, n[which] + u] = jnp.int32(spare)
        lists[which, length] = n[which]


def add_tiles(lists, which, tiles, source, acc, spare):
    n = lists[which, lists.shape[1] - 1]

    def group(g, carry):
        done = []
        for u in range(UNROLL):
            t, s, d = unpack(lists[which, g * UNROLL + u])
            s = jnp.where(d == spare, 0, s)
            done.append((d, jnp.dot(tiles[t], source[s], preferred_element_type=F32)))
        for d, product in done:
            acc[d] += product
        return carry

    lax.fori_loop(0, (n + UNROLL - 1) // UNROLL, group, 0)


def add_tiles_t(lists, which, tiles, source, acc, spare):
    n = lists[which, lists.shape[1] - 1]

    def group(g, carry):
        done = []
        for u in range(UNROLL):
            t, s, d = unpack(lists[which, g * UNROLL + u])
            d = jnp.where(d == spare, 0, d)
            product = lax.dot_general(
                tiles[t], source[d], (((0,), (0,)), ((), ())), preferred_element_type=F32
            )
            done.append((s, product))
        for s, product in done:
            acc[s] += product
        return carry

    lax.fori_loop(0, (n + UNROLL - 1) // UNROLL, group, 0)


def own_kernel(dst_s, src_s, tiles, x, out, lists, acc, *, far_blocks):
    own_blocks = x.shape[0]
    make_lists(dst_s, src_s, lists, own_blocks, far_blocks)
    acc[...] = jnp.zeros_like(acc)
    add_tiles(lists, 0, tiles, x, acc, own_blocks)
    out[...] = acc[:own_blocks]


def own_tiles(tile_dst, tile_src, tiles, x, far_blocks):
    n = tiles.shape[0]
    return pl.pallas_call(
        functools.partial(own_kernel, far_blocks=far_blocks),
        out_shape=(
            jax.ShapeDtypeStruct(x.shape, F32),
            jax.ShapeDtypeStruct((2, n + UNROLL), jnp.int32),
        ),
        in_specs=[SMEM, SMEM, VMEM, VMEM],
        out_specs=(VMEM, SMEM),
        scratch_shapes=[pltpu.VMEM((x.shape[0] + 1,) + x.shape[1:], F32)],
        compiler_params=params(20),
        cost_estimate=cost(2 * n * 128**3, 1 << 23),
        name="own_tiles",
    )(tile_dst, tile_src, tiles, x)


def far_kernel(lists, tiles, incoming, base, out, source, acc):
    n_dom = incoming.shape[0]
    own_blocks, tile, _ = base.shape
    capacity = tile
    hub_dev = incoming.shape[1] - capacity
    hub_blocks = n_dom * hub_dev // tile
    for q in range(n_dom):
        source[hub_blocks + q] = incoming[q, :capacity, :]
        block, row = divmod(q * hub_dev, tile)
        source[block, row : row + hub_dev, :] = incoming[q, capacity:, :]
    acc[:own_blocks] = base[...]
    add_tiles(lists, 1, tiles, source, acc, own_blocks)
    out[...] = acc[:own_blocks].astype(BF16)


def far_tiles(lists, tiles, incoming, base, far_blocks):
    own_blocks, tile, width = base.shape
    return pl.pallas_call(
        far_kernel,
        out_shape=jax.ShapeDtypeStruct(base.shape, BF16),
        in_specs=[SMEM, VMEM, VMEM, VMEM],
        out_specs=VMEM,
        scratch_shapes=[
            pltpu.VMEM((far_blocks, tile, width), BF16),
            pltpu.VMEM((own_blocks + 1, tile, width), F32),
        ],
        compiler_params=params(20),
        cost_estimate=cost(tiles.shape[0] * 128**3, 1 << 22),
        name="far_tiles",
    )(lists, tiles, incoming, base)


def forward_kernel(me_s, *refs, n_feat):
    xs, aggs = refs[:n_feat], refs[n_feat : 2 * n_feat]
    w_self, w_neigh, bias, grad_out, output, grad_pre = refs[2 * n_feat :]
    me = me_s[0]
    width = xs[0].shape[1]

    def product(shards, w):
        rows = [w[pl.ds(pl.multiple_of((me ^ k) * width, width), width), :] for k in range(n_feat)]
        return jnp.dot(
            jnp.concatenate([s[...] for s in shards], axis=1),
            jnp.concatenate(rows, axis=0),
            preferred_element_type=F32,
        )

    pre_act = product(xs, w_self) + product(aggs, w_neigh) + bias[...]
    gate = jax.nn.sigmoid(pre_act)
    output[...] = (pre_act * gate).astype(BF16)
    grad = grad_out[...].astype(F32) * gate * (1.0 + pre_act * (1.0 - gate))
    grad_pre[...] = grad.astype(BF16)


def forward(me, xs, aggs, w_self, w_neigh, bias, grad_out, block=512):
    n_feat = len(xs)
    rows, width = grad_out.shape
    by_rows = pl.BlockSpec((block, width), lambda i, m: (i, 0))
    whole = lambda a: pl.BlockSpec(a.shape, lambda i, m: (0, 0))
    return pl.pallas_call(
        functools.partial(forward_kernel, n_feat=n_feat),
        out_shape=(jax.ShapeDtypeStruct((rows, width), BF16),) * 2,
        grid_spec=pltpu.PrefetchScalarGridSpec(
            num_scalar_prefetch=1,
            grid=(rows // block,),
            in_specs=[by_rows] * (2 * n_feat)
            + [whole(w_self), whole(w_neigh), whole(bias), by_rows],
            out_specs=[by_rows, by_rows],
        ),
        compiler_params=params(20),
        cost_estimate=cost(4 * rows * width * n_feat * width, 1 << 23),
        name="forward_dense",
    )(me, *xs, *aggs, w_self, w_neigh, bias, grad_out)


def weights_kernel(*refs, n_feat):
    shards, grad, out = refs[: 2 * n_feat], refs[2 * n_feat], refs[2 * n_feat + 1]
    n_dom, chunk = out.shape[0], out.shape[1] - 8
    width = grad.shape[1]
    flipped = grad[...].T
    bias = jnp.sum(grad[...].astype(F32), axis=0, keepdims=True)
    for i, shard in enumerate(shards):
        block = jnp.dot(flipped, shard[...], preferred_element_type=F32).T
        for row in range(0, width, min(chunk, width)):
            q, start = divmod(i * width + row, chunk)
            n = min(chunk, width)
            out[q, start : start + n, :] = block[row : row + n, :]
    for q in range(n_dom):
        out[q, chunk:, :] = jnp.broadcast_to(bias, (8, width))


def weight_parts(shards, grad, n_dom):
    n_feat = len(shards) // 2
    width = grad.shape[1]
    chunk = 2 * n_feat * width // n_dom
    return pl.pallas_call(
        functools.partial(weights_kernel, n_feat=n_feat),
        out_shape=jax.ShapeDtypeStruct((n_dom, chunk + 8, width), F32),
        in_specs=[VMEM] * (2 * n_feat + 1),
        out_specs=VMEM,
        compiler_params=params(20),
        cost_estimate=cost(4 * n_feat * width * width * grad.shape[0], 1 << 22),
        name="weight_parts",
    )(*shards, grad)


def back_kernel(*refs):
    grads, w, out = refs[:-2], refs[-2], refs[-1]
    whole = jnp.concatenate([g[...] for g in grads], axis=1)
    rows = jnp.concatenate([w[k] for k in range(w.shape[0])], axis=1)
    product = lax.dot_general(whole, rows, (((1,), (1,)), ((), ())), preferred_element_type=F32)
    out[...] = product.astype(out.dtype)


def back_dense(grads, w, dtype, name, block=512):
    rows, width = grads[0].shape
    by_rows = pl.BlockSpec((block, width), lambda i: (i, 0))
    return pl.pallas_call(
        back_kernel,
        out_shape=jax.ShapeDtypeStruct((rows, width), dtype),
        grid=(rows // block,),
        in_specs=[by_rows] * len(grads) + [pl.BlockSpec(w.shape, lambda i: (0, 0, 0))],
        out_specs=by_rows,
        compiler_params=params(20),
        cost_estimate=cost(2 * rows * width * width * len(grads), 1 << 22),
        name=name,
    )(*grads, w)


def back_far_kernel(lists, tiles, back, weights, out, acc):
    n_dom = out.shape[0]
    own_blocks, tile, _ = back.shape
    chunk = weights.shape[0]
    hub_dev = out.shape[1] - tile - chunk
    hub_blocks = n_dom * hub_dev // tile
    acc[...] = jnp.zeros_like(acc)
    add_tiles_t(lists, 1, tiles, back, acc, own_blocks)
    for q in range(n_dom):
        out[q, :tile, :] = acc[hub_blocks + q].astype(BF16)
        block, row = divmod(q * hub_dev, tile)
        out[q, tile : tile + hub_dev, :] = acc[block, row : row + hub_dev, :].astype(BF16)
        out[q, tile + hub_dev :, :] = weights[...]


def back_far(lists, tiles, back, weights, n_dom, hub_dev):
    _, tile, width = back.shape
    far_blocks = n_dom * hub_dev // tile + n_dom
    rows = tile + hub_dev + weights.shape[0]
    return pl.pallas_call(
        back_far_kernel,
        out_shape=jax.ShapeDtypeStruct((n_dom, rows, width), BF16),
        in_specs=[SMEM, VMEM, VMEM, VMEM],
        out_specs=VMEM,
        scratch_shapes=[pltpu.VMEM((far_blocks + 1, tile, width), F32)],
        compiler_params=params(24),
        cost_estimate=cost(tiles.shape[0] * 128**3, 1 << 22),
        name="back_far",
    )(lists, tiles, back, weights)


def back_own_kernel(lists, tiles, back, direct, out, acc):
    own_blocks = back.shape[0]
    acc[:own_blocks] = direct[...]
    add_tiles_t(lists, 0, tiles, back, acc, own_blocks)
    out[...] = acc[:own_blocks]


def back_own(lists, tiles, back, direct):
    return pl.pallas_call(
        back_own_kernel,
        out_shape=jax.ShapeDtypeStruct(direct.shape, F32),
        in_specs=[SMEM, VMEM, VMEM, VMEM],
        out_specs=VMEM,
        scratch_shapes=[pltpu.VMEM((direct.shape[0] + 1,) + direct.shape[1:], F32)],
        compiler_params=params(20),
        cost_estimate=cost(2 * tiles.shape[0] * 128**3, 1 << 23),
        name="back_own",
    )(lists, tiles, back, direct)


def finish_kernel(count_s, hub_s, me_s, rows, incoming, base, out, self_out, neigh_out, *, n_feat):
    n_dom, capacity = rows.shape
    hub_dev = hub_s.shape[0]
    own_count, width = base.shape
    chunk = incoming.shape[1] - capacity - hub_dev
    block, peers = 256, min(8, n_dom)
    lane = lax.broadcasted_iota(jnp.int32, (1, capacity), 1)

    def some(g, carry):
        start = pl.multiple_of(g * block, block)
        vertex = lax.broadcasted_iota(jnp.int32, (block, capacity), 0) + start
        total = base[pl.ds(start, block), :]
        for first in range(0, n_dom, peers):
            hot, sent = [], []
            for q in range(first, first + peers):
                wanted = jnp.where(lane < count_s[0, q], rows[q : q + 1, :], -1)
                hot.append((vertex == wanted).astype(F32).astype(BF16))
                sent.append(incoming[q, :capacity, :])
            total += jnp.dot(
                jnp.concatenate(hot, axis=1),
                jnp.concatenate(sent, axis=0),
                preferred_element_type=F32,
            )
        out[pl.ds(start, block), :] = total
        return carry

    lax.fori_loop(0, own_count // block, some, 0)
    hub = incoming[0, capacity : capacity + hub_dev, :].astype(F32)
    for q in range(1, n_dom):
        hub += incoming[q, capacity : capacity + hub_dev, :].astype(F32)
    for j in range(hub_dev):
        out[pl.ds(hub_s[j], 1), :] += hub[j : j + 1, :]
    me = me_s[0]
    n = min(chunk, width)
    for row in range(0, 2 * n_feat * width, n):
        q, start = divmod(row, chunk)
        which, k = divmod(row // width, n_feat)
        target = (self_out, neigh_out)[which]
        piece = incoming[q, capacity + hub_dev + start : capacity + hub_dev + start + n, :]
        at = pl.multiple_of((me ^ k) * width + row % width, n)
        target[pl.ds(at, n), :] = piece.astype(F32)


def finish(send_rows, send_count, hub_ids, me, incoming, base, n_feat):
    width = base.shape[1]
    w_shape = jax.ShapeDtypeStruct((n_feat * width, width), F32)
    return pl.pallas_call(
        functools.partial(finish_kernel, n_feat=n_feat),
        out_shape=(jax.ShapeDtypeStruct(base.shape, F32), w_shape, w_shape),
        in_specs=[SMEM, SMEM, SMEM, VMEM, VMEM, VMEM],
        out_specs=(VMEM, VMEM, VMEM),
        compiler_params=params(24),
        cost_estimate=cost(2 * base.size * send_rows.size, 1 << 22),
        name="finish",
    )(send_count, hub_ids, me, send_rows, incoming, base)


def body(
    node_feats,
    edge_tiles,
    tile_dst,
    tile_src,
    hub_ids,
    send_rows,
    send_count,
    w_self,
    w_neigh,
    out_bias,
    grad_out,
    *,
    n_feat,
):
    own_count, width = node_feats.shape
    tile_size = edge_tiles.shape[1]
    listed = send_rows[0]
    n_dom, capacity = listed.shape
    hub_dev = hub_ids.shape[0]
    me = lax.axis_index("feat").astype(jnp.int32)
    me_s = me.reshape(1)
    order = me ^ jnp.arange(n_feat, dtype=jnp.int32)
    far_blocks = n_dom * hub_dev // tile_size + n_dom

    def swap(x, k):
        return lax.ppermute(x, "feat", [(j, j ^ k) for j in range(n_feat)])

    def gather_feat(x):
        shards = {0: x}
        bit = n_feat // 2
        while bit:
            for k in list(shards):
                shards[k ^ bit] = swap(shards[k], bit)
            bit //= 2
        return [shards[k] for k in range(n_feat)]

    feats = gather_feat(node_feats)

    outgoing = pick(listed, send_count, hub_ids, node_feats)
    incoming = lax.all_to_all(outgoing, "dom", 0, 0, tiled=True)
    own_feats = node_feats.reshape(-1, tile_size, width)
    base, lists = own_tiles(tile_dst, tile_src, edge_tiles, own_feats, far_blocks)
    aggregated = far_tiles(lists, edge_tiles, incoming, base, far_blocks).reshape(own_count, width)

    aggs = gather_feat(aggregated)
    output, grad_pre = forward(
        me_s, feats, aggs, w_self, w_neigh, out_bias[None, :], grad_out
    )
    grads = gather_feat(grad_pre)

    parts = weight_parts(feats + aggs, grad_pre, n_dom)
    chunk = parts.shape[1] - 8
    summed_w = jnp.sum(lax.all_to_all(parts, "dom", 0, 0, tiled=True), axis=0)
    grad_bias = summed_w[chunk]
    weights_out = summed_w[:chunk].astype(BF16)

    both = jnp.stack([w_self, w_neigh]).reshape(2, n_feat, width, -1)[:, order]
    rows = lax.concatenate(
        [both[:, 0:1]] + [swap(both[:, k : k + 1], k) for k in range(1, n_feat)], 1
    )
    back_agg = back_dense(grads, rows[1], BF16, "back_agg").reshape(own_feats.shape)
    direct = back_dense(grads, rows[0], F32, "direct").reshape(own_feats.shape)
    back_out = back_far(lists, edge_tiles, back_agg, weights_out, n_dom, hub_dev)
    back_in = lax.all_to_all(back_out, "dom", 0, 0, tiled=True)
    own = back_own(lists, edge_tiles, back_agg, direct).reshape(own_count, width)
    grad_feats, grad_self, grad_neigh = finish(
        listed, send_count, hub_ids, me_s, back_in, own, n_feat
    )
    return (output, grad_feats, grad_self, grad_neigh, grad_bias)


def solution(mesh):
    in_specs = (
        P("dom", "feat"),
        P("dom", None, None),
        P("dom"),
        P("dom"),
        P("dom"),
        P("dom", None, None),
        P("dom", None),
        P(None, "feat"),
        P(None, "feat"),
        P("feat"),
        P("dom", "feat"),
    )
    out_specs = (P("dom", "feat"), P("dom", "feat"), P(None, "feat"), P(None, "feat"), P("feat"))
    n_feat = mesh.shape["feat"]

    def run(*args):
        return body(*args, n_feat=n_feat)

    return jax.shard_map(run, mesh=mesh, in_specs=in_specs, out_specs=out_specs, check_vma=False)
```

```python
import functools

import jax
import jax.numpy as jnp
from jax import lax
from jax.experimental import pallas as pl
from jax.experimental.pallas import tpu as pltpu
from jax.sharding import PartitionSpec as P

F32 = jnp.float32
BF16 = jnp.bfloat16
VMEM = pl.BlockSpec(memory_space=pltpu.VMEM)
SMEM = pl.BlockSpec(memory_space=pltpu.SMEM)
HBM = pl.BlockSpec(memory_space=pltpu.HBM)
UNROLL = 8
T_BITS, S_BITS = 10, 10


def params(mib=24):
    return pltpu.CompilerParams(vmem_limit_bytes=mib << 20)


def hbm(x):
    return pltpu.with_memory_space_constraint(x, pltpu.HBM)


def cost(flops, nbytes):
    return pl.CostEstimate(flops=flops, bytes_accessed=nbytes, transcendentals=0)


def start_copies(sems, *pairs):
    copies = [pltpu.make_async_copy(a, b, sems.at[i]) for i, (a, b) in enumerate(pairs)]
    for copy in copies:
        copy.start()
    return copies


def wait_copies(copies):
    for copy in copies:
        copy.wait()


def pick_kernel(rows_h, count_h, hub_h, x_h, out_h, rows_s, count_s, hub_s, x, x32, stage, out, sems):
    copies = start_copies(sems, (x_h, x), (rows_h, rows_s), (count_h, count_s), (hub_h, hub_s))
    n_dom, capacity = rows_s.shape
    hub_dev = hub_s.shape[0]
    step = 16
    wait_copies(copies)
    x32[...] = x[...].astype(F32)
    for j in range(hub_dev):
        stage[capacity + j : capacity + j + 1, :] = x32[pl.ds(hub_s[j], 1), :]
    hub = stage[capacity:, :].astype(BF16)
    slot = lax.broadcasted_iota(jnp.int32, (capacity, x.shape[1]), 0)

    def peer(q, carry):
        def some(g, carry):
            for u in range(step):
                c = g * step + u
                stage[pl.ds(c, 1), :] = x32[pl.ds(rows_s[q, c], 1), :]
            return carry

        lax.fori_loop(0, capacity // step, some, 0)
        kept = jnp.where(slot < count_s[0, q], stage[:capacity, :], 0.0)
        out[q, :capacity, :] = kept.astype(BF16)
        out[q, capacity:, :] = hub
        return carry

    lax.fori_loop(0, n_dom, peer, 0)
    wait_copies(start_copies(sems, (out, out_h)))


def pick(send_rows, send_count, hub_ids, x):
    n_dom, capacity = send_rows.shape
    rows = capacity + hub_ids.shape[0]
    shape = (n_dom, rows, x.shape[1])
    return pl.pallas_call(
        pick_kernel,
        out_shape=pltpu.HBM(shape, BF16),
        in_specs=[HBM] * 4,
        out_specs=HBM,
        scratch_shapes=[
            pltpu.SMEM(send_rows.shape, jnp.int32),
            pltpu.SMEM(send_count.shape, jnp.int32),
            pltpu.SMEM(hub_ids.shape, jnp.int32),
            pltpu.VMEM(x.shape, BF16),
            pltpu.VMEM(x.shape, F32),
            pltpu.VMEM((rows, x.shape[1]), F32),
            pltpu.VMEM(shape, BF16),
            pltpu.SemaphoreType.DMA((4,)),
        ],
        compiler_params=params(),
        cost_estimate=cost(0, 1 << 21),
        name="pick_rows",
    )(hbm(send_rows), hbm(send_count), hbm(hub_ids), hbm(x))


def unpack(entry):
    t = entry & ((1 << T_BITS) - 1)
    s = (entry >> T_BITS) & ((1 << S_BITS) - 1)
    return t, s, entry >> (T_BITS + S_BITS)


def make_lists(dst_s, src_s, lists, own_blocks, far_blocks):
    length = lists.shape[1] - 1

    def step(t, n):
        s = src_s[t]
        d = dst_s[t]
        far = (s >= own_blocks).astype(jnp.int32)
        lists[0, n[0]] = t + (s << T_BITS) + (d << (T_BITS + S_BITS))
        lists[1, n[1]] = t + ((s - own_blocks) << T_BITS) + (d << (T_BITS + S_BITS))
        return n[0] + 1 - far, n[1] + far

    n = lax.fori_loop(0, dst_s.shape[0], step, (jnp.int32(0), jnp.int32(0)))
    for which, blocks in ((0, own_blocks), (1, far_blocks)):
        spare = (blocks << T_BITS) + (own_blocks << (T_BITS + S_BITS))
        for u in range(UNROLL - 1):
            lists[which, n[which] + u] = jnp.int32(spare)
        lists[which, length] = n[which]


def add_tiles(lists, which, tiles, source, acc, spare):
    n = lists[which, lists.shape[1] - 1]

    def group(g, carry):
        done = []
        for u in range(UNROLL):
            t, s, d = unpack(lists[which, g * UNROLL + u])
            s = jnp.where(d == spare, 0, s)
            done.append((d, jnp.dot(tiles[t], source[s], preferred_element_type=F32)))
        for d, product in done:
            acc[d] += product
        return carry

    lax.fori_loop(0, (n + UNROLL - 1) // UNROLL, group, 0)


def add_tiles_t(lists, which, tiles, source, acc, spare):
    n = lists[which, lists.shape[1] - 1]

    def group(g, carry):
        done = []
        for u in range(UNROLL):
            t, s, d = unpack(lists[which, g * UNROLL + u])
            d = jnp.where(d == spare, 0, d)
            product = lax.dot_general(
                tiles[t], source[d], (((0,), (0,)), ((), ())), preferred_element_type=F32
            )
            done.append((s, product))
        for s, product in done:
            acc[s] += product
        return carry

    lax.fori_loop(0, (n + UNROLL - 1) // UNROLL, group, 0)


def own_kernel(dst_h, src_h, tiles, x_h, out_h, lists, dst_s, src_s, x, acc, sems, *, far_blocks):
    own_blocks = x.shape[0]
    copies = start_copies(sems, (x_h, x), (dst_h, dst_s), (src_h, src_s))
    acc[...] = jnp.zeros_like(acc)
    wait_copies(copies)
    make_lists(dst_s, src_s, lists, own_blocks, far_blocks)
    add_tiles(lists, 0, tiles, x, acc, own_blocks)
    wait_copies(start_copies(sems, (acc.at[pl.ds(0, own_blocks)], out_h)))


def own_tiles(tile_dst, tile_src, tiles, x, far_blocks):
    n = tiles.shape[0]
    return pl.pallas_call(
        functools.partial(own_kernel, far_blocks=far_blocks),
        out_shape=(
            pltpu.HBM(x.shape, F32),
            jax.ShapeDtypeStruct((2, n + UNROLL), jnp.int32),
        ),
        in_specs=[HBM, HBM, VMEM, HBM],
        out_specs=(HBM, SMEM),
        scratch_shapes=[
            pltpu.SMEM((n,), jnp.int32),
            pltpu.SMEM((n,), jnp.int32),
            pltpu.VMEM(x.shape, BF16),
            pltpu.VMEM((x.shape[0] + 1,) + x.shape[1:], F32),
            pltpu.SemaphoreType.DMA((3,)),
        ],
        compiler_params=params(),
        cost_estimate=cost(2 * n * 128**3, 1 << 23),
        name="own_tiles",
    )(hbm(tile_dst), hbm(tile_src), tiles, hbm(x))


def far_kernel(lists, tiles, incoming_h, base_h, out_h, source, acc, out, sems):
    n_dom, rows, _ = incoming_h.shape
    own_blocks, tile, _ = base_h.shape
    hub_dev = rows - tile
    hub_blocks = n_dom * hub_dev // tile
    pairs = [(incoming_h.at[:, pl.ds(0, tile), :], source.at[pl.ds(hub_blocks, n_dom)])]
    pairs.append((base_h, acc.at[pl.ds(0, own_blocks)]))
    for q in range(n_dom):
        block, row = divmod(q * hub_dev, tile)
        pairs.append(
            (incoming_h.at[q, pl.ds(tile, hub_dev), :], source.at[block, pl.ds(row, hub_dev), :])
        )
    wait_copies(start_copies(sems, *pairs))
    add_tiles(lists, 1, tiles, source, acc, own_blocks)
    out[...] = acc[:own_blocks].astype(BF16)
    wait_copies(start_copies(sems, (out, out_h)))


def far_tiles(lists, tiles, incoming, base, far_blocks):
    own_blocks, tile, width = base.shape
    return pl.pallas_call(
        far_kernel,
        out_shape=pltpu.HBM(base.shape, BF16),
        in_specs=[SMEM, VMEM, HBM, HBM],
        out_specs=HBM,
        scratch_shapes=[
            pltpu.VMEM((far_blocks, tile, width), BF16),
            pltpu.VMEM((own_blocks + 1, tile, width), F32),
            pltpu.VMEM(base.shape, BF16),
            pltpu.SemaphoreType.DMA((incoming.shape[0] + 2,)),
        ],
        compiler_params=params(),
        cost_estimate=cost(tiles.shape[0] * 128**3, 1 << 22),
        name="far_tiles",
    )(lists, tiles, hbm(incoming), hbm(base))


def by_shards(me, shards, w):
    width = shards[0].shape[1]
    rows = [
        w[pl.ds(pl.multiple_of((me ^ k) * width, width), width), :] for k in range(len(shards))
    ]
    return jnp.dot(
        jnp.concatenate([s[...] for s in shards], axis=1),
        jnp.concatenate(rows, axis=0),
        preferred_element_type=F32,
    )


def self_kernel(me_s, *refs):
    shards, w, bias, out = refs[:-3], refs[-3], refs[-2], refs[-1]
    out[...] = by_shards(me_s[0], shards, w) + bias[...]


def forward_kernel(me_s, *refs):
    shards = refs[:-5]
    w, own_part, grad_out, output, grad_pre = refs[-5:]
    pre_act = own_part[...] + by_shards(me_s[0], shards, w)
    gate = jax.nn.sigmoid(pre_act)
    output[...] = (pre_act * gate).astype(BF16)
    grad = grad_out[...].astype(F32) * gate * (1.0 + pre_act * (1.0 - gate))
    grad_pre[...] = grad.astype(BF16)


def row_blocks_call(kernel, me, by_row, operands, outs, flops, name, block=512):
    rows, width = by_row[0].shape
    row_spec = pl.BlockSpec((block, width), lambda i, m: (i, 0))
    return pl.pallas_call(
        kernel,
        out_shape=tuple(pltpu.HBM((rows, width), t) for t in outs),
        grid_spec=pltpu.PrefetchScalarGridSpec(
            num_scalar_prefetch=1,
            grid=(rows // block,),
            in_specs=[
                row_spec if a.shape == (rows, width) else pl.BlockSpec(a.shape, lambda i, m: (0, 0))
                for a in operands
            ],
            out_specs=tuple(row_spec for t in outs),
        ),
        compiler_params=params(),
        cost_estimate=cost(flops, 1 << 22),
        name=name,
    )(me, *[hbm(a) for a in operands])


def weights_kernel(*refs, n_feat):
    shards, grad, out_h, out, sems = refs[: 2 * n_feat], *refs[2 * n_feat :]
    n_dom, chunk = out.shape[0], out.shape[1] - 8
    width = grad.shape[1]
    flipped = grad[...].T
    bias = jnp.sum(grad[...].astype(F32), axis=0, keepdims=True)
    for i, shard in enumerate(shards):
        block = jnp.dot(flipped, shard[...], preferred_element_type=F32).T
        for row in range(0, width, min(chunk, width)):
            q, start = divmod(i * width + row, chunk)
            n = min(chunk, width)
            out[q, start : start + n, :] = block[row : row + n, :]
    for q in range(n_dom):
        out[q, chunk:, :] = jnp.broadcast_to(bias, (8, width))
    wait_copies(start_copies(sems, (out, out_h)))


def weight_parts(shards, grad, n_dom):
    n_feat = len(shards) // 2
    width = grad.shape[1]
    chunk = 2 * n_feat * width // n_dom
    return pl.pallas_call(
        functools.partial(weights_kernel, n_feat=n_feat),
        out_shape=pltpu.HBM((n_dom, chunk + 8, width), F32),
        in_specs=[VMEM] * (2 * n_feat + 1),
        out_specs=HBM,
        scratch_shapes=[
            pltpu.VMEM((n_dom, chunk + 8, width), F32),
            pltpu.SemaphoreType.DMA((1,)),
        ],
        compiler_params=params(),
        cost_estimate=cost(4 * n_feat * width * width * grad.shape[0], 1 << 22),
        name="weight_parts",
    )(*[hbm(a) for a in (*shards, grad)])


def back_kernel(*refs):
    grads, w, out = refs[:-2], refs[-2], refs[-1]
    whole = jnp.concatenate([g[...] for g in grads], axis=1)
    rows = jnp.concatenate([w[k] for k in range(w.shape[0])], axis=1)
    product = lax.dot_general(whole, rows, (((1,), (1,)), ((), ())), preferred_element_type=F32)
    out[...] = product.astype(out.dtype)


def back_dense(grads, w, dtype, name, block=512):
    rows, width = grads[0].shape
    by_rows = pl.BlockSpec((block, width), lambda i: (i, 0))
    return pl.pallas_call(
        back_kernel,
        out_shape=pltpu.HBM((rows, width), dtype),
        grid=(rows // block,),
        in_specs=[by_rows] * len(grads) + [pl.BlockSpec(w.shape, lambda i: (0, 0, 0))],
        out_specs=by_rows,
        compiler_params=params(),
        cost_estimate=cost(2 * rows * width * width * len(grads), 1 << 22),
        name=name,
    )(*[hbm(a) for a in (*grads, w)])


def back_far_kernel(lists, tiles, back_h, out_h, back, acc, out, sems):
    n_dom = out.shape[0]
    own_blocks, tile, _ = back.shape
    hub_dev = out.shape[1] - tile
    hub_blocks = n_dom * hub_dev // tile
    copies = start_copies(sems, (back_h, back))
    acc[...] = jnp.zeros_like(acc)
    wait_copies(copies)
    add_tiles_t(lists, 1, tiles, back, acc, own_blocks)
    for q in range(n_dom):
        out[q, :tile, :] = acc[hub_blocks + q].astype(BF16)
        block, row = divmod(q * hub_dev, tile)
        out[q, tile:, :] = acc[block, row : row + hub_dev, :].astype(BF16)
    wait_copies(start_copies(sems, (out, out_h)))


def back_far(lists, tiles, back, n_dom, hub_dev):
    _, tile, width = back.shape
    far_blocks = n_dom * hub_dev // tile + n_dom
    shape = (n_dom, tile + hub_dev, width)
    return pl.pallas_call(
        back_far_kernel,
        out_shape=pltpu.HBM(shape, BF16),
        in_specs=[SMEM, VMEM, HBM],
        out_specs=HBM,
        scratch_shapes=[
            pltpu.VMEM(back.shape, BF16),
            pltpu.VMEM((far_blocks + 1, tile, width), F32),
            pltpu.VMEM(shape, BF16),
            pltpu.SemaphoreType.DMA((1,)),
        ],
        compiler_params=params(),
        cost_estimate=cost(tiles.shape[0] * 128**3, 1 << 22),
        name="back_far",
    )(lists, tiles, hbm(back))


def back_own_kernel(lists, tiles, back_h, direct_h, out_h, back, acc, sems):
    own_blocks = back.shape[0]
    own = acc.at[pl.ds(0, own_blocks)]
    wait_copies(start_copies(sems, (back_h, back), (direct_h, own)))
    add_tiles_t(lists, 0, tiles, back, acc, own_blocks)
    wait_copies(start_copies(sems, (own, out_h)))


def back_own(lists, tiles, back, direct):
    return pl.pallas_call(
        back_own_kernel,
        out_shape=pltpu.HBM(direct.shape, F32),
        in_specs=[SMEM, VMEM, HBM, HBM],
        out_specs=HBM,
        scratch_shapes=[
            pltpu.VMEM(back.shape, BF16),
            pltpu.VMEM((direct.shape[0] + 1,) + direct.shape[1:], F32),
            pltpu.SemaphoreType.DMA((2,)),
        ],
        compiler_params=params(),
        cost_estimate=cost(2 * tiles.shape[0] * 128**3, 1 << 23),
        name="back_own",
    )(lists, tiles, hbm(back), hbm(direct))


def hot_kernel(count_s, rows, out):
    n_dom, capacity = rows.shape
    block = out.shape[0]
    lane = lax.broadcasted_iota(jnp.int32, (1, capacity), 1)
    vertex = lax.broadcasted_iota(jnp.int32, (block, capacity), 0) + pl.program_id(0) * block
    for q in range(n_dom):
        wanted = jnp.where(lane < count_s[0, q], rows[q : q + 1, :], -1)
        one = (vertex == wanted).astype(F32).astype(BF16)
        out[:, q * capacity : (q + 1) * capacity] = one


def hot_rows(send_rows, send_count, own_count, block=256):
    return pl.pallas_call(
        hot_kernel,
        out_shape=pltpu.HBM((own_count, send_rows.size), BF16),
        grid_spec=pltpu.PrefetchScalarGridSpec(
            num_scalar_prefetch=1,
            grid=(own_count // block,),
            in_specs=[pl.BlockSpec(send_rows.shape, lambda i, c: (0, 0))],
            out_specs=pl.BlockSpec((block, send_rows.size), lambda i, c: (i, 0)),
        ),
        compiler_params=params(),
        cost_estimate=cost(0, 1 << 23),
        name="hot_rows",
    )(hbm(send_count), hbm(send_rows))


def finish_kernel(hub_s, hot, incoming, base, out, sent, hub):
    n_dom, rows, width = incoming.shape
    hub_dev = hub_s.shape[0]
    capacity = rows - hub_dev
    block = base.shape[0]

    @pl.when(pl.program_id(0) == 0)
    def _():
        total = jnp.zeros((hub_dev, width), F32)
        for q in range(n_dom):
            sent[q * capacity : (q + 1) * capacity, :] = incoming[q, :capacity, :]
            total += incoming[q, capacity:, :].astype(F32)
        hub[...] = total

    out[...] = base[...] + jnp.dot(hot[...], sent[...], preferred_element_type=F32)
    start = pl.program_id(0) * block
    for j in range(hub_dev):
        row = hub_s[j] - start

        @pl.when((row >= 0) & (row < block))
        def _():
            out[pl.ds(row, 1), :] += hub[j : j + 1, :]


def finish(hub_ids, hot, incoming, base, block=256):
    own_count, width = base.shape
    n_dom, rows, _ = incoming.shape
    hub_dev = hub_ids.shape[0]
    by_rows = lambda n: pl.BlockSpec((block, n), lambda i, h: (i, 0))
    return pl.pallas_call(
        finish_kernel,
        out_shape=pltpu.HBM(base.shape, F32),
        grid_spec=pltpu.PrefetchScalarGridSpec(
            num_scalar_prefetch=1,
            grid=(own_count // block,),
            in_specs=[
                by_rows(hot.shape[1]),
                pl.BlockSpec(incoming.shape, lambda i, h: (0, 0, 0)),
                by_rows(width),
            ],
            out_specs=by_rows(width),
            scratch_shapes=[
                pltpu.VMEM((n_dom * (rows - hub_dev), width), BF16),
                pltpu.VMEM((hub_dev, width), F32),
            ],
        ),
        compiler_params=params(),
        cost_estimate=cost(2 * hot.size * width, 1 << 23),
        name="finish",
    )(hbm(hub_ids), hbm(hot), hbm(incoming), hbm(base))


def cut_kernel(me_s, w_self, w_neigh, *outs):
    width = w_self.shape[1]
    for k, out in enumerate(outs):
        at = pl.ds(pl.multiple_of((me_s[0] ^ k) * width, width), width)
        out[0] = w_self[at, :]
        out[1] = w_neigh[at, :]


def cut_weights(me, w_self, w_neigh, n_feat):
    width = w_self.shape[1]
    return pl.pallas_call(
        cut_kernel,
        out_shape=(pltpu.HBM((2, width, width), BF16),) * n_feat,
        in_specs=[SMEM, VMEM, VMEM],
        out_specs=(VMEM,) * n_feat,
        compiler_params=params(),
        cost_estimate=cost(0, 1 << 20),
        name="cut_weights",
    )(me, hbm(w_self), hbm(w_neigh))


def place_kernel(me_s, sums, self_out, neigh_out):
    rows, width = self_out.shape
    for i in range(2 * rows // width):
        which, k = divmod(i, rows // width)
        target = (self_out, neigh_out)[which]
        at = pl.ds(pl.multiple_of((me_s[0] ^ k) * width, width), width)
        target[at, :] = sums[i * width : (i + 1) * width, :].astype(F32)


def place_weights(me, sums):
    rows, width = sums.shape[0] // 2, sums.shape[1]
    return pl.pallas_call(
        place_kernel,
        out_shape=(pltpu.HBM((rows, width), F32),) * 2,
        in_specs=[SMEM, VMEM],
        out_specs=(VMEM, VMEM),
        compiler_params=params(),
        cost_estimate=cost(0, 1 << 20),
        name="place_weights",
    )(me, hbm(sums))


def body(
    node_feats,
    edge_tiles,
    tile_dst,
    tile_src,
    hub_ids,
    send_rows,
    send_count,
    w_self,
    w_neigh,
    out_bias,
    grad_out,
    *,
    n_feat,
):
    own_count, width = node_feats.shape
    tile_size = edge_tiles.shape[1]
    listed = send_rows[0]
    n_dom, capacity = listed.shape
    hub_dev = hub_ids.shape[0]
    me = lax.axis_index("feat").astype(jnp.int32)
    me_s = me.reshape(1)
    far_blocks = n_dom * hub_dev // tile_size + n_dom

    def swap(x, k):
        return lax.ppermute(x, "feat", [(j, j ^ k) for j in range(n_feat)])

    def gather_feat(x):
        shards = {0: x}
        bit = n_feat // 2
        while bit:
            for k in list(shards):
                shards[k ^ bit] = swap(shards[k], bit)
            bit //= 2
        return [shards[k] for k in range(n_feat)]

    feats = gather_feat(node_feats)

    outgoing = pick(listed, send_count, hub_ids, node_feats)
    incoming = lax.all_to_all(outgoing, "dom", 0, 0, tiled=True)
    own_feats = node_feats.reshape(-1, tile_size, width)
    base, lists = own_tiles(tile_dst, tile_src, edge_tiles, own_feats, far_blocks)
    aggregated = far_tiles(lists, edge_tiles, incoming, base, far_blocks).reshape(own_count, width)

    aggs = gather_feat(aggregated)
    flops = 2 * own_count * n_feat * width * width
    (own_part,) = row_blocks_call(
        self_kernel, me_s, feats, [*feats, w_self, out_bias[None, :]], [F32], flops, "self_dense"
    )
    output, grad_pre = row_blocks_call(
        forward_kernel,
        me_s,
        aggs,
        [*aggs, w_neigh, own_part, grad_out],
        [BF16, BF16],
        flops,
        "forward_dense",
    )
    grads = gather_feat(grad_pre)

    parts = weight_parts(feats + aggs, grad_pre, n_dom)
    chunk = parts.shape[1] - 8
    summed_w = jnp.sum(lax.all_to_all(parts, "dom", 0, 0, tiled=True), axis=0)
    grad_bias = summed_w[chunk]
    weights_out = jnp.broadcast_to(summed_w[None, :chunk].astype(BF16), (n_dom, chunk, width))

    cut = cut_weights(me_s, w_self, w_neigh, n_feat)
    rows = jnp.stack([cut[0]] + [swap(cut[k], k) for k in range(1, n_feat)], axis=1)
    back_agg = back_dense(grads, rows[1], BF16, "back_agg").reshape(own_feats.shape)
    direct = back_dense(grads, rows[0], F32, "direct").reshape(own_feats.shape)
    back_out = back_far(lists, edge_tiles, back_agg, n_dom, hub_dev)
    back_in = lax.all_to_all(back_out, "dom", 0, 0, tiled=True)
    own = back_own(lists, edge_tiles, back_agg, direct).reshape(own_count, width)
    weights_in = lax.all_to_all(weights_out, "dom", 0, 0, tiled=True)
    hot = hot_rows(listed, send_count, own_count)
    grad_feats = finish(hub_ids, hot, back_in, own)
    grad_self, grad_neigh = place_weights(me_s, weights_in.reshape(-1, width))
    return (output, grad_feats, grad_self, grad_neigh, grad_bias)


def solution(mesh):
    in_specs = (
        P("dom", "feat"),
        P("dom", None, None),
        P("dom"),
        P("dom"),
        P("dom"),
        P("dom", None, None),
        P("dom", None),
        P(None, "feat"),
        P(None, "feat"),
        P("feat"),
        P("dom", "feat"),
    )
    out_specs = (P("dom", "feat"), P("dom", "feat"), P(None, "feat"), P(None, "feat"), P("feat"))
    n_feat = mesh.shape["feat"]

    def run(*args):
        return body(*args, n_feat=n_feat)

    return jax.shard_map(run, mesh=mesh, in_specs=in_specs, out_specs=out_specs, check_vma=False)
```

```python
import functools

import jax
import jax.numpy as jnp
from jax import lax
from jax.experimental import pallas as pl
from jax.experimental.pallas import tpu as pltpu
from jax.sharding import PartitionSpec as P

F32 = jnp.float32
BF16 = jnp.bfloat16
VMEM = pl.BlockSpec(memory_space=pltpu.VMEM)
SMEM = pl.BlockSpec(memory_space=pltpu.SMEM)
HBM = pl.BlockSpec(memory_space=pltpu.HBM)
ANY = pl.BlockSpec(memory_space=pl.ANY)
UNROLL = 8
T_BITS, S_BITS = 10, 10


def params(mib=24):
    return pltpu.CompilerParams(vmem_limit_bytes=mib << 20)


def hbm(x):
    return pltpu.with_memory_space_constraint(x, pltpu.HBM)


def cost(flops, nbytes):
    return pl.CostEstimate(flops=flops, bytes_accessed=nbytes, transcendentals=0)


def start_copies(sems, *pairs):
    copies = [pltpu.make_async_copy(a, b, sems.at[i]) for i, (a, b) in enumerate(pairs)]
    for copy in copies:
        copy.start()
    return copies


def wait_copies(copies):
    for copy in copies:
        copy.wait()


def pick_kernel(rows_h, count_h, hub_h, x_h, out_h, rows_s, count_s, hub_s, x, x32, stage, out, sems):
    copies = start_copies(sems, (x_h, x), (rows_h, rows_s), (count_h, count_s), (hub_h, hub_s))
    n_dom, capacity = rows_s.shape
    hub_dev = hub_s.shape[0]
    step = 16
    wait_copies(copies)
    x32[...] = x[...].astype(F32)
    for j in range(hub_dev):
        stage[capacity + j : capacity + j + 1, :] = x32[pl.ds(hub_s[j], 1), :]
    hub = stage[capacity:, :].astype(BF16)
    slot = lax.broadcasted_iota(jnp.int32, (capacity, x.shape[1]), 0)

    def peer(q, carry):
        def some(g, carry):
            for u in range(step):
                c = g * step + u
                stage[pl.ds(c, 1), :] = x32[pl.ds(rows_s[q, c], 1), :]
            return carry

        lax.fori_loop(0, capacity // step, some, 0)
        kept = jnp.where(slot < count_s[0, q], stage[:capacity, :], 0.0)
        out[q, :capacity, :] = kept.astype(BF16)
        out[q, capacity:, :] = hub
        return carry

    lax.fori_loop(0, n_dom, peer, 0)
    wait_copies(start_copies(sems, (out, out_h)))


def pick(send_rows, send_count, hub_ids, x):
    n_dom, capacity = send_rows.shape
    rows = capacity + hub_ids.shape[0]
    shape = (n_dom, rows, x.shape[1])
    return pl.pallas_call(
        pick_kernel,
        out_shape=pltpu.HBM(shape, BF16),
        in_specs=[HBM] * 4,
        out_specs=HBM,
        scratch_shapes=[
            pltpu.SMEM(send_rows.shape, jnp.int32),
            pltpu.SMEM(send_count.shape, jnp.int32),
            pltpu.SMEM(hub_ids.shape, jnp.int32),
            pltpu.VMEM(x.shape, BF16),
            pltpu.VMEM(x.shape, F32),
            pltpu.VMEM((rows, x.shape[1]), F32),
            pltpu.VMEM(shape, BF16),
            pltpu.SemaphoreType.DMA((4,)),
        ],
        compiler_params=params(),
        cost_estimate=cost(0, 1 << 21),
        name="pick_rows",
    )(hbm(send_rows), hbm(send_count), hbm(hub_ids), hbm(x))


def unpack(entry):
    t = entry & ((1 << T_BITS) - 1)
    s = (entry >> T_BITS) & ((1 << S_BITS) - 1)
    return t, s, entry >> (T_BITS + S_BITS)


def make_lists(dst_s, src_s, lists, own_blocks, far_blocks):
    length = lists.shape[1] - 1

    def step(t, n):
        s = src_s[t]
        d = dst_s[t]
        far = (s >= own_blocks).astype(jnp.int32)
        lists[0, n[0]] = t + (s << T_BITS) + (d << (T_BITS + S_BITS))
        lists[1, n[1]] = t + ((s - own_blocks) << T_BITS) + (d << (T_BITS + S_BITS))
        return n[0] + 1 - far, n[1] + far

    n = lax.fori_loop(0, dst_s.shape[0], step, (jnp.int32(0), jnp.int32(0)))
    for which, blocks in ((0, own_blocks), (1, far_blocks)):
        spare = (blocks << T_BITS) + (own_blocks << (T_BITS + S_BITS))
        for u in range(UNROLL - 1):
            lists[which, n[which] + u] = jnp.int32(spare)
        lists[which, length] = n[which]


def add_tiles(lists, which, tiles, source, acc, spare):
    n = lists[which, lists.shape[1] - 1]

    def group(g, carry):
        done = []
        for u in range(UNROLL):
            t, s, d = unpack(lists[which, g * UNROLL + u])
            s = jnp.where(d == spare, 0, s)
            done.append((d, jnp.dot(tiles[t], source[s], preferred_element_type=F32)))
        for d, product in done:
            acc[d] += product
        return carry

    lax.fori_loop(0, (n + UNROLL - 1) // UNROLL, group, 0)


def add_tiles_t(lists, which, tiles, source, acc, spare):
    n = lists[which, lists.shape[1] - 1]

    def group(g, carry):
        done = []
        for u in range(UNROLL):
            t, s, d = unpack(lists[which, g * UNROLL + u])
            d = jnp.where(d == spare, 0, d)
            product = lax.dot_general(
                tiles[t], source[d], (((0,), (0,)), ((), ())), preferred_element_type=F32
            )
            done.append((s, product))
        for s, product in done:
            acc[s] += product
        return carry

    lax.fori_loop(0, (n + UNROLL - 1) // UNROLL, group, 0)


def own_kernel(dst_h, src_h, tiles, x_h, out_h, lists, dst_s, src_s, x, acc, sems, *, far_blocks):
    own_blocks = x.shape[0]
    copies = start_copies(sems, (x_h, x), (dst_h, dst_s), (src_h, src_s))
    acc[...] = jnp.zeros_like(acc)
    wait_copies(copies)
    make_lists(dst_s, src_s, lists, own_blocks, far_blocks)
    add_tiles(lists, 0, tiles, x, acc, own_blocks)
    wait_copies(start_copies(sems, (acc.at[pl.ds(0, own_blocks)], out_h)))


def own_tiles(tile_dst, tile_src, tiles, x, far_blocks):
    n = tiles.shape[0]
    return pl.pallas_call(
        functools.partial(own_kernel, far_blocks=far_blocks),
        out_shape=(
            pltpu.HBM(x.shape, F32),
            jax.ShapeDtypeStruct((2, n + UNROLL), jnp.int32),
        ),
        in_specs=[HBM, HBM, VMEM, HBM],
        out_specs=(HBM, SMEM),
        scratch_shapes=[
            pltpu.SMEM((n,), jnp.int32),
            pltpu.SMEM((n,), jnp.int32),
            pltpu.VMEM(x.shape, BF16),
            pltpu.VMEM((x.shape[0] + 1,) + x.shape[1:], F32),
            pltpu.SemaphoreType.DMA((3,)),
        ],
        compiler_params=params(),
        cost_estimate=cost(2 * n * 128**3, 1 << 23),
        name="own_tiles",
    )(hbm(tile_dst), hbm(tile_src), tiles, hbm(x))


def far_kernel(lists, tiles, incoming_h, base_h, out_h, source, acc, out, sems):
    n_dom, rows, _ = incoming_h.shape
    own_blocks, tile, _ = base_h.shape
    hub_dev = rows - tile
    hub_blocks = n_dom * hub_dev // tile
    pairs = [(incoming_h.at[:, pl.ds(0, tile), :], source.at[pl.ds(hub_blocks, n_dom)])]
    pairs.append((base_h, acc.at[pl.ds(0, own_blocks)]))
    for q in range(n_dom):
        block, row = divmod(q * hub_dev, tile)
        pairs.append(
            (incoming_h.at[q, pl.ds(tile, hub_dev), :], source.at[block, pl.ds(row, hub_dev), :])
        )
    wait_copies(start_copies(sems, *pairs))
    add_tiles(lists, 1, tiles, source, acc, own_blocks)
    out[...] = acc[:own_blocks].astype(BF16)
    wait_copies(start_copies(sems, (out, out_h)))


def far_tiles(lists, tiles, incoming, base, far_blocks):
    own_blocks, tile, width = base.shape
    return pl.pallas_call(
        far_kernel,
        out_shape=pltpu.HBM(base.shape, BF16),
        in_specs=[SMEM, VMEM, HBM, HBM],
        out_specs=HBM,
        scratch_shapes=[
            pltpu.VMEM((far_blocks, tile, width), BF16),
            pltpu.VMEM((own_blocks + 1, tile, width), F32),
            pltpu.VMEM(base.shape, BF16),
            pltpu.SemaphoreType.DMA((incoming.shape[0] + 2,)),
        ],
        compiler_params=params(),
        cost_estimate=cost(tiles.shape[0] * 128**3, 1 << 22),
        name="far_tiles",
    )(lists, tiles, hbm(incoming), hbm(base))


def by_shards(me, shards, w):
    width = shards[0].shape[1]
    rows = [
        w[pl.ds(pl.multiple_of((me ^ k) * width, width), width), :] for k in range(len(shards))
    ]
    return jnp.dot(
        jnp.concatenate([s[...] for s in shards], axis=1),
        jnp.concatenate(rows, axis=0),
        preferred_element_type=F32,
    )


def stream(step, ins_h, ins, outs_h, outs, sems, block):
    rows = ins[0].shape[0]
    n_in = len(ins)
    pending = []
    for i in range(rows // block):
        at = pl.ds(i * block, block)
        pairs = [(a.at[at], b.at[at]) for a, b in zip(ins_h, ins)]
        pending.append(start_copies(sems.at[i], *pairs))
    leaving = []
    for i in range(rows // block):
        at = pl.ds(i * block, block)
        wait_copies(pending[i])
        step(at, [r.at[at] for r in ins], [r.at[at] for r in outs])
        pairs = [(a.at[at], b.at[at]) for a, b in zip(outs, outs_h)]
        leaving.append(start_copies(sems.at[i, pl.ds(n_in, len(outs))], *pairs))
    for copies in leaving:
        wait_copies(copies)


def stream_call(kernel, me, streamed, whole, outs, flops, name, block=512):
    rows = streamed[0].shape[0]
    n_in, n_whole, n_out = len(streamed), len(whole), len(outs)

    def run(me_s, *refs):
        ins_h, refs = refs[:n_in], refs[n_in:]
        held, refs = refs[:n_whole], refs[n_whole:]
        outs_h, refs = refs[:n_out], refs[n_out:]
        ins, refs = refs[:n_in], refs[n_in:]
        out, sems = refs[:n_out], refs[n_out]
        stream(
            lambda at, i, o: kernel(me_s[0], i, held, o), ins_h, ins, outs_h, out, sems, block
        )

    return pl.pallas_call(
        run,
        out_shape=tuple(pltpu.HBM(shape, t) for shape, t in outs),
        in_specs=[SMEM] + [ANY] * n_in + [VMEM] * n_whole,
        out_specs=(HBM,) * n_out,
        scratch_shapes=[pltpu.VMEM(x.shape, x.dtype) for x in streamed]
        + [pltpu.VMEM(shape, t) for shape, t in outs]
        + [pltpu.SemaphoreType.DMA((rows // block, n_in + n_out))],
        compiler_params=params(),
        cost_estimate=cost(flops, 1 << 22),
        name=name,
    )(me, *streamed, *[hbm(x) for x in whole])


def self_step(me, ins, held, outs):
    w, bias = held
    outs[0][...] = by_shards(me, ins, w) + bias[...]


def forward_step(me, ins, held, outs):
    *shards, own_part, grad_out = ins
    output, grad_pre = outs
    pre_act = own_part[...] + by_shards(me, shards, held[0])
    gate = jax.nn.sigmoid(pre_act)
    output[...] = (pre_act * gate).astype(BF16)
    grad = grad_out[...].astype(F32) * gate * (1.0 + pre_act * (1.0 - gate))
    grad_pre[...] = grad.astype(BF16)


def weights_kernel(*refs, n_feat):
    shards, grad, out_h, out, sems = refs[: 2 * n_feat], *refs[2 * n_feat :]
    n_dom, chunk = out.shape[0], out.shape[1] - 8
    width = grad.shape[1]
    flipped = grad[...].T
    bias = jnp.sum(grad[...].astype(F32), axis=0, keepdims=True)
    for i, shard in enumerate(shards):
        block = jnp.dot(flipped, shard[...], preferred_element_type=F32).T
        for row in range(0, width, min(chunk, width)):
            q, start = divmod(i * width + row, chunk)
            n = min(chunk, width)
            out[q, start : start + n, :] = block[row : row + n, :]
    for q in range(n_dom):
        out[q, chunk:, :] = jnp.broadcast_to(bias, (8, width))
    wait_copies(start_copies(sems, (out, out_h)))


def weight_parts(shards, grad, n_dom):
    n_feat = len(shards) // 2
    width = grad.shape[1]
    chunk = 2 * n_feat * width // n_dom
    return pl.pallas_call(
        functools.partial(weights_kernel, n_feat=n_feat),
        out_shape=pltpu.HBM((n_dom, chunk + 8, width), F32),
        in_specs=[VMEM] * (2 * n_feat + 1),
        out_specs=HBM,
        scratch_shapes=[
            pltpu.VMEM((n_dom, chunk + 8, width), F32),
            pltpu.SemaphoreType.DMA((1,)),
        ],
        compiler_params=params(),
        cost_estimate=cost(4 * n_feat * width * width * grad.shape[0], 1 << 22),
        name="weight_parts",
    )(*shards, grad)


def split_copies(sems, pairs, block):
    rows = pairs[0][0].shape[0]
    return [
        start_copies(
            sems.at[i], *[(a.at[pl.ds(i * block, block)], b.at[pl.ds(i * block, block)]) for a, b in pairs]
        )
        for i in range(rows // block)
    ]


def back_far_kernel(*refs, n_feat):
    lists, tiles = refs[:2]
    grads_h, w = refs[2 : 2 + n_feat], refs[2 + n_feat : 2 + 2 * n_feat]
    out_h, back_h, direct_h = refs[2 + 2 * n_feat : 5 + 2 * n_feat]
    grads = refs[5 + 2 * n_feat : 5 + 3 * n_feat]
    back, direct, acc, out, sems, out_sems = refs[5 + 3 * n_feat :]
    n_dom = out.shape[0]
    own_blocks, tile, width = back.shape
    hub_dev = out.shape[1] - tile
    hub_blocks = n_dom * hub_dev // tile
    block = 4 * tile
    pending = split_copies(sems, list(zip(grads_h, grads)), block)
    acc[...] = jnp.zeros_like(acc)
    rows = jnp.concatenate([r[...].reshape(2 * width, -1) for r in w], axis=1)
    for i, copies in enumerate(pending):
        wait_copies(copies)
        whole = jnp.concatenate([g[i * block : (i + 1) * block, :] for g in grads], axis=1)
        both = lax.dot_general(whole, rows, (((1,), (1,)), ((), ())), preferred_element_type=F32)
        direct[4 * i : 4 * (i + 1)] = both[:, :width].reshape(4, tile, width)
        back[4 * i : 4 * (i + 1)] = both[:, width:].astype(BF16).reshape(4, tile, width)
    leaving = start_copies(out_sems, (direct, direct_h), (back, back_h))
    add_tiles_t(lists, 1, tiles, back, acc, own_blocks)
    for q in range(n_dom):
        out[q, :tile, :] = acc[hub_blocks + q].astype(BF16)
        at, row = divmod(q * hub_dev, tile)
        out[q, tile:, :] = acc[at, row : row + hub_dev, :].astype(BF16)
    leaving += start_copies(out_sems.at[pl.ds(2, 1)], (out, out_h))
    wait_copies(leaving)


def back_far(lists, tiles, grads, w, n_dom, hub_dev, tile):
    n_feat = len(grads)
    rows, width = grads[0].shape
    far_blocks = n_dom * hub_dev // tile + n_dom
    shape = (n_dom, tile + hub_dev, width)
    back_shape = (rows // tile, tile, width)
    return pl.pallas_call(
        functools.partial(back_far_kernel, n_feat=n_feat),
        out_shape=(pltpu.HBM(shape, BF16), pltpu.HBM(back_shape, BF16), pltpu.HBM(back_shape, F32)),
        in_specs=[SMEM, VMEM] + [ANY] * n_feat + [VMEM] * n_feat,
        out_specs=(HBM, HBM, HBM),
        scratch_shapes=[pltpu.VMEM((rows, width), BF16)] * n_feat
        + [
            pltpu.VMEM(back_shape, BF16),
            pltpu.VMEM(back_shape, F32),
            pltpu.VMEM((far_blocks + 1, tile, width), F32),
            pltpu.VMEM(shape, BF16),
            pltpu.SemaphoreType.DMA((rows // (4 * tile), n_feat)),
            pltpu.SemaphoreType.DMA((3,)),
        ],
        compiler_params=params(),
        cost_estimate=cost(4 * rows * width * width * n_feat, 1 << 22),
        name="back_far",
    )(lists, tiles, *grads, *w)


def back_own_kernel(lists, tiles, back_h, direct_h, out_h, back, acc, sems):
    own_blocks = back.shape[0]
    own = acc.at[pl.ds(0, own_blocks)]
    wait_copies(start_copies(sems, (back_h, back), (direct_h, own)))
    add_tiles_t(lists, 0, tiles, back, acc, own_blocks)
    wait_copies(start_copies(sems, (own, out_h)))


def back_own(lists, tiles, back, direct):
    return pl.pallas_call(
        back_own_kernel,
        out_shape=pltpu.HBM(direct.shape, F32),
        in_specs=[SMEM, VMEM, HBM, HBM],
        out_specs=HBM,
        scratch_shapes=[
            pltpu.VMEM(back.shape, BF16),
            pltpu.VMEM((direct.shape[0] + 1,) + direct.shape[1:], F32),
            pltpu.SemaphoreType.DMA((2,)),
        ],
        compiler_params=params(),
        cost_estimate=cost(2 * tiles.shape[0] * 128**3, 1 << 23),
        name="back_own",
    )(lists, tiles, hbm(back), hbm(direct))


def finish_kernel(rows_s, count_h, hub_h, incoming_h, base_h, out_h, count_s, hub_s, sent, hubs, base, sems, out_sems):
    n_dom, capacity = rows_s.shape
    hub_dev = hub_s.shape[0]
    own_count, width = base.shape
    block, peers = 256, min(8, n_dom)
    copies = start_copies(
        sems,
        (count_h, count_s),
        (hub_h, hub_s),
        (incoming_h.at[:, pl.ds(0, capacity), :], sent),
        (incoming_h.at[:, pl.ds(capacity, hub_dev), :], hubs),
        (base_h, base),
    )
    wait_copies(copies)
    hub = hubs[0].astype(F32)
    for q in range(1, n_dom):
        hub += hubs[q].astype(F32)
    for j in range(hub_dev):
        base[pl.ds(hub_s[j], 1), :] += hub[j : j + 1, :]
    lane = lax.broadcasted_iota(jnp.int32, (1, capacity), 1)
    leaving = []
    for start in range(0, own_count, block):
        vertex = lax.broadcasted_iota(jnp.int32, (block, capacity), 0) + start
        total = base[start : start + block, :]
        for first in range(0, n_dom, peers):
            hot, rows = [], []
            for q in range(first, first + peers):
                wanted = jnp.where(lane < count_s[0, q], rows_s[q : q + 1, :], -1)
                hot.append((vertex == wanted).astype(F32).astype(BF16))
                rows.append(sent[q])
            total += jnp.dot(
                jnp.concatenate(hot, axis=1),
                jnp.concatenate(rows, axis=0),
                preferred_element_type=F32,
            )
        base[start : start + block, :] = total
        at = pl.ds(start, block)
        leaving.append(start_copies(out_sems.at[pl.ds(start // block, 1)], (base.at[at], out_h.at[at])))
    for copies in leaving:
        wait_copies(copies)


def finish(send_rows, send_count, hub_ids, incoming, base):
    n_dom, capacity = send_rows.shape
    hub_dev = hub_ids.shape[0]
    own_count, width = base.shape
    return pl.pallas_call(
        finish_kernel,
        out_shape=pltpu.HBM(base.shape, F32),
        in_specs=[VMEM, HBM, HBM, ANY, HBM],
        out_specs=HBM,
        scratch_shapes=[
            pltpu.SMEM(send_count.shape, jnp.int32),
            pltpu.SMEM(hub_ids.shape, jnp.int32),
            pltpu.VMEM((n_dom, capacity, width), BF16),
            pltpu.VMEM((n_dom, hub_dev, width), BF16),
            pltpu.VMEM(base.shape, F32),
            pltpu.SemaphoreType.DMA((5,)),
            pltpu.SemaphoreType.DMA((own_count // 256,)),
        ],
        compiler_params=params(),
        cost_estimate=cost(2 * base.size * send_rows.size, 1 << 22),
        name="finish",
    )(hbm(send_rows), hbm(send_count), hbm(hub_ids), incoming, hbm(base))


def cut_kernel(me_s, w_self, w_neigh, *outs):
    width = w_self.shape[1]
    for k, out in enumerate(outs):
        at = pl.ds(pl.multiple_of((me_s[0] ^ k) * width, width), width)
        out[0] = w_self[at, :]
        out[1] = w_neigh[at, :]


def cut_weights(me, w_self, w_neigh, n_feat):
    width = w_self.shape[1]
    return pl.pallas_call(
        cut_kernel,
        out_shape=(pltpu.HBM((2, width, width), BF16),) * n_feat,
        in_specs=[SMEM, VMEM, VMEM],
        out_specs=(VMEM,) * n_feat,
        compiler_params=params(),
        cost_estimate=cost(0, 1 << 20),
        name="cut_weights",
    )(me, hbm(w_self), hbm(w_neigh))


def sum_kernel(parts, out, bias):
    n_dom, chunk, _ = out.shape
    total = parts[0]
    for q in range(1, n_dom):
        total += parts[q]
    bias[...] = total[chunk : chunk + 1, :]
    rows = total[:chunk, :].astype(BF16)
    for q in range(n_dom):
        out[q] = rows


def sum_parts(parts):
    n_dom, rows, width = parts.shape
    return pl.pallas_call(
        sum_kernel,
        out_shape=(pltpu.HBM((n_dom, rows - 8, width), BF16), pltpu.HBM((1, width), F32)),
        in_specs=[VMEM],
        out_specs=(VMEM, VMEM),
        compiler_params=params(),
        cost_estimate=cost(0, 1 << 20),
        name="sum_parts",
    )(hbm(parts))


def place_kernel(me_s, sums, self_out, neigh_out):
    rows, width = self_out.shape
    for i in range(2 * rows // width):
        which, k = divmod(i, rows // width)
        target = (self_out, neigh_out)[which]
        at = pl.ds(pl.multiple_of((me_s[0] ^ k) * width, width), width)
        target[at, :] = sums[i * width : (i + 1) * width, :].astype(F32)


def place_weights(me, sums):
    rows, width = sums.shape[0] // 2, sums.shape[1]
    return pl.pallas_call(
        place_kernel,
        out_shape=(pltpu.HBM((rows, width), F32),) * 2,
        in_specs=[SMEM, VMEM],
        out_specs=(VMEM, VMEM),
        compiler_params=params(),
        cost_estimate=cost(0, 1 << 20),
        name="place_weights",
    )(me, sums)


def body(
    node_feats,
    edge_tiles,
    tile_dst,
    tile_src,
    hub_ids,
    send_rows,
    send_count,
    w_self,
    w_neigh,
    out_bias,
    grad_out,
    *,
    n_feat,
):
    own_count, width = node_feats.shape
    tile_size = edge_tiles.shape[1]
    listed = send_rows[0]
    n_dom, capacity = listed.shape
    hub_dev = hub_ids.shape[0]
    me = lax.axis_index("feat").astype(jnp.int32)
    me_s = me.reshape(1)
    far, near = 2, 1
    assert n_feat == 4
    far_blocks = n_dom * hub_dev // tile_size + n_dom

    def swap(x, k):
        return lax.ppermute(x, "feat", [(j, j ^ k) for j in range(n_feat)])

    feat_far = swap(node_feats, far)

    outgoing = pick(listed, send_count, hub_ids, node_feats)
    incoming = lax.all_to_all(outgoing, "dom", 0, 0, tiled=True)
    own_feats = node_feats.reshape(-1, tile_size, width)
    base, lists = own_tiles(tile_dst, tile_src, edge_tiles, own_feats, far_blocks)
    aggregated = far_tiles(lists, edge_tiles, incoming, base, far_blocks).reshape(own_count, width)

    agg_far = swap(aggregated, far)
    feat_far, aggregated = lax.optimization_barrier((feat_far, aggregated))
    feats = [hbm(node_feats), swap(node_feats, near), feat_far, swap(feat_far, near)]
    flops = 2 * own_count * n_feat * width * width
    rows_out = ((own_count, width), BF16)
    (own_part,) = stream_call(
        self_step,
        me_s,
        feats,
        [w_self, out_bias[None, :]],
        [((own_count, width), F32)],
        flops,
        "self_dense",
    )
    cut = cut_weights(me_s, w_self, w_neigh, n_feat)
    agg_far, own_part, *cut = lax.optimization_barrier((agg_far, own_part, *cut))
    w_rows = [hbm(cut[0])] + [swap(cut[k], k) for k in range(1, n_feat)]
    aggs = [hbm(aggregated), swap(aggregated, near), agg_far, swap(agg_far, near)]
    output, grad_pre = stream_call(
        forward_step,
        me_s,
        [*aggs, hbm(own_part), hbm(grad_out)],
        [w_neigh],
        [rows_out, rows_out],
        flops,
        "forward_dense",
    )

    grad_far = swap(grad_pre, far)
    parts = weight_parts(feats + aggs, hbm(grad_pre), n_dom)
    part_sums = lax.all_to_all(parts, "dom", 0, 0, tiled=True)
    grads = [hbm(grad_pre), swap(grad_pre, near), grad_far, swap(grad_far, near)]

    back_out, back_agg, direct = back_far(
        lists, edge_tiles, grads, w_rows, n_dom, hub_dev, tile_size
    )
    back_in = lax.all_to_all(back_out, "dom", 0, 0, tiled=True)
    own = back_own(lists, edge_tiles, back_agg, direct).reshape(own_count, width)
    weights_out, grad_bias = sum_parts(part_sums)
    weights_out, back_in, own = lax.optimization_barrier((weights_out, back_in, own))
    weights_in = lax.all_to_all(weights_out, "dom", 0, 0, tiled=True)
    grad_feats = finish(listed, send_count, hub_ids, back_in, own)
    grad_self, grad_neigh = place_weights(me_s, weights_in.reshape(-1, width))
    return (output, grad_feats, grad_self, grad_neigh, grad_bias[0])


def solution(mesh):
    in_specs = (
        P("dom", "feat"),
        P("dom", None, None),
        P("dom"),
        P("dom"),
        P("dom"),
        P("dom", None, None),
        P("dom", None),
        P(None, "feat"),
        P(None, "feat"),
        P("feat"),
        P("dom", "feat"),
    )
    out_specs = (P("dom", "feat"), P("dom", "feat"), P(None, "feat"), P(None, "feat"), P("feat"))
    n_feat = mesh.shape["feat"]

    def run(*args):
        return body(*args, n_feat=n_feat)

    return jax.shard_map(run, mesh=mesh, in_specs=in_specs, out_specs=out_specs, check_vma=False)
```

```python
import functools

import jax
import jax.numpy as jnp
from jax import lax
from jax.experimental import pallas as pl
from jax.experimental.pallas import tpu as pltpu
from jax.sharding import PartitionSpec as P

F32 = jnp.float32
BF16 = jnp.bfloat16
VMEM = pl.BlockSpec(memory_space=pltpu.VMEM)
SMEM = pl.BlockSpec(memory_space=pltpu.SMEM)
HBM = pl.BlockSpec(memory_space=pltpu.HBM)
ANY = pl.BlockSpec(memory_space=pl.ANY)
UNROLL = 8
CHUNKS = 2
T_BITS, S_BITS = 10, 10


def params(mib=24):
    return pltpu.CompilerParams(vmem_limit_bytes=mib << 20)


def hbm(x):
    return pltpu.with_memory_space_constraint(x, pltpu.HBM)


def cost(flops, nbytes):
    return pl.CostEstimate(flops=flops, bytes_accessed=nbytes, transcendentals=0)


def start_copies(sems, *pairs):
    copies = [pltpu.make_async_copy(a, b, sems.at[i]) for i, (a, b) in enumerate(pairs)]
    for copy in copies:
        copy.start()
    return copies


def wait_copies(copies):
    for copy in copies:
        copy.wait()


def pick_kernel(rows_h, count_h, hub_h, x_h, out_h, rows_s, count_s, hub_s, x, x32, stage, out, sems, out_sems):
    copies = start_copies(sems, (x_h, x), (rows_h, rows_s), (count_h, count_s), (hub_h, hub_s))
    n_dom, capacity = rows_s.shape
    hub_dev = hub_s.shape[0]
    step = 16
    wait_copies(copies)
    x32[...] = x[...].astype(F32)
    for j in range(hub_dev):
        stage[capacity + j : capacity + j + 1, :] = x32[pl.ds(hub_s[j], 1), :]
    hub = stage[capacity:, :].astype(BF16)
    slot = lax.broadcasted_iota(jnp.int32, (capacity, x.shape[1]), 0)

    def peer(q, carry):
        def some(g, carry):
            for u in range(step):
                c = g * step + u
                stage[pl.ds(c, 1), :] = x32[pl.ds(rows_s[q, c], 1), :]
            return carry

        lax.fori_loop(0, capacity // step, some, 0)
        kept = jnp.where(slot < count_s[0, q], stage[:capacity, :], 0.0)
        out[q, :capacity, :] = kept.astype(BF16)
        out[q, capacity:, :] = hub
        pltpu.make_async_copy(out.at[q], out_h.at[q], out_sems.at[q]).start()
        return carry

    lax.fori_loop(0, n_dom, peer, 0)
    for q in range(n_dom):
        pltpu.make_async_copy(out.at[q], out_h.at[q], out_sems.at[q]).wait()


def pick(send_rows, send_count, hub_ids, x):
    n_dom, capacity = send_rows.shape
    rows = capacity + hub_ids.shape[0]
    shape = (n_dom, rows, x.shape[1])
    return pl.pallas_call(
        pick_kernel,
        out_shape=pltpu.HBM(shape, BF16),
        in_specs=[HBM] * 4,
        out_specs=HBM,
        scratch_shapes=[
            pltpu.SMEM(send_rows.shape, jnp.int32),
            pltpu.SMEM(send_count.shape, jnp.int32),
            pltpu.SMEM(hub_ids.shape, jnp.int32),
            pltpu.VMEM(x.shape, BF16),
            pltpu.VMEM(x.shape, F32),
            pltpu.VMEM((rows, x.shape[1]), F32),
            pltpu.VMEM(shape, BF16),
            pltpu.SemaphoreType.DMA((4,)),
            pltpu.SemaphoreType.DMA((n_dom,)),
        ],
        compiler_params=params(),
        cost_estimate=cost(0, 1 << 21),
        name="pick_rows",
    )(hbm(send_rows), hbm(send_count), hbm(hub_ids), hbm(x))


def unpack(entry):
    t = entry & ((1 << T_BITS) - 1)
    s = (entry >> T_BITS) & ((1 << S_BITS) - 1)
    return t, s, entry >> (T_BITS + S_BITS)


def make_lists(dst_s, src_s, lists, own_blocks, far_blocks):
    length = lists.shape[1] - 1

    def step(t, n):
        s = src_s[t]
        d = dst_s[t]
        far = (s >= own_blocks).astype(jnp.int32)
        lists[0, n[0]] = t + (s << T_BITS) + (d << (T_BITS + S_BITS))
        lists[1, n[1]] = t + ((s - own_blocks) << T_BITS) + (d << (T_BITS + S_BITS))
        return n[0] + 1 - far, n[1] + far

    n = lax.fori_loop(0, dst_s.shape[0], step, (jnp.int32(0), jnp.int32(0)))
    for which, blocks in ((0, own_blocks), (1, far_blocks)):
        spare = (blocks << T_BITS) + (own_blocks << (T_BITS + S_BITS))
        for u in range(UNROLL - 1):
            lists[which, n[which] + u] = jnp.int32(spare)
        lists[which, length] = n[which]


def add_tiles(lists, which, tiles, source, acc, spare):
    n = lists[which, lists.shape[1] - 1]

    def group(g, carry):
        done = []
        for u in range(UNROLL):
            t, s, d = unpack(lists[which, g * UNROLL + u])
            s = jnp.where(d == spare, 0, s)
            done.append((d, jnp.dot(tiles[t], source[s], preferred_element_type=F32)))
        for d, product in done:
            acc[d] += product
        return carry

    lax.fori_loop(0, (n + UNROLL - 1) // UNROLL, group, 0)


def add_tiles_t(lists, which, tiles, source, acc, spare):
    n = lists[which, lists.shape[1] - 1]

    def group(g, carry):
        done = []
        for u in range(UNROLL):
            t, s, d = unpack(lists[which, g * UNROLL + u])
            d = jnp.where(d == spare, 0, d)
            product = lax.dot_general(
                tiles[t], source[d], (((0,), (0,)), ((), ())), preferred_element_type=F32
            )
            done.append((s, product))
        for s, product in done:
            acc[s] += product
        return carry

    lax.fori_loop(0, (n + UNROLL - 1) // UNROLL, group, 0)


def own_kernel(dst_h, src_h, tiles, x_h, out_h, lists, dst_s, src_s, x, acc, sems, *, far_blocks):
    own_blocks = x.shape[0]
    copies = start_copies(sems, (x_h, x), (dst_h, dst_s), (src_h, src_s))
    acc[...] = jnp.zeros_like(acc)
    wait_copies(copies)
    make_lists(dst_s, src_s, lists, own_blocks, far_blocks)
    add_tiles(lists, 0, tiles, x, acc, own_blocks)
    wait_copies(start_copies(sems, (acc.at[pl.ds(0, own_blocks)], out_h)))


def own_tiles(tile_dst, tile_src, tiles, x, far_blocks):
    n = tiles.shape[0]
    return pl.pallas_call(
        functools.partial(own_kernel, far_blocks=far_blocks),
        out_shape=(
            pltpu.HBM(x.shape, F32),
            jax.ShapeDtypeStruct((2, n + UNROLL), jnp.int32),
        ),
        in_specs=[HBM, HBM, VMEM, HBM],
        out_specs=(HBM, SMEM),
        scratch_shapes=[
            pltpu.SMEM((n,), jnp.int32),
            pltpu.SMEM((n,), jnp.int32),
            pltpu.VMEM(x.shape, BF16),
            pltpu.VMEM((x.shape[0] + 1,) + x.shape[1:], F32),
            pltpu.SemaphoreType.DMA((3,)),
        ],
        compiler_params=params(),
        cost_estimate=cost(2 * n * 128**3, 1 << 23),
        name="own_tiles",
    )(hbm(tile_dst), hbm(tile_src), tiles, hbm(x))


def far_kernel(lists, tiles, incoming_h, base_h, *refs):
    *outs_h, source, acc, out, sems = refs
    n_dom, rows, _ = incoming_h.shape
    own_blocks, tile, _ = base_h.shape
    hub_dev = rows - tile
    hub_blocks = n_dom * hub_dev // tile
    pairs = [(incoming_h.at[:, pl.ds(0, tile), :], source.at[pl.ds(hub_blocks, n_dom)])]
    pairs.append((base_h, acc.at[pl.ds(0, own_blocks)]))
    for q in range(n_dom):
        block, row = divmod(q * hub_dev, tile)
        pairs.append(
            (incoming_h.at[q, pl.ds(tile, hub_dev), :], source.at[block, pl.ds(row, hub_dev), :])
        )
    wait_copies(start_copies(sems, *pairs))
    add_tiles(lists, 1, tiles, source, acc, own_blocks)
    out[...] = acc[:own_blocks].astype(BF16)
    n = own_blocks // len(outs_h)
    wait_copies(
        start_copies(sems, *[(out.at[pl.ds(c * n, n)], o) for c, o in enumerate(outs_h)])
    )


def far_tiles(lists, tiles, incoming, base, far_blocks):
    own_blocks, tile, width = base.shape
    return pl.pallas_call(
        far_kernel,
        out_shape=(pltpu.HBM((own_blocks // CHUNKS, tile, width), BF16),) * CHUNKS,
        in_specs=[SMEM, VMEM, HBM, HBM],
        out_specs=(HBM,) * CHUNKS,
        scratch_shapes=[
            pltpu.VMEM((far_blocks, tile, width), BF16),
            pltpu.VMEM((own_blocks + 1, tile, width), F32),
            pltpu.VMEM(base.shape, BF16),
            pltpu.SemaphoreType.DMA((incoming.shape[0] + 2,)),
        ],
        compiler_params=params(),
        cost_estimate=cost(tiles.shape[0] * 128**3, 1 << 22),
        name="far_tiles",
    )(lists, tiles, hbm(incoming), hbm(base))


def forward_kernel(me_s, *refs, n_feat, chunk, block):
    n_in = 2 * n_feat + 1
    ins_h, refs = refs[:n_in], refs[n_in:]
    w_self, w_neigh, bias = refs[:3]
    output_h, grad_h, *refs = refs[-(n_in + 5) :]
    ins, (output, grad_pre, sems) = refs[:n_in], refs[n_in:]
    rows, width = output.shape
    first = chunk * rows
    pending = []
    for i in range(rows // block):
        at = pl.ds(i * block, block)
        there = pl.ds(first + i * block, block)
        pairs = [
            (a.at[at if n_feat <= j < 2 * n_feat else there], b.at[at])
            for j, (a, b) in enumerate(zip(ins_h, ins))
        ]
        pending.append(start_copies(sems.at[i], *pairs))

    def by_shard(w):
        return [
            w[pl.ds(pl.multiple_of((me_s[0] ^ k) * width, width), width), :] for k in range(n_feat)
        ]

    weights = jnp.concatenate(by_shard(w_self) + by_shard(w_neigh), axis=0)
    leaving = []
    for i in range(rows // block):
        at = slice(i * block, (i + 1) * block)
        wait_copies(pending[i])
        shards = jnp.concatenate([r[at, :] for r in ins[:-1]], axis=1)
        pre_act = jnp.dot(shards, weights, preferred_element_type=F32) + bias[...]
        gate = jax.nn.sigmoid(pre_act)
        output[at, :] = (pre_act * gate).astype(BF16)
        grad = ins[-1][at, :].astype(F32) * gate * (1.0 + pre_act * (1.0 - gate))
        grad_pre[at, :] = grad.astype(BF16)
        here = pl.ds(i * block, block)
        leaving += start_copies(
            sems.at[i, pl.ds(n_in, 2)],
            (output.at[here], output_h.at[pl.ds(first + i * block, block)]),
            (grad_pre.at[here], grad_h.at[here]),
        )
    wait_copies(leaving)


def forward(me, chunk, feats, aggs, w_self, w_neigh, bias, grad_out, output, block=256):
    n_feat = len(feats)
    rows, width = aggs[0].shape
    streamed = [*feats, *aggs, hbm(grad_out)]
    n_in = len(streamed)
    previous = [] if output is None else [output]
    return pl.pallas_call(
        functools.partial(forward_kernel, n_feat=n_feat, chunk=chunk, block=block),
        out_shape=(pltpu.HBM(grad_out.shape, BF16), pltpu.HBM((rows, width), BF16)),
        in_specs=[SMEM] + [ANY] * n_in + [VMEM] * 3 + [HBM] * len(previous),
        out_specs=(HBM, HBM),
        scratch_shapes=[pltpu.VMEM((rows, width), BF16)] * (n_in + 2)
        + [pltpu.SemaphoreType.DMA((rows // block, n_in + 2))],
        input_output_aliases={n_in + 4: 0} if previous else {},
        compiler_params=params(),
        cost_estimate=cost(4 * rows * width * n_feat * width, 1 << 22),
        name="forward_dense",
    )(me, *streamed, hbm(w_self), hbm(w_neigh), hbm(bias), *[hbm(p) for p in previous])


def weights_kernel(*refs, n_feat):
    n_agg = n_feat * CHUNKS
    feats_h, refs = refs[:n_feat], refs[n_feat:]
    aggs_h, refs = refs[:n_agg], refs[n_agg:]
    grads_h, out_h, refs = refs[:CHUNKS], refs[CHUNKS], refs[CHUNKS + 1 :]
    shards, refs = refs[: 2 * n_feat], refs[2 * n_feat :]
    grad, out, sems, shard_sems = refs
    n_dom, chunk = out.shape[0], out.shape[1] - 8
    rows, width = grad.shape
    piece = rows // CHUNKS
    part = lambda c: pl.ds(c * piece, piece)
    first = start_copies(sems, *[(g, grad.at[part(c)]) for c, g in enumerate(grads_h)])
    pending = []
    for k in range(n_feat):
        pending.append(start_copies(shard_sems.at[k], (feats_h[k], shards[k])))
    for k in range(n_feat):
        pairs = [(aggs_h[c * n_feat + k], shards[n_feat + k].at[part(c)]) for c in range(CHUNKS)]
        pending.append(start_copies(shard_sems.at[n_feat + k], *pairs))
    wait_copies(first)
    flipped = grad[...].T
    bias = jnp.sum(grad[...].astype(F32), axis=0, keepdims=True)
    for q in range(n_dom):
        out[q, chunk:, :] = jnp.broadcast_to(bias, (8, width))
    n = min(chunk, width)
    for i in range(0, 2 * n_feat, 2):
        wait_copies(pending[i])
        wait_copies(pending[i + 1])
        pair = jnp.concatenate([shards[i][...], shards[i + 1][...]], axis=1)
        blocks = jnp.dot(flipped, pair, preferred_element_type=F32).T
        for row in range(0, 2 * width, n):
            q, start = divmod(i * width + row, chunk)
            out[q, start : start + n, :] = blocks[row : row + n, :]
    wait_copies(start_copies(sems, (out, out_h)))


def weight_parts(feats, aggs, grads, n_dom):
    n_feat = len(feats)
    rows, width = feats[0].shape
    chunk = 2 * n_feat * width // n_dom
    flat = [*feats, *[a for chunk_aggs in aggs for a in chunk_aggs], *grads]
    return pl.pallas_call(
        functools.partial(weights_kernel, n_feat=n_feat),
        out_shape=pltpu.HBM((n_dom, chunk + 8, width), F32),
        in_specs=[ANY] * len(flat),
        out_specs=HBM,
        scratch_shapes=[pltpu.VMEM((rows, width), BF16)] * (2 * n_feat + 1)
        + [
            pltpu.VMEM((n_dom, chunk + 8, width), F32),
            pltpu.SemaphoreType.DMA((CHUNKS,)),
            pltpu.SemaphoreType.DMA((2 * n_feat, CHUNKS)),
        ],
        compiler_params=params(),
        cost_estimate=cost(4 * n_feat * width * width * rows, 1 << 22),
        name="weight_parts",
    )(*flat)


def split_copies(sems, pairs, block):
    rows = pairs[0][0].shape[0]
    return [
        start_copies(
            sems.at[i], *[(a.at[pl.ds(i * block, block)], b.at[pl.ds(i * block, block)]) for a, b in pairs]
        )
        for i in range(rows // block)
    ]


def back_far_kernel(*refs, n_feat):
    n_grads = n_feat * CHUNKS
    lists, tiles, *refs = refs
    grads_h, w, refs = refs[:n_grads], refs[n_grads : n_grads + n_feat], refs[n_grads + n_feat :]
    out_h, back_h, direct_h, *refs = refs
    grads, refs = refs[:n_grads], refs[n_grads:]
    back, direct, acc, out, sems, out_sems = refs
    n_dom = out.shape[0]
    own_blocks, tile, width = back.shape
    hub_dev = out.shape[1] - tile
    hub_blocks = n_dom * hub_dev // tile
    block = 4 * tile
    pending = []
    for c in range(CHUNKS):
        here = slice(c * n_feat, (c + 1) * n_feat)
        pairs = list(zip(grads_h[here], grads[here]))
        per_chunk = pairs[0][0].shape[0] // block
        pending += split_copies(sems.at[pl.ds(c * per_chunk, per_chunk)], pairs, block)
    acc[...] = jnp.zeros_like(acc)
    own_w, near_w, far_w, both_w = w
    rows = [r.reshape(2 * width, -1) for r in (own_w[...], near_w[...], far_w[0], both_w[1])]
    rows = jnp.concatenate(rows, axis=1)
    for i, copies in enumerate(pending):
        wait_copies(copies)
        c, at = divmod(i, per_chunk)
        at = slice(at * block, (at + 1) * block)
        whole = jnp.concatenate([g[at, :] for g in grads[c * n_feat : (c + 1) * n_feat]], axis=1)
        both = lax.dot_general(whole, rows, (((1,), (1,)), ((), ())), preferred_element_type=F32)
        direct[4 * i : 4 * (i + 1)] = both[:, :width].reshape(4, tile, width)
        back[4 * i : 4 * (i + 1)] = both[:, width:].astype(BF16).reshape(4, tile, width)
    leaving = start_copies(out_sems, (direct, direct_h), (back, back_h))
    add_tiles_t(lists, 1, tiles, back, acc, own_blocks)
    for q in range(n_dom):
        out[q, :tile, :] = acc[hub_blocks + q].astype(BF16)
        at, row = divmod(q * hub_dev, tile)
        out[q, tile:, :] = acc[at, row : row + hub_dev, :].astype(BF16)
    leaving += start_copies(out_sems.at[pl.ds(2, 1)], (out, out_h))
    wait_copies(leaving)


def back_far(lists, tiles, grads, w, n_dom, hub_dev, tile):
    n_feat = len(w)
    piece, width = grads[0].shape
    rows = piece * CHUNKS
    far_blocks = n_dom * hub_dev // tile + n_dom
    shape = (n_dom, tile + hub_dev, width)
    back_shape = (rows // tile, tile, width)
    return pl.pallas_call(
        functools.partial(back_far_kernel, n_feat=n_feat),
        out_shape=(pltpu.HBM(shape, BF16), pltpu.HBM(back_shape, BF16), pltpu.HBM(back_shape, F32)),
        in_specs=[SMEM, VMEM] + [ANY] * len(grads) + [VMEM] * n_feat,
        out_specs=(HBM, HBM, HBM),
        scratch_shapes=[pltpu.VMEM((piece, width), BF16)] * len(grads)
        + [
            pltpu.VMEM(back_shape, BF16),
            pltpu.VMEM(back_shape, F32),
            pltpu.VMEM((far_blocks + 1, tile, width), F32),
            pltpu.VMEM(shape, BF16),
            pltpu.SemaphoreType.DMA((rows // (4 * tile), n_feat)),
            pltpu.SemaphoreType.DMA((3,)),
        ],
        compiler_params=params(),
        cost_estimate=cost(45 * rows * width * width * n_feat, 1 << 12),
        name="back_far",
    )(lists, tiles, *grads, *w)


def back_own_kernel(lists, tiles, back_h, direct_h, out_h, back, acc, sems):
    own_blocks = back.shape[0]
    own = acc.at[pl.ds(0, own_blocks)]
    wait_copies(start_copies(sems, (back_h, back), (direct_h, own)))
    add_tiles_t(lists, 0, tiles, back, acc, own_blocks)
    wait_copies(start_copies(sems, (own, out_h)))


def back_own(lists, tiles, back, direct):
    return pl.pallas_call(
        back_own_kernel,
        out_shape=pltpu.HBM(direct.shape, F32),
        in_specs=[SMEM, VMEM, HBM, HBM],
        out_specs=HBM,
        scratch_shapes=[
            pltpu.VMEM(back.shape, BF16),
            pltpu.VMEM((direct.shape[0] + 1,) + direct.shape[1:], F32),
            pltpu.SemaphoreType.DMA((2,)),
        ],
        compiler_params=params(),
        cost_estimate=cost(2 * tiles.shape[0] * 128**3, 1 << 23),
        name="back_own",
    )(lists, tiles, hbm(back), hbm(direct))


def finish_kernel(rows_s, count_h, hub_h, incoming_h, base_h, out_h, count_s, hub_s, sent, hubs, base, sems, out_sems):
    n_dom, capacity = rows_s.shape
    hub_dev = hub_s.shape[0]
    own_count, width = base.shape
    block, peers = 256, min(8, n_dom)
    copies = start_copies(
        sems,
        (count_h, count_s),
        (hub_h, hub_s),
        (incoming_h.at[:, pl.ds(0, capacity), :], sent),
        (incoming_h.at[:, pl.ds(capacity, hub_dev), :], hubs),
        (base_h, base),
    )
    wait_copies(copies)
    hub = hubs[0].astype(F32)
    for q in range(1, n_dom):
        hub += hubs[q].astype(F32)
    for j in range(hub_dev):
        base[pl.ds(hub_s[j], 1), :] += hub[j : j + 1, :]
    lane = lax.broadcasted_iota(jnp.int32, (1, capacity), 1)
    leaving = []
    for start in range(0, own_count, block):
        vertex = lax.broadcasted_iota(jnp.int32, (block, capacity), 0) + start
        total = base[start : start + block, :]
        for first in range(0, n_dom, peers):
            hot, rows = [], []
            for q in range(first, first + peers):
                wanted = jnp.where(lane < count_s[0, q], rows_s[q : q + 1, :], -1)
                hot.append((vertex == wanted).astype(F32).astype(BF16))
                rows.append(sent[q])
            total += jnp.dot(
                jnp.concatenate(hot, axis=1),
                jnp.concatenate(rows, axis=0),
                preferred_element_type=F32,
            )
        base[start : start + block, :] = total
        at = pl.ds(start, block)
        leaving.append(start_copies(out_sems.at[pl.ds(start // block, 1)], (base.at[at], out_h.at[at])))
    for copies in leaving:
        wait_copies(copies)


def finish(send_rows, send_count, hub_ids, incoming, base):
    n_dom, capacity = send_rows.shape
    hub_dev = hub_ids.shape[0]
    own_count, width = base.shape
    return pl.pallas_call(
        finish_kernel,
        out_shape=pltpu.HBM(base.shape, F32),
        in_specs=[VMEM, HBM, HBM, ANY, HBM],
        out_specs=HBM,
        scratch_shapes=[
            pltpu.SMEM(send_count.shape, jnp.int32),
            pltpu.SMEM(hub_ids.shape, jnp.int32),
            pltpu.VMEM((n_dom, capacity, width), BF16),
            pltpu.VMEM((n_dom, hub_dev, width), BF16),
            pltpu.VMEM(base.shape, F32),
            pltpu.SemaphoreType.DMA((5,)),
            pltpu.SemaphoreType.DMA((own_count // 256,)),
        ],
        compiler_params=params(),
        cost_estimate=cost(2 * base.size * send_rows.size, 1 << 22),
        name="finish",
    )(hbm(send_rows), hbm(send_count), hbm(hub_ids), incoming, hbm(base))


def cut_kernel(me_s, w_self, w_neigh, *outs):
    width = w_self.shape[1]
    own, near, far = outs
    for k, out in enumerate((own, near, far.at[0], far.at[1])):
        at = pl.ds(pl.multiple_of((me_s[0] ^ k) * width, width), width)
        out[0] = w_self[at, :]
        out[1] = w_neigh[at, :]


def cut_weights(me, w_self, w_neigh):
    width = w_self.shape[1]
    one = (2, width, width)
    return pl.pallas_call(
        cut_kernel,
        out_shape=tuple(pltpu.HBM(shape, BF16) for shape in (one, one, (2,) + one)),
        in_specs=[SMEM, VMEM, VMEM],
        out_specs=(VMEM,) * 3,
        compiler_params=params(),
        cost_estimate=cost(0, 1 << 20),
        name="cut_weights",
    )(me, hbm(w_self), hbm(w_neigh))


def sum_kernel(parts, out, bias):
    n_dom, chunk, _ = out.shape
    total = parts[0]
    for q in range(1, n_dom):
        total += parts[q]
    bias[...] = total[chunk : chunk + 1, :]
    rows = total[:chunk, :].astype(BF16)
    for q in range(n_dom):
        out[q] = rows


def sum_parts(parts):
    n_dom, rows, width = parts.shape
    return pl.pallas_call(
        sum_kernel,
        out_shape=(pltpu.HBM((n_dom, rows - 8, width), BF16), pltpu.HBM((1, width), F32)),
        in_specs=[VMEM],
        out_specs=(VMEM, VMEM),
        compiler_params=params(),
        cost_estimate=cost(0, 1 << 20),
        name="sum_parts",
    )(hbm(parts))


def place_kernel(me_s, sums, self_out, neigh_out):
    rows, width = self_out.shape
    for i in range(2 * rows // width):
        which, k = divmod(i, rows // width)
        target = (self_out, neigh_out)[which]
        at = pl.ds(pl.multiple_of((me_s[0] ^ k) * width, width), width)
        target[at, :] = sums[i * width : (i + 1) * width, :].astype(F32)


def place_weights(me, sums):
    rows, width = sums.shape[0] // 2, sums.shape[1]
    return pl.pallas_call(
        place_kernel,
        out_shape=(pltpu.HBM((rows, width), F32),) * 2,
        in_specs=[SMEM, VMEM],
        out_specs=(VMEM, VMEM),
        compiler_params=params(),
        cost_estimate=cost(0, 1 << 20),
        name="place_weights",
    )(me, sums)


def body(
    node_feats,
    edge_tiles,
    tile_dst,
    tile_src,
    hub_ids,
    send_rows,
    send_count,
    w_self,
    w_neigh,
    out_bias,
    grad_out,
    *,
    n_feat,
):
    own_count, width = node_feats.shape
    tile_size = edge_tiles.shape[1]
    listed = send_rows[0]
    n_dom, capacity = listed.shape
    hub_dev = hub_ids.shape[0]
    me = lax.axis_index("feat").astype(jnp.int32)
    me_s = me.reshape(1)
    far, near = 2, 1
    assert n_feat == 4
    far_blocks = n_dom * hub_dev // tile_size + n_dom

    def swap(x, k):
        return lax.ppermute(x, "feat", [(j, j ^ k) for j in range(n_feat)])

    feat_far = swap(node_feats, far)

    outgoing = pick(listed, send_count, hub_ids, node_feats)
    incoming = lax.all_to_all(outgoing, "dom", 0, 0, tiled=True)
    own_feats = node_feats.reshape(-1, tile_size, width)
    base, lists = own_tiles(tile_dst, tile_src, edge_tiles, own_feats, far_blocks)
    pieces = far_tiles(lists, edge_tiles, incoming, base, far_blocks)
    pieces = [p.reshape(-1, width) for p in pieces]
    feat_far, *pieces = lax.optimization_barrier((feat_far, *pieces))
    feats = [hbm(node_feats), swap(node_feats, near), feat_far, swap(feat_far, near)]

    agg_far = [swap(p, far) for p in pieces]
    cut = cut_weights(me_s, w_self, w_neigh)
    agg_far[0], *cut = lax.optimization_barrier((agg_far[0], *cut))
    far_w = swap(cut[2], far)
    w_rows = [hbm(cut[0]), swap(cut[1], near), far_w, swap(far_w, near)]
    output, aggs, grads, grad_far = None, [], [], []
    for c in range(CHUNKS):
        if c:
            agg_far[c], grads[c - 1] = lax.optimization_barrier((agg_far[c], grads[c - 1]))
        shards = [hbm(pieces[c]), swap(pieces[c], near), agg_far[c], swap(agg_far[c], near)]
        output, grad = forward(
            me_s, c, feats, shards, w_self, w_neigh, out_bias[None, :], grad_out, output
        )
        aggs.append(shards)
        grads.append(grad)
        grad_far.append(swap(grad, far) if c == 0 else None)
    grad_far[0], grads[1] = lax.optimization_barrier((grad_far[0], grads[1]))
    grad_far[1] = swap(grads[1], far)
    parts = weight_parts(feats, aggs, [hbm(g) for g in grads], n_dom)
    part_sums = lax.all_to_all(parts, "dom", 0, 0, tiled=True)
    whole_grads = []
    for c in range(CHUNKS):
        whole_grads += [
            hbm(grads[c]), swap(grads[c], near), grad_far[c], swap(grad_far[c], near)
        ]

    back_out, back_agg, direct = back_far(
        lists, edge_tiles, whole_grads, w_rows, n_dom, hub_dev, tile_size
    )
    back_in = lax.all_to_all(back_out, "dom", 0, 0, tiled=True)
    own = back_own(lists, edge_tiles, back_agg, direct).reshape(own_count, width)
    weights_out, grad_bias = sum_parts(part_sums)
    weights_out, back_in, own = lax.optimization_barrier((weights_out, back_in, own))
    weights_in = lax.all_to_all(weights_out, "dom", 0, 0, tiled=True)
    grad_feats = finish(listed, send_count, hub_ids, back_in, own)
    grad_self, grad_neigh = place_weights(me_s, weights_in.reshape(-1, width))
    return (output, grad_feats, grad_self, grad_neigh, grad_bias[0])


def solution(mesh):
    in_specs = (
        P("dom", "feat"),
        P("dom", None, None),
        P("dom"),
        P("dom"),
        P("dom"),
        P("dom", None, None),
        P("dom", None),
        P(None, "feat"),
        P(None, "feat"),
        P("feat"),
        P("dom", "feat"),
    )
    out_specs = (P("dom", "feat"), P("dom", "feat"), P(None, "feat"), P(None, "feat"), P("feat"))
    n_feat = mesh.shape["feat"]

    def run(*args):
        return body(*args, n_feat=n_feat)

    return jax.shard_map(run, mesh=mesh, in_specs=in_specs, out_specs=out_specs, check_vma=False)
```

```python
import functools

import jax
import jax.numpy as jnp
from jax import lax
from jax.experimental import pallas as pl
from jax.experimental.pallas import tpu as pltpu
from jax.sharding import PartitionSpec as P

F32 = jnp.float32
BF16 = jnp.bfloat16
VMEM = pl.BlockSpec(memory_space=pltpu.VMEM)
SMEM = pl.BlockSpec(memory_space=pltpu.SMEM)
HBM = pl.BlockSpec(memory_space=pltpu.HBM)
ANY = pl.BlockSpec(memory_space=pl.ANY)
UNROLL = 8
T_BITS, S_BITS = 10, 10


def params(mib=24):
    return pltpu.CompilerParams(vmem_limit_bytes=mib << 20)


def hbm(x):
    return pltpu.with_memory_space_constraint(x, pltpu.HBM)


def cost(flops, nbytes):
    return pl.CostEstimate(flops=flops, bytes_accessed=nbytes, transcendentals=0)


def start_copies(sems, *pairs):
    copies = [pltpu.make_async_copy(a, b, sems.at[i]) for i, (a, b) in enumerate(pairs)]
    for copy in copies:
        copy.start()
    return copies


def wait_copies(copies):
    for copy in copies:
        copy.wait()


def pick_kernel(rows_h, count_h, hub_h, x_h, out_h, rows_s, count_s, hub_s, x, x32, stage, out, sems):
    copies = start_copies(sems, (x_h, x), (rows_h, rows_s), (count_h, count_s), (hub_h, hub_s))
    n_dom, capacity = rows_s.shape
    hub_dev = hub_s.shape[0]
    step = 16
    wait_copies(copies)
    x32[...] = x[...].astype(F32)
    for j in range(hub_dev):
        stage[capacity + j : capacity + j + 1, :] = x32[pl.ds(hub_s[j], 1), :]
    hub = stage[capacity:, :].astype(BF16)
    slot = lax.broadcasted_iota(jnp.int32, (capacity, x.shape[1]), 0)

    def peer(q, carry):
        def some(g, carry):
            for u in range(step):
                c = g * step + u
                stage[pl.ds(c, 1), :] = x32[pl.ds(rows_s[q, c], 1), :]
            return carry

        lax.fori_loop(0, capacity // step, some, 0)
        kept = jnp.where(slot < count_s[0, q], stage[:capacity, :], 0.0)
        out[q, :capacity, :] = kept.astype(BF16)
        out[q, capacity:, :] = hub
        return carry

    lax.fori_loop(0, n_dom, peer, 0)
    wait_copies(start_copies(sems, (out, out_h)))


def pick(send_rows, send_count, hub_ids, x):
    n_dom, capacity = send_rows.shape
    rows = capacity + hub_ids.shape[0]
    shape = (n_dom, rows, x.shape[1])
    return pl.pallas_call(
        pick_kernel,
        out_shape=pltpu.HBM(shape, BF16),
        in_specs=[HBM] * 4,
        out_specs=HBM,
        scratch_shapes=[
            pltpu.SMEM(send_rows.shape, jnp.int32),
            pltpu.SMEM(send_count.shape, jnp.int32),
            pltpu.SMEM(hub_ids.shape, jnp.int32),
            pltpu.VMEM(x.shape, BF16),
            pltpu.VMEM(x.shape, F32),
            pltpu.VMEM((rows, x.shape[1]), F32),
            pltpu.VMEM(shape, BF16),
            pltpu.SemaphoreType.DMA((4,)),
        ],
        compiler_params=params(),
        cost_estimate=cost(0, 1 << 21),
        name="pick_rows",
    )(hbm(send_rows), hbm(send_count), hbm(hub_ids), hbm(x))


def unpack(entry):
    t = entry & ((1 << T_BITS) - 1)
    s = (entry >> T_BITS) & ((1 << S_BITS) - 1)
    return t, s, entry >> (T_BITS + S_BITS)


def make_lists(dst_s, src_s, lists, own_blocks, far_blocks):
    length = lists.shape[1] - 1

    def step(t, n):
        s = src_s[t]
        d = dst_s[t]
        far = (s >= own_blocks).astype(jnp.int32)
        lists[0, n[0]] = t + (s << T_BITS) + (d << (T_BITS + S_BITS))
        lists[1, n[1]] = t + ((s - own_blocks) << T_BITS) + (d << (T_BITS + S_BITS))
        return n[0] + 1 - far, n[1] + far

    n = lax.fori_loop(0, dst_s.shape[0], step, (jnp.int32(0), jnp.int32(0)))
    for which, blocks in ((0, own_blocks), (1, far_blocks)):
        spare = (blocks << T_BITS) + (own_blocks << (T_BITS + S_BITS))
        for u in range(UNROLL - 1):
            lists[which, n[which] + u] = jnp.int32(spare)
        lists[which, length] = n[which]


def add_tiles(lists, which, tiles, source, acc, spare):
    n = lists[which, lists.shape[1] - 1]

    def group(g, carry):
        done = []
        for u in range(UNROLL):
            t, s, d = unpack(lists[which, g * UNROLL + u])
            s = jnp.where(d == spare, 0, s)
            done.append((d, jnp.dot(tiles[t], source[s], preferred_element_type=F32)))
        for d, product in done:
            acc[d] += product
        return carry

    lax.fori_loop(0, (n + UNROLL - 1) // UNROLL, group, 0)


def add_tiles_t(lists, which, tiles, source, acc, spare):
    n = lists[which, lists.shape[1] - 1]

    def group(g, carry):
        done = []
        for u in range(UNROLL):
            t, s, d = unpack(lists[which, g * UNROLL + u])
            d = jnp.where(d == spare, 0, d)
            product = lax.dot_general(
                tiles[t], source[d], (((0,), (0,)), ((), ())), preferred_element_type=F32
            )
            done.append((s, product))
        for s, product in done:
            acc[s] += product
        return carry

    lax.fori_loop(0, (n + UNROLL - 1) // UNROLL, group, 0)


def own_kernel(dst_h, src_h, tiles, x_h, out_h, lists, dst_s, src_s, x, acc, sems, *, far_blocks):
    own_blocks = x.shape[0]
    copies = start_copies(sems, (x_h, x), (dst_h, dst_s), (src_h, src_s))
    acc[...] = jnp.zeros_like(acc)
    wait_copies(copies)
    make_lists(dst_s, src_s, lists, own_blocks, far_blocks)
    add_tiles(lists, 0, tiles, x, acc, own_blocks)
    wait_copies(start_copies(sems, (acc.at[pl.ds(0, own_blocks)], out_h)))


def own_tiles(tile_dst, tile_src, tiles, x, far_blocks):
    n = tiles.shape[0]
    return pl.pallas_call(
        functools.partial(own_kernel, far_blocks=far_blocks),
        out_shape=(
            pltpu.HBM(x.shape, F32),
            jax.ShapeDtypeStruct((2, n + UNROLL), jnp.int32),
        ),
        in_specs=[HBM, HBM, VMEM, HBM],
        out_specs=(HBM, SMEM),
        scratch_shapes=[
            pltpu.SMEM((n,), jnp.int32),
            pltpu.SMEM((n,), jnp.int32),
            pltpu.VMEM(x.shape, BF16),
            pltpu.VMEM((x.shape[0] + 1,) + x.shape[1:], F32),
            pltpu.SemaphoreType.DMA((3,)),
        ],
        compiler_params=params(),
        cost_estimate=cost(2 * n * 128**3, 1 << 23),
        name="own_tiles",
    )(hbm(tile_dst), hbm(tile_src), tiles, hbm(x))


def far_kernel(lists, tiles, incoming_h, base_h, out_h, source, acc, out, sems):
    n_dom, rows, _ = incoming_h.shape
    own_blocks, tile, _ = base_h.shape
    hub_dev = rows - tile
    hub_blocks = n_dom * hub_dev // tile
    pairs = [(incoming_h.at[:, pl.ds(0, tile), :], source.at[pl.ds(hub_blocks, n_dom)])]
    pairs.append((base_h, acc.at[pl.ds(0, own_blocks)]))
    for q in range(n_dom):
        block, row = divmod(q * hub_dev, tile)
        pairs.append(
            (incoming_h.at[q, pl.ds(tile, hub_dev), :], source.at[block, pl.ds(row, hub_dev), :])
        )
    wait_copies(start_copies(sems, *pairs))
    add_tiles(lists, 1, tiles, source, acc, own_blocks)
    out[...] = acc[:own_blocks].astype(BF16)
    wait_copies(start_copies(sems, (out, out_h)))


def far_tiles(lists, tiles, incoming, base, far_blocks):
    own_blocks, tile, width = base.shape
    return pl.pallas_call(
        far_kernel,
        out_shape=pltpu.HBM(base.shape, BF16),
        in_specs=[SMEM, VMEM, HBM, HBM],
        out_specs=HBM,
        scratch_shapes=[
            pltpu.VMEM((far_blocks, tile, width), BF16),
            pltpu.VMEM((own_blocks + 1, tile, width), F32),
            pltpu.VMEM(base.shape, BF16),
            pltpu.SemaphoreType.DMA((incoming.shape[0] + 2,)),
        ],
        compiler_params=params(),
        cost_estimate=cost(tiles.shape[0] * 128**3, 1 << 22),
        name="far_tiles",
    )(lists, tiles, hbm(incoming), hbm(base))


def by_shards(me, shards, w):
    width = shards[0].shape[1]
    rows = [
        w[pl.ds(pl.multiple_of((me ^ k) * width, width), width), :] for k in range(len(shards))
    ]
    return jnp.dot(
        jnp.concatenate([s[...] for s in shards], axis=1),
        jnp.concatenate(rows, axis=0),
        preferred_element_type=F32,
    )


def stream(step, ins_h, ins, outs_h, outs, sems, block):
    rows = ins[0].shape[0]
    n_in = len(ins)
    pending = []
    for i in range(rows // block):
        at = pl.ds(i * block, block)
        pairs = [(a.at[at], b.at[at]) for a, b in zip(ins_h, ins)]
        pending.append(start_copies(sems.at[i], *pairs))
    leaving = []
    for i in range(rows // block):
        at = pl.ds(i * block, block)
        wait_copies(pending[i])
        step(at, [r.at[at] for r in ins], [r.at[at] for r in outs])
        pairs = [(a.at[at], b.at[at]) for a, b in zip(outs, outs_h)]
        leaving.append(start_copies(sems.at[i, pl.ds(n_in, len(outs))], *pairs))
    for copies in leaving:
        wait_copies(copies)


def stream_call(kernel, me, streamed, whole, outs, flops, name, block=512):
    rows = streamed[0].shape[0]
    n_in, n_whole, n_out = len(streamed), len(whole), len(outs)

    def run(me_s, *refs):
        ins_h, refs = refs[:n_in], refs[n_in:]
        held, refs = refs[:n_whole], refs[n_whole:]
        outs_h, refs = refs[:n_out], refs[n_out:]
        ins, refs = refs[:n_in], refs[n_in:]
        out, sems = refs[:n_out], refs[n_out]
        stream(
            lambda at, i, o: kernel(me_s[0], i, held, o), ins_h, ins, outs_h, out, sems, block
        )

    return pl.pallas_call(
        run,
        out_shape=tuple(pltpu.HBM(shape, t) for shape, t in outs),
        in_specs=[SMEM] + [ANY] * n_in + [VMEM] * n_whole,
        out_specs=(HBM,) * n_out,
        scratch_shapes=[pltpu.VMEM(x.shape, x.dtype) for x in streamed]
        + [pltpu.VMEM(shape, t) for shape, t in outs]
        + [pltpu.SemaphoreType.DMA((rows // block, n_in + n_out))],
        compiler_params=params(),
        cost_estimate=cost(flops, 1 << 22),
        name=name,
    )(me, *streamed, *[hbm(x) for x in whole])


def self_step(me, ins, held, outs):
    w, bias = held
    outs[0][...] = by_shards(me, ins, w) + bias[...]


def forward_step(me, ins, held, outs):
    *shards, own_part, grad_out = ins
    output, grad_pre = outs
    pre_act = own_part[...] + by_shards(me, shards, held[0])
    gate = jax.nn.sigmoid(pre_act)
    output[...] = (pre_act * gate).astype(BF16)
    grad = grad_out[...].astype(F32) * gate * (1.0 + pre_act * (1.0 - gate))
    grad_pre[...] = grad.astype(BF16)


def weights_kernel(*refs, n_feat):
    shards, grad, out_h, out, sems = refs[: 2 * n_feat], *refs[2 * n_feat :]
    n_dom, chunk = out.shape[0], out.shape[1] - 8
    width = grad.shape[1]
    flipped = grad[...].T
    bias = jnp.sum(grad[...].astype(F32), axis=0, keepdims=True)
    for i, shard in enumerate(shards):
        block = jnp.dot(flipped, shard[...], preferred_element_type=F32).T
        for row in range(0, width, min(chunk, width)):
            q, start = divmod(i * width + row, chunk)
            n = min(chunk, width)
            out[q, start : start + n, :] = block[row : row + n, :]
    for q in range(n_dom):
        out[q, chunk:, :] = jnp.broadcast_to(bias, (8, width))
    wait_copies(start_copies(sems, (out, out_h)))


def weight_parts(shards, grad, n_dom):
    n_feat = len(shards) // 2
    width = grad.shape[1]
    chunk = 2 * n_feat * width // n_dom
    return pl.pallas_call(
        functools.partial(weights_kernel, n_feat=n_feat),
        out_shape=pltpu.HBM((n_dom, chunk + 8, width), F32),
        in_specs=[VMEM] * (2 * n_feat + 1),
        out_specs=HBM,
        scratch_shapes=[
            pltpu.VMEM((n_dom, chunk + 8, width), F32),
            pltpu.SemaphoreType.DMA((1,)),
        ],
        compiler_params=params(),
        cost_estimate=cost(4 * n_feat * width * width * grad.shape[0], 1 << 22),
        name="weight_parts",
    )(*shards, grad)


def split_copies(sems, pairs, block):
    rows = pairs[0][0].shape[0]
    return [
        start_copies(
            sems.at[i], *[(a.at[pl.ds(i * block, block)], b.at[pl.ds(i * block, block)]) for a, b in pairs]
        )
        for i in range(rows // block)
    ]


def back_far_kernel(*refs, n_feat):
    lists, tiles = refs[:2]
    grads_h, w = refs[2 : 2 + n_feat], refs[2 + n_feat : 2 + 2 * n_feat]
    out_h, back_h, direct_h = refs[2 + 2 * n_feat : 5 + 2 * n_feat]
    grads = refs[5 + 2 * n_feat : 5 + 3 * n_feat]
    back, direct, acc, out, sems, out_sems = refs[5 + 3 * n_feat :]
    n_dom = out.shape[0]
    own_blocks, tile, width = back.shape
    hub_dev = out.shape[1] - tile
    hub_blocks = n_dom * hub_dev // tile
    block = 4 * tile
    pending = split_copies(sems, list(zip(grads_h, grads)), block)
    acc[...] = jnp.zeros_like(acc)
    own_w, near_w, far_w, both_w = w
    rows = [r.reshape(2 * width, -1) for r in (own_w[...], near_w[...], far_w[0], both_w[1])]
    rows = jnp.concatenate(rows, axis=1)
    for i, copies in enumerate(pending):
        wait_copies(copies)
        whole = jnp.concatenate([g[i * block : (i + 1) * block, :] for g in grads], axis=1)
        both = lax.dot_general(whole, rows, (((1,), (1,)), ((), ())), preferred_element_type=F32)
        direct[4 * i : 4 * (i + 1)] = both[:, :width].reshape(4, tile, width)
        back[4 * i : 4 * (i + 1)] = both[:, width:].astype(BF16).reshape(4, tile, width)
    leaving = start_copies(out_sems, (direct, direct_h), (back, back_h))
    add_tiles_t(lists, 1, tiles, back, acc, own_blocks)
    for q in range(n_dom):
        out[q, :tile, :] = acc[hub_blocks + q].astype(BF16)
        at, row = divmod(q * hub_dev, tile)
        out[q, tile:, :] = acc[at, row : row + hub_dev, :].astype(BF16)
    leaving += start_copies(out_sems.at[pl.ds(2, 1)], (out, out_h))
    wait_copies(leaving)


def back_far(lists, tiles, grads, w, n_dom, hub_dev, tile):
    n_feat = len(grads)
    rows, width = grads[0].shape
    far_blocks = n_dom * hub_dev // tile + n_dom
    shape = (n_dom, tile + hub_dev, width)
    back_shape = (rows // tile, tile, width)
    return pl.pallas_call(
        functools.partial(back_far_kernel, n_feat=n_feat),
        out_shape=(pltpu.HBM(shape, BF16), pltpu.HBM(back_shape, BF16), pltpu.HBM(back_shape, F32)),
        in_specs=[SMEM, VMEM] + [ANY] * n_feat + [VMEM] * n_feat,
        out_specs=(HBM, HBM, HBM),
        scratch_shapes=[pltpu.VMEM((rows, width), BF16)] * n_feat
        + [
            pltpu.VMEM(back_shape, BF16),
            pltpu.VMEM(back_shape, F32),
            pltpu.VMEM((far_blocks + 1, tile, width), F32),
            pltpu.VMEM(shape, BF16),
            pltpu.SemaphoreType.DMA((rows // (4 * tile), n_feat)),
            pltpu.SemaphoreType.DMA((3,)),
        ],
        compiler_params=params(),
        cost_estimate=cost(4 * rows * width * width * n_feat, 1 << 22),
        name="back_far",
    )(lists, tiles, *grads, *[hbm(r) for r in w])


def back_own_kernel(lists, tiles, back_h, direct_h, out_h, back, acc, sems):
    own_blocks = back.shape[0]
    own = acc.at[pl.ds(0, own_blocks)]
    wait_copies(start_copies(sems, (back_h, back), (direct_h, own)))
    add_tiles_t(lists, 0, tiles, back, acc, own_blocks)
    wait_copies(start_copies(sems, (own, out_h)))


def back_own(lists, tiles, back, direct):
    return pl.pallas_call(
        back_own_kernel,
        out_shape=pltpu.HBM(direct.shape, F32),
        in_specs=[SMEM, VMEM, HBM, HBM],
        out_specs=HBM,
        scratch_shapes=[
            pltpu.VMEM(back.shape, BF16),
            pltpu.VMEM((direct.shape[0] + 1,) + direct.shape[1:], F32),
            pltpu.SemaphoreType.DMA((2,)),
        ],
        compiler_params=params(),
        cost_estimate=cost(2 * tiles.shape[0] * 128**3, 1 << 23),
        name="back_own",
    )(lists, tiles, hbm(back), hbm(direct))


def finish_kernel(rows_s, count_h, hub_h, incoming_h, base_h, out_h, count_s, hub_s, sent, hubs, base, sems, out_sems):
    n_dom, capacity = rows_s.shape
    hub_dev = hub_s.shape[0]
    own_count, width = base.shape
    block, peers = 256, min(8, n_dom)
    copies = start_copies(
        sems,
        (count_h, count_s),
        (hub_h, hub_s),
        (incoming_h.at[:, pl.ds(0, capacity), :], sent),
        (incoming_h.at[:, pl.ds(capacity, hub_dev), :], hubs),
        (base_h, base),
    )
    wait_copies(copies)
    hub = hubs[0].astype(F32)
    for q in range(1, n_dom):
        hub += hubs[q].astype(F32)
    for j in range(hub_dev):
        base[pl.ds(hub_s[j], 1), :] += hub[j : j + 1, :]
    lane = lax.broadcasted_iota(jnp.int32, (1, capacity), 1)
    leaving = []
    for start in range(0, own_count, block):
        vertex = lax.broadcasted_iota(jnp.int32, (block, capacity), 0) + start
        total = base[start : start + block, :]
        for first in range(0, n_dom, peers):
            hot, rows = [], []
            for q in range(first, first + peers):
                wanted = jnp.where(lane < count_s[0, q], rows_s[q : q + 1, :], -1)
                hot.append((vertex == wanted).astype(F32).astype(BF16))
                rows.append(sent[q])
            total += jnp.dot(
                jnp.concatenate(hot, axis=1),
                jnp.concatenate(rows, axis=0),
                preferred_element_type=F32,
            )
        base[start : start + block, :] = total
        at = pl.ds(start, block)
        leaving.append(start_copies(out_sems.at[pl.ds(start // block, 1)], (base.at[at], out_h.at[at])))
    for copies in leaving:
        wait_copies(copies)


def finish(send_rows, send_count, hub_ids, incoming, base):
    n_dom, capacity = send_rows.shape
    hub_dev = hub_ids.shape[0]
    own_count, width = base.shape
    return pl.pallas_call(
        finish_kernel,
        out_shape=pltpu.HBM(base.shape, F32),
        in_specs=[VMEM, HBM, HBM, ANY, HBM],
        out_specs=HBM,
        scratch_shapes=[
            pltpu.SMEM(send_count.shape, jnp.int32),
            pltpu.SMEM(hub_ids.shape, jnp.int32),
            pltpu.VMEM((n_dom, capacity, width), BF16),
            pltpu.VMEM((n_dom, hub_dev, width), BF16),
            pltpu.VMEM(base.shape, F32),
            pltpu.SemaphoreType.DMA((5,)),
            pltpu.SemaphoreType.DMA((own_count // 256,)),
        ],
        compiler_params=params(),
        cost_estimate=cost(2 * base.size * send_rows.size, 1 << 22),
        name="finish",
    )(hbm(send_rows), hbm(send_count), hbm(hub_ids), incoming, hbm(base))


def cut_kernel(me_s, w_self, w_neigh, *outs):
    width = w_self.shape[1]
    own, near, far = outs
    for k, out in enumerate((own, near, far.at[0], far.at[1])):
        at = pl.ds(pl.multiple_of((me_s[0] ^ k) * width, width), width)
        out[0] = w_self[at, :]
        out[1] = w_neigh[at, :]


def cut_weights(me, w_self, w_neigh):
    width = w_self.shape[1]
    one = (2, width, width)
    return pl.pallas_call(
        cut_kernel,
        out_shape=tuple(pltpu.HBM(shape, BF16) for shape in (one, one, (2,) + one)),
        in_specs=[SMEM, VMEM, VMEM],
        out_specs=(VMEM,) * 3,
        compiler_params=params(),
        cost_estimate=cost(0, 1 << 20),
        name="cut_weights",
    )(me, hbm(w_self), hbm(w_neigh))


def sum_kernel(parts, out, bias):
    n_dom, chunk = parts.shape[0], out.shape[0]
    total = parts[0]
    for q in range(1, n_dom):
        total += parts[q]
    bias[...] = total[chunk : chunk + 1, :]
    out[...] = total[:chunk, :].astype(BF16)


def sum_parts(parts):
    _, rows, width = parts.shape
    return pl.pallas_call(
        sum_kernel,
        out_shape=(pltpu.HBM((rows - 8, width), BF16), pltpu.HBM((1, width), F32)),
        in_specs=[VMEM],
        out_specs=(VMEM, VMEM),
        compiler_params=params(),
        cost_estimate=cost(0, 1 << 20),
        name="sum_parts",
    )(hbm(parts))


def place_kernel(me_s, *refs, order):
    *sums, self_out, neigh_out = refs
    rows, width = self_out.shape
    chunk = 2 * rows // len(order)
    n = min(chunk, width)
    per_ref = sums[0].shape[0] // chunk
    for i, k in enumerate(order):
        ref, first = sums[i // per_ref], i % per_ref * chunk
        for part in range(0, chunk, n):
            row = (me_s[1] ^ k) * chunk + part
            feat = me_s[0] ^ (row // width % (rows // width))
            at = pl.ds(pl.multiple_of(feat * width + row % width, n), n)
            piece = ref[first + part : first + part + n, :].astype(F32)

            @pl.when(row < rows)
            def _():
                self_out[at, :] = piece

            @pl.when(row >= rows)
            def _():
                neigh_out[at, :] = piece


def place_weights(both, sums, order, rows):
    width = sums[0].shape[1]
    return pl.pallas_call(
        functools.partial(place_kernel, order=order),
        out_shape=(pltpu.HBM((rows, width), F32),) * 2,
        in_specs=[SMEM] + [VMEM] * len(sums),
        out_specs=(VMEM, VMEM),
        compiler_params=params(),
        cost_estimate=cost(0, 1 << 20),
        name="place_weights",
    )(both, *sums)


def body(
    node_feats,
    edge_tiles,
    tile_dst,
    tile_src,
    hub_ids,
    send_rows,
    send_count,
    w_self,
    w_neigh,
    out_bias,
    grad_out,
    *,
    n_feat,
):
    own_count, width = node_feats.shape
    tile_size = edge_tiles.shape[1]
    listed = send_rows[0]
    n_dom, capacity = listed.shape
    hub_dev = hub_ids.shape[0]
    me = lax.axis_index("feat").astype(jnp.int32)
    me_s = me.reshape(1)
    far, near = 2, 1
    assert n_feat == 4
    far_blocks = n_dom * hub_dev // tile_size + n_dom

    def swap(x, k):
        return lax.ppermute(x, "feat", [(j, j ^ k) for j in range(n_feat)])

    feat_far = swap(node_feats, far)

    outgoing = pick(listed, send_count, hub_ids, node_feats)
    incoming = lax.all_to_all(outgoing, "dom", 0, 0, tiled=True)
    own_feats = node_feats.reshape(-1, tile_size, width)
    base, lists = own_tiles(tile_dst, tile_src, edge_tiles, own_feats, far_blocks)
    aggregated = far_tiles(lists, edge_tiles, incoming, base, far_blocks).reshape(own_count, width)

    agg_far = swap(aggregated, far)
    feat_far, aggregated = lax.optimization_barrier((feat_far, aggregated))
    feats = [hbm(node_feats), swap(node_feats, near), feat_far, swap(feat_far, near)]
    flops = 2 * own_count * n_feat * width * width
    rows_out = ((own_count, width), BF16)
    (own_part,) = stream_call(
        self_step,
        me_s,
        feats,
        [w_self, out_bias[None, :]],
        [((own_count, width), F32)],
        flops,
        "self_dense",
    )
    cut = cut_weights(me_s, w_self, w_neigh)
    agg_far, own_part, *cut = lax.optimization_barrier((agg_far, own_part, *cut))
    far_w = swap(cut[2], far)
    w_rows = [cut[0], swap(cut[1], near), far_w, swap(far_w, near)]
    aggs = [hbm(aggregated), swap(aggregated, near), agg_far, swap(agg_far, near)]
    output, grad_pre = stream_call(
        forward_step,
        me_s,
        [*aggs, hbm(own_part), hbm(grad_out)],
        [w_neigh],
        [rows_out, rows_out],
        flops,
        "forward_dense",
    )

    grad_pre, *w_rows = lax.optimization_barrier((grad_pre, *w_rows))
    grad_far = swap(grad_pre, far)
    parts = weight_parts(feats + aggs, hbm(grad_pre), n_dom)
    part_sums = lax.all_to_all(parts, "dom", 0, 0, tiled=True)
    grads = [hbm(grad_pre), swap(grad_pre, near), grad_far, swap(grad_far, near)]

    back_out, back_agg, direct = back_far(
        lists, edge_tiles, grads, w_rows, n_dom, hub_dev, tile_size
    )
    part_sums, back_out = lax.optimization_barrier((part_sums, back_out))
    back_in = lax.all_to_all(back_out, "dom", 0, 0, tiled=True)
    own = back_own(lists, edge_tiles, back_agg, direct).reshape(own_count, width)
    weights, grad_bias = sum_parts(part_sums)
    sums, chunk_of, bit = [weights], [0], n_dom // 2
    while bit:
        weights = jnp.concatenate(sums, axis=0)
        sums = [weights, lax.ppermute(weights, "dom", [(j, j ^ bit) for j in range(n_dom)])]
        chunk_of += [k ^ bit for k in chunk_of]
        bit //= 2
    grad_feats = finish(listed, send_count, hub_ids, back_in, own)
    both = jnp.stack([me, lax.axis_index("dom").astype(jnp.int32)])
    grad_self, grad_neigh = place_weights(both, sums, chunk_of, n_feat * width)
    return (output, grad_feats, grad_self, grad_neigh, grad_bias[0])


def solution(mesh):
    in_specs = (
        P("dom", "feat"),
        P("dom", None, None),
        P("dom"),
        P("dom"),
        P("dom"),
        P("dom", None, None),
        P("dom", None),
        P(None, "feat"),
        P(None, "feat"),
        P("feat"),
        P("dom", "feat"),
    )
    out_specs = (P("dom", "feat"), P("dom", "feat"), P(None, "feat"), P(None, "feat"), P("feat"))
    n_feat = mesh.shape["feat"]

    def run(*args):
        return body(*args, n_feat=n_feat)

    return jax.shard_map(run, mesh=mesh, in_specs=in_specs, out_specs=out_specs, check_vma=False)
```

```python
import functools

import jax
import jax.numpy as jnp
from jax import lax
from jax.experimental import pallas as pl
from jax.experimental.pallas import tpu as pltpu
from jax.sharding import PartitionSpec as P

F32 = jnp.float32
BF16 = jnp.bfloat16
VMEM = pl.BlockSpec(memory_space=pltpu.VMEM)
SMEM = pl.BlockSpec(memory_space=pltpu.SMEM)
HBM = pl.BlockSpec(memory_space=pltpu.HBM)
ANY = pl.BlockSpec(memory_space=pl.ANY)
UNROLL = 8
T_BITS, S_BITS = 10, 10


def params(mib=24):
    return pltpu.CompilerParams(vmem_limit_bytes=mib << 20)


def hbm(x):
    return pltpu.with_memory_space_constraint(x, pltpu.HBM)


def cost(flops, nbytes):
    return pl.CostEstimate(flops=flops, bytes_accessed=nbytes, transcendentals=0)


def start_copies(sems, *pairs):
    copies = [pltpu.make_async_copy(a, b, sems.at[i]) for i, (a, b) in enumerate(pairs)]
    for copy in copies:
        copy.start()
    return copies


def wait_copies(copies):
    for copy in copies:
        copy.wait()


def pick_kernel(rows_h, count_h, hub_h, x_h, out_h, rows_s, count_s, hub_s, x, x32, stage, out, sems):
    copies = start_copies(sems, (x_h, x), (rows_h, rows_s), (count_h, count_s), (hub_h, hub_s))
    n_dom, capacity = rows_s.shape
    hub_dev = hub_s.shape[0]
    step = 16
    wait_copies(copies)
    x32[...] = x[...].astype(F32)
    for j in range(hub_dev):
        stage[capacity + j : capacity + j + 1, :] = x32[pl.ds(hub_s[j], 1), :]
    hub = stage[capacity:, :].astype(BF16)
    slot = lax.broadcasted_iota(jnp.int32, (capacity, x.shape[1]), 0)

    def peer(q, carry):
        def some(g, carry):
            for u in range(step):
                c = g * step + u
                stage[pl.ds(c, 1), :] = x32[pl.ds(rows_s[q, c], 1), :]
            return carry

        lax.fori_loop(0, capacity // step, some, 0)
        kept = jnp.where(slot < count_s[0, q], stage[:capacity, :], 0.0)
        out[q, :capacity, :] = kept.astype(BF16)
        out[q, capacity:, :] = hub
        return carry

    lax.fori_loop(0, n_dom, peer, 0)
    wait_copies(start_copies(sems, (out, out_h)))


def pick(send_rows, send_count, hub_ids, x):
    n_dom, capacity = send_rows.shape
    rows = capacity + hub_ids.shape[0]
    shape = (n_dom, rows, x.shape[1])
    return pl.pallas_call(
        pick_kernel,
        out_shape=pltpu.HBM(shape, BF16),
        in_specs=[HBM] * 4,
        out_specs=HBM,
        scratch_shapes=[
            pltpu.SMEM(send_rows.shape, jnp.int32),
            pltpu.SMEM(send_count.shape, jnp.int32),
            pltpu.SMEM(hub_ids.shape, jnp.int32),
            pltpu.VMEM(x.shape, BF16),
            pltpu.VMEM(x.shape, F32),
            pltpu.VMEM((rows, x.shape[1]), F32),
            pltpu.VMEM(shape, BF16),
            pltpu.SemaphoreType.DMA((4,)),
        ],
        compiler_params=params(),
        cost_estimate=cost(0, 1 << 21),
        name="pick_rows",
    )(hbm(send_rows), hbm(send_count), hbm(hub_ids), hbm(x))


def unpack(entry):
    t = entry & ((1 << T_BITS) - 1)
    s = (entry >> T_BITS) & ((1 << S_BITS) - 1)
    return t, s, entry >> (T_BITS + S_BITS)


def make_lists(dst_s, src_s, lists, own_blocks, far_blocks):
    length = lists.shape[1] - 1

    def step(t, n):
        s = src_s[t]
        d = dst_s[t]
        far = (s >= own_blocks).astype(jnp.int32)
        lists[0, n[0]] = t + (s << T_BITS) + (d << (T_BITS + S_BITS))
        lists[1, n[1]] = t + ((s - own_blocks) << T_BITS) + (d << (T_BITS + S_BITS))
        return n[0] + 1 - far, n[1] + far

    n = lax.fori_loop(0, dst_s.shape[0], step, (jnp.int32(0), jnp.int32(0)))
    for which, blocks in ((0, own_blocks), (1, far_blocks)):
        spare = (blocks << T_BITS) + (own_blocks << (T_BITS + S_BITS))
        for u in range(UNROLL - 1):
            lists[which, n[which] + u] = jnp.int32(spare)
        lists[which, length] = n[which]


def add_tiles(lists, which, tiles, source, acc, spare):
    n = lists[which, lists.shape[1] - 1]

    def group(g, carry):
        done = []
        for u in range(UNROLL):
            t, s, d = unpack(lists[which, g * UNROLL + u])
            s = jnp.where(d == spare, 0, s)
            done.append((d, jnp.dot(tiles[t], source[s], preferred_element_type=F32)))
        for d, product in done:
            acc[d] += product
        return carry

    lax.fori_loop(0, (n + UNROLL - 1) // UNROLL, group, 0)


def add_tiles_t(lists, which, tiles, source, acc, spare):
    n = lists[which, lists.shape[1] - 1]

    def group(g, carry):
        done = []
        for u in range(UNROLL):
            t, s, d = unpack(lists[which, g * UNROLL + u])
            d = jnp.where(d == spare, 0, d)
            product = lax.dot_general(
                tiles[t], source[d], (((0,), (0,)), ((), ())), preferred_element_type=F32
            )
            done.append((s, product))
        for s, product in done:
            acc[s] += product
        return carry

    lax.fori_loop(0, (n + UNROLL - 1) // UNROLL, group, 0)


def own_kernel(
    dst_h, src_h, tiles_h, x_h, out_h, lists, dst_s, src_s, x, tiles, acc, sems, *, far_blocks
):
    own_blocks = x.shape[0]
    copies = start_copies(sems, (dst_h, dst_s), (src_h, src_s), (x_h, x), (tiles_h, tiles))
    acc[...] = jnp.zeros_like(acc)
    wait_copies(copies[:2])
    make_lists(dst_s, src_s, lists, own_blocks, far_blocks)
    wait_copies(copies[2:])
    add_tiles(lists, 0, tiles, x, acc, own_blocks)
    wait_copies(start_copies(sems, (acc.at[pl.ds(0, own_blocks)], out_h)))


def own_tiles(tile_dst, tile_src, tiles, x, far_blocks):
    n = tiles.shape[0]
    return pl.pallas_call(
        functools.partial(own_kernel, far_blocks=far_blocks),
        out_shape=(
            pltpu.HBM(x.shape, F32),
            jax.ShapeDtypeStruct((2, n + UNROLL), jnp.int32),
        ),
        in_specs=[HBM, HBM, HBM, HBM],
        out_specs=(HBM, SMEM),
        scratch_shapes=[
            pltpu.SMEM((n,), jnp.int32),
            pltpu.SMEM((n,), jnp.int32),
            pltpu.VMEM(x.shape, BF16),
            pltpu.VMEM(tiles.shape, BF16),
            pltpu.VMEM((x.shape[0] + 1,) + x.shape[1:], F32),
            pltpu.SemaphoreType.DMA((4,)),
        ],
        compiler_params=params(),
        cost_estimate=cost(2 * n * 128**3, 1 << 23),
        name="own_tiles",
    )(hbm(tile_dst), hbm(tile_src), hbm(tiles), hbm(x))


def far_kernel(lists, tiles, incoming_h, base_h, out_h, source, acc, out, sems):
    n_dom, rows, _ = incoming_h.shape
    own_blocks, tile, _ = base_h.shape
    hub_dev = rows - tile
    hub_blocks = n_dom * hub_dev // tile
    pairs = [(incoming_h.at[:, pl.ds(0, tile), :], source.at[pl.ds(hub_blocks, n_dom)])]
    pairs.append((base_h, acc.at[pl.ds(0, own_blocks)]))
    for q in range(n_dom):
        block, row = divmod(q * hub_dev, tile)
        pairs.append(
            (incoming_h.at[q, pl.ds(tile, hub_dev), :], source.at[block, pl.ds(row, hub_dev), :])
        )
    wait_copies(start_copies(sems, *pairs))
    add_tiles(lists, 1, tiles, source, acc, own_blocks)
    out[...] = acc[:own_blocks].astype(BF16)
    wait_copies(start_copies(sems, (out, out_h)))


def far_tiles(lists, tiles, incoming, base, far_blocks):
    own_blocks, tile, width = base.shape
    return pl.pallas_call(
        far_kernel,
        out_shape=pltpu.HBM(base.shape, BF16),
        in_specs=[SMEM, VMEM, HBM, HBM],
        out_specs=HBM,
        scratch_shapes=[
            pltpu.VMEM((far_blocks, tile, width), BF16),
            pltpu.VMEM((own_blocks + 1, tile, width), F32),
            pltpu.VMEM(base.shape, BF16),
            pltpu.SemaphoreType.DMA((incoming.shape[0] + 2,)),
        ],
        compiler_params=params(),
        cost_estimate=cost(tiles.shape[0] * 128**3, 1 << 22),
        name="far_tiles",
    )(lists, tiles, hbm(incoming), hbm(base))


def by_shards(me, shards, w):
    width = shards[0].shape[1]
    rows = [
        w[pl.ds(pl.multiple_of((me ^ k) * width, width), width), :] for k in range(len(shards))
    ]
    return jnp.dot(
        jnp.concatenate([s[...] for s in shards], axis=1),
        jnp.concatenate(rows, axis=0),
        preferred_element_type=F32,
    )


def stream(step, ins_h, ins, outs_h, outs, sems, block):
    rows = ins[0].shape[0]
    n_in = len(ins)
    pending = []
    for i in range(rows // block):
        at = pl.ds(i * block, block)
        pairs = [(a.at[at], b.at[at]) for a, b in zip(ins_h, ins)]
        pending.append(start_copies(sems.at[i], *pairs))
    leaving = []
    for i in range(rows // block):
        at = pl.ds(i * block, block)
        wait_copies(pending[i])
        step(at, [r.at[at] for r in ins], [r.at[at] for r in outs])
        pairs = [(a.at[at], b.at[at]) for a, b in zip(outs, outs_h)]
        leaving.append(start_copies(sems.at[i, pl.ds(n_in, len(outs))], *pairs))
    for copies in leaving:
        wait_copies(copies)


def stream_call(kernel, me, streamed, whole, outs, flops, name, block=512):
    rows = streamed[0].shape[0]
    n_in, n_whole, n_out = len(streamed), len(whole), len(outs)

    def run(me_s, *refs):
        ins_h, refs = refs[:n_in], refs[n_in:]
        held, refs = refs[:n_whole], refs[n_whole:]
        outs_h, refs = refs[:n_out], refs[n_out:]
        ins, refs = refs[:n_in], refs[n_in:]
        out, sems = refs[:n_out], refs[n_out]
        stream(
            lambda at, i, o: kernel(me_s[0], i, held, o), ins_h, ins, outs_h, out, sems, block
        )

    return pl.pallas_call(
        run,
        out_shape=tuple(pltpu.HBM(shape, t) for shape, t in outs),
        in_specs=[SMEM] + [ANY] * n_in + [VMEM] * n_whole,
        out_specs=(HBM,) * n_out,
        scratch_shapes=[pltpu.VMEM(x.shape, x.dtype) for x in streamed]
        + [pltpu.VMEM(shape, t) for shape, t in outs]
        + [pltpu.SemaphoreType.DMA((rows // block, n_in + n_out))],
        compiler_params=params(),
        cost_estimate=cost(flops, 1 << 22),
        name=name,
    )(me, *streamed, *[hbm(x) for x in whole])


def self_step(me, ins, held, outs):
    w, bias = held
    outs[0][...] = by_shards(me, ins, w) + bias[...]


def forward_step(me, ins, held, outs):
    *shards, own_part, grad_out = ins
    output, grad_pre = outs
    pre_act = own_part[...] + by_shards(me, shards, held[0])
    gate = jax.nn.sigmoid(pre_act)
    output[...] = (pre_act * gate).astype(BF16)
    grad = grad_out[...].astype(F32) * gate * (1.0 + pre_act * (1.0 - gate))
    grad_pre[...] = grad.astype(BF16)


def weights_kernel(*refs, n_feat):
    shards, grad, out_h, out, sems = refs[: 2 * n_feat], *refs[2 * n_feat :]
    n_dom, chunk = out.shape[0], out.shape[1] - 16
    width = grad.shape[1]
    flipped = grad[...].T
    bias = jnp.sum(grad[...].astype(F32), axis=0, keepdims=True)
    for i, shard in enumerate(shards):
        block = jnp.dot(flipped, shard[...], preferred_element_type=F32).T
        for row in range(0, width, min(chunk, width)):
            q, start = divmod(i * width + row, chunk)
            n = min(chunk, width)
            out[q, start : start + n, :] = block[row : row + n, :].astype(BF16)
    line = lax.broadcasted_iota(jnp.int32, (16, width), 0)
    terms, left = jnp.zeros((16, width), F32), jnp.broadcast_to(bias, (16, width))
    for i in range(3):
        term = left.astype(BF16).astype(F32)
        terms = jnp.where(line == i, term, terms)
        left = left - term
    for q in range(n_dom):
        out[q, chunk:, :] = terms.astype(BF16)
    wait_copies(start_copies(sems, (out, out_h)))


def weight_parts(shards, grad, n_dom):
    n_feat = len(shards) // 2
    width = grad.shape[1]
    chunk = 2 * n_feat * width // n_dom
    return pl.pallas_call(
        functools.partial(weights_kernel, n_feat=n_feat),
        out_shape=pltpu.HBM((n_dom, chunk + 16, width), BF16),
        in_specs=[VMEM] * (2 * n_feat + 1),
        out_specs=HBM,
        scratch_shapes=[
            pltpu.VMEM((n_dom, chunk + 16, width), BF16),
            pltpu.SemaphoreType.DMA((1,)),
        ],
        compiler_params=params(),
        cost_estimate=cost(4 * n_feat * width * width * grad.shape[0], 1 << 22),
        name="weight_parts",
    )(*shards, grad)


def split_copies(sems, pairs, block):
    rows = pairs[0][0].shape[0]
    return [
        start_copies(
            sems.at[i], *[(a.at[pl.ds(i * block, block)], b.at[pl.ds(i * block, block)]) for a, b in pairs]
        )
        for i in range(rows // block)
    ]


def back_far_kernel(*refs, n_feat):
    lists, tiles, parts_h, *refs = refs
    grads_h, w, refs = refs[:n_feat], refs[n_feat : 2 * n_feat], refs[2 * n_feat :]
    out_h, back_h, direct_h, bias, *refs = refs
    grads, refs = refs[:n_feat], refs[n_feat:]
    back, direct, acc, out, parts, sems, out_sems, parts_sem = refs
    n_dom = out.shape[0]
    own_blocks, tile, width = back.shape
    chunk = parts.shape[1] - 16
    hub_dev = out.shape[1] - tile - chunk
    hub_blocks = n_dom * hub_dev // tile
    block = 4 * tile
    pending = split_copies(sems, list(zip(grads_h, grads)), block)
    parts_copy = start_copies(parts_sem, (parts_h, parts))
    acc[...] = jnp.zeros_like(acc)
    own_w, near_w, far_w, both_w = w
    rows = [r.reshape(2 * width, -1) for r in (own_w[...], near_w[...], far_w[0], both_w[1])]
    rows = jnp.concatenate(rows, axis=1)
    for i, copies in enumerate(pending):
        wait_copies(copies)
        whole = jnp.concatenate([g[i * block : (i + 1) * block, :] for g in grads], axis=1)
        both = lax.dot_general(whole, rows, (((1,), (1,)), ((), ())), preferred_element_type=F32)
        direct[4 * i : 4 * (i + 1)] = both[:, :width].reshape(4, tile, width)
        back[4 * i : 4 * (i + 1)] = both[:, width:].astype(BF16).reshape(4, tile, width)
    leaving = start_copies(out_sems, (direct, direct_h), (back, back_h))
    wait_copies(parts_copy)
    total = parts[0].astype(F32)
    for q in range(1, n_dom):
        total += parts[q].astype(F32)
    bias[...] = total[chunk : chunk + 1, :] + total[chunk + 1 : chunk + 2, :] + total[chunk + 2 : chunk + 3, :]
    weights = total[:chunk, :].astype(BF16)
    add_tiles_t(lists, 1, tiles, back, acc, own_blocks)
    for q in range(n_dom):
        out[q, :tile, :] = acc[hub_blocks + q].astype(BF16)
        at, row = divmod(q * hub_dev, tile)
        out[q, tile : tile + hub_dev, :] = acc[at, row : row + hub_dev, :].astype(BF16)
        out[q, tile + hub_dev :, :] = weights
    leaving += start_copies(out_sems.at[pl.ds(2, 1)], (out, out_h))
    wait_copies(leaving)


def back_far(lists, tiles, part_sums, grads, w, hub_dev, tile):
    n_feat = len(grads)
    n_dom, part_rows, _ = part_sums.shape
    rows, width = grads[0].shape
    far_blocks = n_dom * hub_dev // tile + n_dom
    shape = (n_dom, tile + hub_dev + part_rows - 16, width)
    back_shape = (rows // tile, tile, width)
    return pl.pallas_call(
        functools.partial(back_far_kernel, n_feat=n_feat),
        out_shape=(
            pltpu.HBM(shape, BF16),
            pltpu.HBM(back_shape, BF16),
            pltpu.HBM(back_shape, F32),
            pltpu.HBM((1, width), F32),
        ),
        in_specs=[SMEM, VMEM, ANY] + [ANY] * n_feat + [VMEM] * n_feat,
        out_specs=(HBM, HBM, HBM, VMEM),
        scratch_shapes=[pltpu.VMEM((rows, width), BF16)] * n_feat
        + [
            pltpu.VMEM(back_shape, BF16),
            pltpu.VMEM(back_shape, F32),
            pltpu.VMEM((far_blocks + 1, tile, width), F32),
            pltpu.VMEM(shape, BF16),
            pltpu.VMEM(part_sums.shape, BF16),
            pltpu.SemaphoreType.DMA((rows // (4 * tile), n_feat)),
            pltpu.SemaphoreType.DMA((3,)),
            pltpu.SemaphoreType.DMA((1,)),
        ],
        compiler_params=params(),
        cost_estimate=cost(4 * rows * width * width * n_feat, 1 << 22),
        name="back_far",
    )(lists, tiles, part_sums, *grads, *[hbm(r) for r in w])


def back_own_kernel(lists, tiles, back_h, direct_h, out_h, back, acc, sems):
    own_blocks = back.shape[0]
    own = acc.at[pl.ds(0, own_blocks)]
    wait_copies(start_copies(sems, (back_h, back), (direct_h, own)))
    add_tiles_t(lists, 0, tiles, back, acc, own_blocks)
    wait_copies(start_copies(sems, (own, out_h)))


def back_own(lists, tiles, back, direct):
    return pl.pallas_call(
        back_own_kernel,
        out_shape=pltpu.HBM(direct.shape, F32),
        in_specs=[SMEM, VMEM, HBM, HBM],
        out_specs=HBM,
        scratch_shapes=[
            pltpu.VMEM(back.shape, BF16),
            pltpu.VMEM((direct.shape[0] + 1,) + direct.shape[1:], F32),
            pltpu.SemaphoreType.DMA((2,)),
        ],
        compiler_params=params(),
        cost_estimate=cost(2 * tiles.shape[0] * 128**3, 1 << 23),
        name="back_own",
    )(lists, tiles, hbm(back), hbm(direct))


def finish_kernel(me_s, rows_s, count_h, hub_h, incoming_h, base_h, out_h, self_out, neigh_out, count_s, hub_s, sent, hubs, sums, base, sems, out_sems):
    n_dom, capacity = rows_s.shape
    hub_dev = hub_s.shape[0]
    own_count, width = base.shape
    block, peers = 256, min(8, n_dom)
    copies = start_copies(
        sems,
        (count_h, count_s),
        (hub_h, hub_s),
        (incoming_h.at[:, pl.ds(0, capacity), :], sent),
        (incoming_h.at[:, pl.ds(capacity, hub_dev), :], hubs),
        (base_h, base),
        (incoming_h.at[:, pl.ds(capacity + hub_dev, sums.shape[1]), :], sums),
    )
    wait_copies(copies)
    hub = hubs[0].astype(F32)
    for q in range(1, n_dom):
        hub += hubs[q].astype(F32)
    for j in range(hub_dev):
        base[pl.ds(hub_s[j], 1), :] += hub[j : j + 1, :]
    lane = lax.broadcasted_iota(jnp.int32, (1, capacity), 1)
    leaving = []
    for start in range(0, own_count, block):
        vertex = lax.broadcasted_iota(jnp.int32, (block, capacity), 0) + start
        total = base[start : start + block, :]
        for first in range(0, n_dom, peers):
            hot, rows = [], []
            for q in range(first, first + peers):
                wanted = jnp.where(lane < count_s[0, q], rows_s[q : q + 1, :], -1)
                hot.append((vertex == wanted).astype(F32).astype(BF16))
                rows.append(sent[q])
            total += jnp.dot(
                jnp.concatenate(hot, axis=1),
                jnp.concatenate(rows, axis=0),
                preferred_element_type=F32,
            )
        base[start : start + block, :] = total
        at = pl.ds(start, block)
        leaving.append(start_copies(out_sems.at[pl.ds(start // block, 1)], (base.at[at], out_h.at[at])))
    chunk, n_feat = sums.shape[1], self_out.shape[0] // width
    n = min(chunk, width)
    for row in range(0, 2 * n_feat * width, n):
        q, first = divmod(row, chunk)
        which, k = divmod(row // width, n_feat)
        at = pl.multiple_of((me_s[0] ^ k) * width + row % width, n)
        (self_out, neigh_out)[which][pl.ds(at, n), :] = sums[q, first : first + n, :].astype(F32)
    for copies in leaving:
        wait_copies(copies)


def finish(me, send_rows, send_count, hub_ids, incoming, base, n_feat):
    n_dom, capacity = send_rows.shape
    hub_dev = hub_ids.shape[0]
    own_count, width = base.shape
    return pl.pallas_call(
        finish_kernel,
        out_shape=(pltpu.HBM(base.shape, F32),) + (pltpu.HBM((n_feat * width, width), F32),) * 2,
        in_specs=[SMEM, VMEM, HBM, HBM, ANY, HBM],
        out_specs=(HBM, VMEM, VMEM),
        scratch_shapes=[
            pltpu.SMEM(send_count.shape, jnp.int32),
            pltpu.SMEM(hub_ids.shape, jnp.int32),
            pltpu.VMEM((n_dom, capacity, width), BF16),
            pltpu.VMEM((n_dom, hub_dev, width), BF16),
            pltpu.VMEM((n_dom, 2 * n_feat * width // n_dom, width), BF16),
            pltpu.VMEM(base.shape, F32),
            pltpu.SemaphoreType.DMA((6,)),
            pltpu.SemaphoreType.DMA((own_count // 256,)),
        ],
        compiler_params=params(),
        cost_estimate=cost(2 * base.size * send_rows.size, 1 << 22),
        name="finish",
    )(me, hbm(send_rows), hbm(send_count), hbm(hub_ids), incoming, hbm(base))


def cut_kernel(me_s, w_self, w_neigh, *outs):
    width = w_self.shape[1]
    own, near, far = outs
    for k, out in enumerate((own, near, far.at[0], far.at[1])):
        at = pl.ds(pl.multiple_of((me_s[0] ^ k) * width, width), width)
        out[0] = w_self[at, :]
        out[1] = w_neigh[at, :]


def cut_weights(me, w_self, w_neigh):
    width = w_self.shape[1]
    one = (2, width, width)
    return pl.pallas_call(
        cut_kernel,
        out_shape=tuple(pltpu.HBM(shape, BF16) for shape in (one, one, (2,) + one)),
        in_specs=[SMEM, VMEM, VMEM],
        out_specs=(VMEM,) * 3,
        compiler_params=params(),
        cost_estimate=cost(0, 1 << 20),
        name="cut_weights",
    )(me, hbm(w_self), hbm(w_neigh))


def body(
    node_feats,
    edge_tiles,
    tile_dst,
    tile_src,
    hub_ids,
    send_rows,
    send_count,
    w_self,
    w_neigh,
    out_bias,
    grad_out,
    *,
    n_feat,
):
    own_count, width = node_feats.shape
    tile_size = edge_tiles.shape[1]
    listed = send_rows[0]
    n_dom, capacity = listed.shape
    hub_dev = hub_ids.shape[0]
    me = lax.axis_index("feat").astype(jnp.int32)
    me_s = me.reshape(1)
    far, near = 2, 1
    assert n_feat == 4
    far_blocks = n_dom * hub_dev // tile_size + n_dom

    def swap(x, k):
        return lax.ppermute(x, "feat", [(j, j ^ k) for j in range(n_feat)])

    feat_far = swap(node_feats, far)

    outgoing = pick(listed, send_count, hub_ids, node_feats)
    incoming = lax.all_to_all(outgoing, "dom", 0, 0, tiled=True)
    cut = cut_weights(me_s, w_self, w_neigh)
    own_feats, *cut = lax.optimization_barrier((node_feats.reshape(-1, tile_size, width), *cut))
    far_w = swap(cut[2], far)
    base, lists = own_tiles(tile_dst, tile_src, edge_tiles, own_feats, far_blocks)
    aggregated = far_tiles(lists, edge_tiles, incoming, base, far_blocks).reshape(own_count, width)

    aggregated, far_w = lax.optimization_barrier((aggregated, far_w))
    w_rows = [cut[0], swap(cut[1], near), far_w, swap(far_w, near)]
    agg_far = swap(aggregated, far)
    feat_far, aggregated = lax.optimization_barrier((feat_far, aggregated))
    feats = [hbm(node_feats), swap(node_feats, near), feat_far, swap(feat_far, near)]
    flops = 2 * own_count * n_feat * width * width
    rows_out = ((own_count, width), BF16)
    (own_part,) = stream_call(
        self_step,
        me_s,
        feats,
        [w_self, out_bias[None, :]],
        [((own_count, width), F32)],
        flops,
        "self_dense",
    )
    agg_far, own_part = lax.optimization_barrier((agg_far, own_part))
    aggs = [hbm(aggregated), swap(aggregated, near), agg_far, swap(agg_far, near)]
    output, grad_pre = stream_call(
        forward_step,
        me_s,
        [*aggs, hbm(own_part), hbm(grad_out)],
        [w_neigh],
        [rows_out, rows_out],
        flops,
        "forward_dense",
    )

    grad_far = swap(grad_pre, far)
    parts = weight_parts(feats + aggs, hbm(grad_pre), n_dom)
    part_sums = lax.all_to_all(parts, "dom", 0, 0, tiled=True)
    grad_far, part_sums = lax.optimization_barrier((grad_far, part_sums))
    grads = [hbm(grad_pre), swap(grad_pre, near), grad_far, swap(grad_far, near)]

    back_out, back_agg, direct, grad_bias = back_far(
        lists, edge_tiles, part_sums, grads, w_rows, hub_dev, tile_size
    )
    back_in = lax.all_to_all(back_out, "dom", 0, 0, tiled=True)
    own = back_own(lists, edge_tiles, back_agg, direct).reshape(own_count, width)
    grad_feats, grad_self, grad_neigh = finish(
        me_s, listed, send_count, hub_ids, back_in, own, n_feat
    )
    return (output, grad_feats, grad_self, grad_neigh, grad_bias[0])


def solution(mesh):
    in_specs = (
        P("dom", "feat"),
        P("dom", None, None),
        P("dom"),
        P("dom"),
        P("dom"),
        P("dom", None, None),
        P("dom", None),
        P(None, "feat"),
        P(None, "feat"),
        P("feat"),
        P("dom", "feat"),
    )
    out_specs = (P("dom", "feat"), P("dom", "feat"), P(None, "feat"), P(None, "feat"), P("feat"))
    n_feat = mesh.shape["feat"]

    def run(*args):
        return body(*args, n_feat=n_feat)

    return jax.shard_map(run, mesh=mesh, in_specs=in_specs, out_specs=out_specs, check_vma=False)
```

```python
import functools

import jax
import jax.numpy as jnp
from jax import lax
from jax.experimental import pallas as pl
from jax.experimental.pallas import tpu as pltpu
from jax.sharding import PartitionSpec as P

F32 = jnp.float32
BF16 = jnp.bfloat16
VMEM = pl.BlockSpec(memory_space=pltpu.VMEM)
SMEM = pl.BlockSpec(memory_space=pltpu.SMEM)
HBM = pl.BlockSpec(memory_space=pltpu.HBM)
ANY = pl.BlockSpec(memory_space=pl.ANY)
UNROLL = 8
T_BITS, S_BITS = 10, 10


def params(mib=24):
    return pltpu.CompilerParams(vmem_limit_bytes=mib << 20)


def hbm(x):
    return pltpu.with_memory_space_constraint(x, pltpu.HBM)


def cost(flops, nbytes):
    return pl.CostEstimate(flops=flops, bytes_accessed=nbytes, transcendentals=0)


def start_copies(sems, *pairs):
    copies = [pltpu.make_async_copy(a, b, sems.at[i]) for i, (a, b) in enumerate(pairs)]
    for copy in copies:
        copy.start()
    return copies


def wait_copies(copies):
    for copy in copies:
        copy.wait()


def pick_kernel(rows_h, count_h, hub_h, x_h, out_h, rows_s, count_s, hub_s, x, x32, stage, out, sems, out_sems):
    copies = start_copies(sems, (x_h, x), (rows_h, rows_s), (count_h, count_s), (hub_h, hub_s))
    n_dom, capacity = rows_s.shape
    hub_dev = hub_s.shape[0]
    step = 16
    wait_copies(copies)
    x32[...] = x[...].astype(F32)
    for j in range(hub_dev):
        stage[capacity + j : capacity + j + 1, :] = x32[pl.ds(hub_s[j], 1), :]
    hub = stage[capacity:, :].astype(BF16)
    slot = lax.broadcasted_iota(jnp.int32, (capacity, x.shape[1]), 0)

    def peer(q, carry):
        def some(g, carry):
            for u in range(step):
                c = g * step + u
                stage[pl.ds(c, 1), :] = x32[pl.ds(rows_s[q, c], 1), :]
            return carry

        lax.fori_loop(0, capacity // step, some, 0)
        kept = jnp.where(slot < count_s[0, q], stage[:capacity, :], 0.0)
        out[q, :capacity, :] = kept.astype(BF16)
        out[q, capacity:, :] = hub
        pltpu.make_async_copy(out.at[q], out_h.at[q], out_sems.at[q]).start()
        return carry

    lax.fori_loop(0, n_dom, peer, 0)
    for q in range(n_dom):
        pltpu.make_async_copy(out.at[q], out_h.at[q], out_sems.at[q]).wait()


def pick(send_rows, send_count, hub_ids, x):
    n_dom, capacity = send_rows.shape
    rows = capacity + hub_ids.shape[0]
    shape = (n_dom, rows, x.shape[1])
    return pl.pallas_call(
        pick_kernel,
        out_shape=pltpu.HBM(shape, BF16),
        in_specs=[HBM] * 4,
        out_specs=HBM,
        scratch_shapes=[
            pltpu.SMEM(send_rows.shape, jnp.int32),
            pltpu.SMEM(send_count.shape, jnp.int32),
            pltpu.SMEM(hub_ids.shape, jnp.int32),
            pltpu.VMEM(x.shape, BF16),
            pltpu.VMEM(x.shape, F32),
            pltpu.VMEM((rows, x.shape[1]), F32),
            pltpu.VMEM(shape, BF16),
            pltpu.SemaphoreType.DMA((4,)),
            pltpu.SemaphoreType.DMA((n_dom,)),
        ],
        compiler_params=params(),
        cost_estimate=cost(0, 1 << 21),
        name="pick_rows",
    )(hbm(send_rows), hbm(send_count), hbm(hub_ids), hbm(x))


def unpack(entry):
    t = entry & ((1 << T_BITS) - 1)
    s = (entry >> T_BITS) & ((1 << S_BITS) - 1)
    return t, s, entry >> (T_BITS + S_BITS)


def make_lists(dst_s, src_s, lists, own_blocks, far_blocks):
    length = lists.shape[1] - 1

    def step(t, n):
        s = src_s[t]
        d = dst_s[t]
        far = (s >= own_blocks).astype(jnp.int32)
        lists[0, n[0]] = t + (s << T_BITS) + (d << (T_BITS + S_BITS))
        lists[1, n[1]] = t + ((s - own_blocks) << T_BITS) + (d << (T_BITS + S_BITS))
        return n[0] + 1 - far, n[1] + far

    n = lax.fori_loop(0, dst_s.shape[0], step, (jnp.int32(0), jnp.int32(0)))
    for which, blocks in ((0, own_blocks), (1, far_blocks)):
        spare = (blocks << T_BITS) + (own_blocks << (T_BITS + S_BITS))
        for u in range(UNROLL - 1):
            lists[which, n[which] + u] = jnp.int32(spare)
        lists[which, length] = n[which]


def add_tiles(lists, which, tiles, source, acc, spare):
    n = lists[which, lists.shape[1] - 1]

    def group(g, carry):
        done = []
        for u in range(UNROLL):
            t, s, d = unpack(lists[which, g * UNROLL + u])
            s = jnp.where(d == spare, 0, s)
            done.append((d, jnp.dot(tiles[t], source[s], preferred_element_type=F32)))
        for d, product in done:
            acc[d] += product
        return carry

    lax.fori_loop(0, (n + UNROLL - 1) // UNROLL, group, 0)


def add_tiles_t(lists, which, tiles, source, acc, spare):
    n = lists[which, lists.shape[1] - 1]

    def group(g, carry):
        done = []
        for u in range(UNROLL):
            t, s, d = unpack(lists[which, g * UNROLL + u])
            d = jnp.where(d == spare, 0, d)
            product = lax.dot_general(
                tiles[t], source[d], (((0,), (0,)), ((), ())), preferred_element_type=F32
            )
            done.append((s, product))
        for s, product in done:
            acc[s] += product
        return carry

    lax.fori_loop(0, (n + UNROLL - 1) // UNROLL, group, 0)


def own_kernel(
    dst_h, src_h, tiles_h, x_h, out_h, lists, dst_s, src_s, x, tiles, acc, sems, *, far_blocks
):
    own_blocks = x.shape[0]
    copies = start_copies(sems, (dst_h, dst_s), (src_h, src_s), (x_h, x), (tiles_h, tiles))
    acc[...] = jnp.zeros_like(acc)
    wait_copies(copies[:2])
    make_lists(dst_s, src_s, lists, own_blocks, far_blocks)
    wait_copies(copies[2:])
    add_tiles(lists, 0, tiles, x, acc, own_blocks)
    wait_copies(start_copies(sems, (acc.at[pl.ds(0, own_blocks)], out_h)))


def own_tiles(tile_dst, tile_src, tiles, x, far_blocks):
    n = tiles.shape[0]
    return pl.pallas_call(
        functools.partial(own_kernel, far_blocks=far_blocks),
        out_shape=(
            pltpu.HBM(x.shape, F32),
            jax.ShapeDtypeStruct((2, n + UNROLL), jnp.int32),
        ),
        in_specs=[HBM, HBM, HBM, HBM],
        out_specs=(HBM, SMEM),
        scratch_shapes=[
            pltpu.SMEM((n,), jnp.int32),
            pltpu.SMEM((n,), jnp.int32),
            pltpu.VMEM(x.shape, BF16),
            pltpu.VMEM(tiles.shape, BF16),
            pltpu.VMEM((x.shape[0] + 1,) + x.shape[1:], F32),
            pltpu.SemaphoreType.DMA((4,)),
        ],
        compiler_params=params(),
        cost_estimate=cost(2 * n * 128**3, 1 << 23),
        name="own_tiles",
    )(hbm(tile_dst), hbm(tile_src), hbm(tiles), hbm(x))


def far_kernel(lists, tiles, incoming_h, base_h, out_h, source, acc, out, sems):
    n_dom, rows, _ = incoming_h.shape
    own_blocks, tile, _ = base_h.shape
    hub_dev = rows - tile
    hub_blocks = n_dom * hub_dev // tile
    pairs = [(incoming_h.at[:, pl.ds(0, tile), :], source.at[pl.ds(hub_blocks, n_dom)])]
    pairs.append((base_h, acc.at[pl.ds(0, own_blocks)]))
    for q in range(n_dom):
        block, row = divmod(q * hub_dev, tile)
        pairs.append(
            (incoming_h.at[q, pl.ds(tile, hub_dev), :], source.at[block, pl.ds(row, hub_dev), :])
        )
    wait_copies(start_copies(sems, *pairs))
    add_tiles(lists, 1, tiles, source, acc, own_blocks)
    out[...] = acc[:own_blocks].astype(BF16)
    wait_copies(start_copies(sems, (out, out_h)))


def far_tiles(lists, tiles, incoming, base, far_blocks):
    own_blocks, tile, width = base.shape
    return pl.pallas_call(
        far_kernel,
        out_shape=pltpu.HBM(base.shape, BF16),
        in_specs=[SMEM, VMEM, HBM, HBM],
        out_specs=HBM,
        scratch_shapes=[
            pltpu.VMEM((far_blocks, tile, width), BF16),
            pltpu.VMEM((own_blocks + 1, tile, width), F32),
            pltpu.VMEM(base.shape, BF16),
            pltpu.SemaphoreType.DMA((incoming.shape[0] + 2,)),
        ],
        compiler_params=params(),
        cost_estimate=cost(tiles.shape[0] * 128**3, 1 << 22),
        name="far_tiles",
    )(lists, tiles, hbm(incoming), hbm(base))


def by_shards(me, shards, w):
    width = shards[0].shape[1]
    rows = [
        w[pl.ds(pl.multiple_of((me ^ k) * width, width), width), :] for k in range(len(shards))
    ]
    return jnp.dot(
        jnp.concatenate([s[...] for s in shards], axis=1),
        jnp.concatenate(rows, axis=0),
        preferred_element_type=F32,
    )


def stream(step, ins_h, ins, outs_h, outs, sems, block):
    rows = ins[0].shape[0]
    n_in = len(ins)
    pending = []
    for i in range(rows // block):
        at = pl.ds(i * block, block)
        pairs = [(a.at[at], b.at[at]) for a, b in zip(ins_h, ins)]
        pending.append(start_copies(sems.at[i], *pairs))
    leaving = []
    for i in range(rows // block):
        at = pl.ds(i * block, block)
        wait_copies(pending[i])
        step(at, [r.at[at] for r in ins], [r.at[at] for r in outs])
        pairs = [(a.at[at], b.at[at]) for a, b in zip(outs, outs_h)]
        leaving.append(start_copies(sems.at[i, pl.ds(n_in, len(outs))], *pairs))
    for copies in leaving:
        wait_copies(copies)


def stream_call(kernel, me, streamed, whole, outs, flops, name, block=256):
    rows = streamed[0].shape[0]
    n_in, n_whole, n_out = len(streamed), len(whole), len(outs)

    def run(me_s, *refs):
        ins_h, refs = refs[:n_in], refs[n_in:]
        held, refs = refs[:n_whole], refs[n_whole:]
        outs_h, refs = refs[:n_out], refs[n_out:]
        ins, refs = refs[:n_in], refs[n_in:]
        out, sems = refs[:n_out], refs[n_out]
        stream(
            lambda at, i, o: kernel(me_s[0], i, held, o), ins_h, ins, outs_h, out, sems, block
        )

    return pl.pallas_call(
        run,
        out_shape=tuple(pltpu.HBM(shape, t) for shape, t in outs),
        in_specs=[SMEM] + [ANY] * n_in + [VMEM] * n_whole,
        out_specs=(HBM,) * n_out,
        scratch_shapes=[pltpu.VMEM(x.shape, x.dtype) for x in streamed]
        + [pltpu.VMEM(shape, t) for shape, t in outs]
        + [pltpu.SemaphoreType.DMA((rows // block, n_in + n_out))],
        compiler_params=params(),
        cost_estimate=cost(flops, 1 << 22),
        name=name,
    )(me, *streamed, *[hbm(x) for x in whole])


def self_step(me, ins, held, outs):
    w, bias = held
    outs[0][...] = by_shards(me, ins, w) + bias[...]


def forward_step(me, ins, held, outs):
    *shards, own_part, grad_out = ins
    output, grad_pre = outs
    pre_act = own_part[...] + by_shards(me, shards, held[0])
    gate = jax.nn.sigmoid(pre_act)
    output[...] = (pre_act * gate).astype(BF16)
    grad = grad_out[...].astype(F32) * gate * (1.0 + pre_act * (1.0 - gate))
    grad_pre[...] = grad.astype(BF16)


def weights_kernel(*refs, n_feat):
    shards, grad, out_h, out, sems = refs[: 2 * n_feat], *refs[2 * n_feat :]
    n_dom, chunk = out.shape[0], out.shape[1] - 8
    width = grad.shape[1]
    flipped = grad[...].T
    bias = jnp.sum(grad[...].astype(F32), axis=0, keepdims=True)
    for i, shard in enumerate(shards):
        block = jnp.dot(flipped, shard[...], preferred_element_type=F32).T
        for row in range(0, width, min(chunk, width)):
            q, start = divmod(i * width + row, chunk)
            n = min(chunk, width)
            out[q, start : start + n, :] = block[row : row + n, :]
    for q in range(n_dom):
        out[q, chunk:, :] = jnp.broadcast_to(bias, (8, width))
    wait_copies(start_copies(sems, (out, out_h)))


def weight_parts(shards, grad, n_dom):
    n_feat = len(shards) // 2
    width = grad.shape[1]
    chunk = 2 * n_feat * width // n_dom
    return pl.pallas_call(
        functools.partial(weights_kernel, n_feat=n_feat),
        out_shape=pltpu.HBM((n_dom, chunk + 8, width), F32),
        in_specs=[VMEM] * (2 * n_feat + 1),
        out_specs=HBM,
        scratch_shapes=[
            pltpu.VMEM((n_dom, chunk + 8, width), F32),
            pltpu.SemaphoreType.DMA((1,)),
        ],
        compiler_params=params(),
        cost_estimate=cost(4 * n_feat * width * width * grad.shape[0], 1 << 22),
        name="weight_parts",
    )(*shards, grad)


def split_copies(sems, pairs, block):
    rows = pairs[0][0].shape[0]
    return [
        start_copies(
            sems.at[i], *[(a.at[pl.ds(i * block, block)], b.at[pl.ds(i * block, block)]) for a, b in pairs]
        )
        for i in range(rows // block)
    ]


def back_far_kernel(*refs, n_feat):
    lists, tiles = refs[:2]
    grads_h, w = refs[2 : 2 + n_feat], refs[2 + n_feat : 2 + 2 * n_feat]
    out_h, back_h, direct_h = refs[2 + 2 * n_feat : 5 + 2 * n_feat]
    grads = refs[5 + 2 * n_feat : 5 + 3 * n_feat]
    back, direct, acc, out, sems, out_sems = refs[5 + 3 * n_feat :]
    n_dom = out.shape[0]
    own_blocks, tile, width = back.shape
    hub_dev = out.shape[1] - tile
    hub_blocks = n_dom * hub_dev // tile
    block = 4 * tile
    pending = split_copies(sems, list(zip(grads_h, grads)), block)
    acc[...] = jnp.zeros_like(acc)
    own_w, near_w, far_w, both_w = w
    rows = [r.reshape(2 * width, -1) for r in (own_w[...], near_w[...], far_w[0], both_w[1])]
    rows = jnp.concatenate(rows, axis=1)
    for i, copies in enumerate(pending):
        wait_copies(copies)
        whole = jnp.concatenate([g[i * block : (i + 1) * block, :] for g in grads], axis=1)
        both = lax.dot_general(whole, rows, (((1,), (1,)), ((), ())), preferred_element_type=F32)
        direct[4 * i : 4 * (i + 1)] = both[:, :width].reshape(4, tile, width)
        back[4 * i : 4 * (i + 1)] = both[:, width:].astype(BF16).reshape(4, tile, width)
    leaving = start_copies(out_sems, (direct, direct_h), (back, back_h))
    add_tiles_t(lists, 1, tiles, back, acc, own_blocks)
    for q in range(n_dom):
        out[q, :tile, :] = acc[hub_blocks + q].astype(BF16)
        at, row = divmod(q * hub_dev, tile)
        out[q, tile:, :] = acc[at, row : row + hub_dev, :].astype(BF16)
    leaving += start_copies(out_sems.at[pl.ds(2, 1)], (out, out_h))
    wait_copies(leaving)


def back_far(lists, tiles, grads, w, n_dom, hub_dev, tile):
    n_feat = len(grads)
    rows, width = grads[0].shape
    far_blocks = n_dom * hub_dev // tile + n_dom
    shape = (n_dom, tile + hub_dev, width)
    back_shape = (rows // tile, tile, width)
    return pl.pallas_call(
        functools.partial(back_far_kernel, n_feat=n_feat),
        out_shape=(pltpu.HBM(shape, BF16), pltpu.HBM(back_shape, BF16), pltpu.HBM(back_shape, F32)),
        in_specs=[SMEM, VMEM] + [ANY] * n_feat + [VMEM] * n_feat,
        out_specs=(HBM, HBM, HBM),
        scratch_shapes=[pltpu.VMEM((rows, width), BF16)] * n_feat
        + [
            pltpu.VMEM(back_shape, BF16),
            pltpu.VMEM(back_shape, F32),
            pltpu.VMEM((far_blocks + 1, tile, width), F32),
            pltpu.VMEM(shape, BF16),
            pltpu.SemaphoreType.DMA((rows // (4 * tile), n_feat)),
            pltpu.SemaphoreType.DMA((3,)),
        ],
        compiler_params=params(),
        cost_estimate=cost(4 * rows * width * width * n_feat, 1 << 22),
        name="back_far",
    )(lists, tiles, *grads, *[hbm(r) for r in w])


def back_own_kernel(lists, tiles, back_h, direct_h, out_h, back, acc, sems):
    own_blocks = back.shape[0]
    own = acc.at[pl.ds(0, own_blocks)]
    wait_copies(start_copies(sems, (back_h, back), (direct_h, own)))
    add_tiles_t(lists, 0, tiles, back, acc, own_blocks)
    wait_copies(start_copies(sems, (own, out_h)))


def back_own(lists, tiles, back, direct):
    return pl.pallas_call(
        back_own_kernel,
        out_shape=pltpu.HBM(direct.shape, F32),
        in_specs=[SMEM, VMEM, HBM, HBM],
        out_specs=HBM,
        scratch_shapes=[
            pltpu.VMEM(back.shape, BF16),
            pltpu.VMEM((direct.shape[0] + 1,) + direct.shape[1:], F32),
            pltpu.SemaphoreType.DMA((2,)),
        ],
        compiler_params=params(),
        cost_estimate=cost(2 * tiles.shape[0] * 128**3, 1 << 23),
        name="back_own",
    )(lists, tiles, hbm(back), hbm(direct))


def finish_kernel(rows_s, count_h, hub_h, incoming_h, base_h, out_h, count_s, hub_s, sent, hubs, base, sems, out_sems):
    n_dom, capacity = rows_s.shape
    hub_dev = hub_s.shape[0]
    own_count, width = base.shape
    block, peers = 256, min(8, n_dom)
    copies = start_copies(
        sems,
        (count_h, count_s),
        (hub_h, hub_s),
        (incoming_h.at[:, pl.ds(0, capacity), :], sent),
        (incoming_h.at[:, pl.ds(capacity, hub_dev), :], hubs),
        (base_h, base),
    )
    wait_copies(copies)
    hub = hubs[0].astype(F32)
    for q in range(1, n_dom):
        hub += hubs[q].astype(F32)
    for j in range(hub_dev):
        base[pl.ds(hub_s[j], 1), :] += hub[j : j + 1, :]
    lane = lax.broadcasted_iota(jnp.int32, (1, capacity), 1)
    leaving = []
    for start in range(0, own_count, block):
        vertex = lax.broadcasted_iota(jnp.int32, (block, capacity), 0) + start
        total = base[start : start + block, :]
        for first in range(0, n_dom, peers):
            hot, rows = [], []
            for q in range(first, first + peers):
                wanted = jnp.where(lane < count_s[0, q], rows_s[q : q + 1, :], -1)
                hot.append((vertex == wanted).astype(F32).astype(BF16))
                rows.append(sent[q])
            total += jnp.dot(
                jnp.concatenate(hot, axis=1),
                jnp.concatenate(rows, axis=0),
                preferred_element_type=F32,
            )
        base[start : start + block, :] = total
        at = pl.ds(start, block)
        leaving.append(start_copies(out_sems.at[pl.ds(start // block, 1)], (base.at[at], out_h.at[at])))
    for copies in leaving:
        wait_copies(copies)


def finish(send_rows, send_count, hub_ids, incoming, base):
    n_dom, capacity = send_rows.shape
    hub_dev = hub_ids.shape[0]
    own_count, width = base.shape
    return pl.pallas_call(
        finish_kernel,
        out_shape=pltpu.HBM(base.shape, F32),
        in_specs=[VMEM, HBM, HBM, ANY, HBM],
        out_specs=HBM,
        scratch_shapes=[
            pltpu.SMEM(send_count.shape, jnp.int32),
            pltpu.SMEM(hub_ids.shape, jnp.int32),
            pltpu.VMEM((n_dom, capacity, width), BF16),
            pltpu.VMEM((n_dom, hub_dev, width), BF16),
            pltpu.VMEM(base.shape, F32),
            pltpu.SemaphoreType.DMA((5,)),
            pltpu.SemaphoreType.DMA((own_count // 256,)),
        ],
        compiler_params=params(),
        cost_estimate=cost(2 * base.size * send_rows.size, 1 << 22),
        name="finish",
    )(hbm(send_rows), hbm(send_count), hbm(hub_ids), incoming, hbm(base))


def cut_kernel(me_s, w_self, w_neigh, *outs):
    width = w_self.shape[1]
    own, near, far = outs
    for k, out in enumerate((own, near, far.at[0], far.at[1])):
        at = pl.ds(pl.multiple_of((me_s[0] ^ k) * width, width), width)
        out[0] = w_self[at, :]
        out[1] = w_neigh[at, :]


def cut_weights(me, w_self, w_neigh):
    width = w_self.shape[1]
    one = (2, width, width)
    return pl.pallas_call(
        cut_kernel,
        out_shape=tuple(pltpu.HBM(shape, BF16) for shape in (one, one, (2,) + one)),
        in_specs=[SMEM, VMEM, VMEM],
        out_specs=(VMEM,) * 3,
        compiler_params=params(),
        cost_estimate=cost(0, 1 << 20),
        name="cut_weights",
    )(me, hbm(w_self), hbm(w_neigh))


def sum_kernel(parts, out, bias):
    n_dom, chunk, _ = out.shape
    total = parts[0]
    for q in range(1, n_dom):
        total += parts[q]
    bias[...] = total[chunk : chunk + 1, :]
    rows = total[:chunk, :].astype(BF16)
    for q in range(n_dom):
        out[q] = rows


def sum_parts(parts):
    n_dom, rows, width = parts.shape
    return pl.pallas_call(
        sum_kernel,
        out_shape=(pltpu.HBM((n_dom, rows - 8, width), BF16), pltpu.HBM((1, width), F32)),
        in_specs=[VMEM],
        out_specs=(VMEM, VMEM),
        compiler_params=params(),
        cost_estimate=cost(0, 1 << 20),
        name="sum_parts",
    )(hbm(parts))


def place_kernel(me_s, sums, self_out, neigh_out):
    rows, width = self_out.shape
    for i in range(2 * rows // width):
        which, k = divmod(i, rows // width)
        target = (self_out, neigh_out)[which]
        at = pl.ds(pl.multiple_of((me_s[0] ^ k) * width, width), width)
        target[at, :] = sums[i * width : (i + 1) * width, :].astype(F32)


def place_weights(me, sums):
    rows, width = sums.shape[0] // 2, sums.shape[1]
    return pl.pallas_call(
        place_kernel,
        out_shape=(pltpu.HBM((rows, width), F32),) * 2,
        in_specs=[SMEM, VMEM],
        out_specs=(VMEM, VMEM),
        compiler_params=params(),
        cost_estimate=cost(0, 1 << 20),
        name="place_weights",
    )(me, sums)


def body(
    node_feats,
    edge_tiles,
    tile_dst,
    tile_src,
    hub_ids,
    send_rows,
    send_count,
    w_self,
    w_neigh,
    out_bias,
    grad_out,
    *,
    n_feat,
):
    own_count, width = node_feats.shape
    tile_size = edge_tiles.shape[1]
    listed = send_rows[0]
    n_dom, capacity = listed.shape
    hub_dev = hub_ids.shape[0]
    me = lax.axis_index("feat").astype(jnp.int32)
    me_s = me.reshape(1)
    far, near = 2, 1
    assert n_feat == 4
    far_blocks = n_dom * hub_dev // tile_size + n_dom

    def swap(x, k):
        return lax.ppermute(x, "feat", [(j, j ^ k) for j in range(n_feat)])

    feat_far = swap(node_feats, far)

    outgoing = pick(listed, send_count, hub_ids, node_feats)
    incoming = lax.all_to_all(outgoing, "dom", 0, 0, tiled=True)
    cut = cut_weights(me_s, w_self, w_neigh)
    own_feats, *cut = lax.optimization_barrier((node_feats.reshape(-1, tile_size, width), *cut))
    far_w = swap(cut[2], far)
    base, lists = own_tiles(tile_dst, tile_src, edge_tiles, own_feats, far_blocks)
    aggregated = far_tiles(lists, edge_tiles, incoming, base, far_blocks).reshape(own_count, width)

    aggregated, far_w = lax.optimization_barrier((aggregated, far_w))
    w_rows = [cut[0], swap(cut[1], near), far_w, swap(far_w, near)]
    agg_far = swap(aggregated, far)
    feat_far, aggregated = lax.optimization_barrier((feat_far, aggregated))
    feats = [hbm(node_feats), swap(node_feats, near), feat_far, swap(feat_far, near)]
    flops = 2 * own_count * n_feat * width * width
    rows_out = ((own_count, width), BF16)
    (own_part,) = stream_call(
        self_step,
        me_s,
        feats,
        [w_self, out_bias[None, :]],
        [((own_count, width), F32)],
        flops,
        "self_dense",
    )
    agg_far, own_part, *w_rows = lax.optimization_barrier((agg_far, own_part, *w_rows))
    aggs = [hbm(aggregated), swap(aggregated, near), agg_far, swap(agg_far, near)]
    output, grad_pre = stream_call(
        forward_step,
        me_s,
        [*aggs, hbm(own_part), hbm(grad_out)],
        [w_neigh],
        [rows_out, rows_out],
        flops,
        "forward_dense",
    )

    grad_far = swap(grad_pre, far)
    parts = weight_parts(feats + aggs, hbm(grad_pre), n_dom)
    part_sums = lax.all_to_all(parts, "dom", 0, 0, tiled=True)
    grads = [hbm(grad_pre), swap(grad_pre, near), grad_far, swap(grad_far, near)]

    back_out, back_agg, direct = back_far(
        lists, edge_tiles, grads, w_rows, n_dom, hub_dev, tile_size
    )
    back_in = lax.all_to_all(back_out, "dom", 0, 0, tiled=True)
    own = back_own(lists, edge_tiles, back_agg, direct).reshape(own_count, width)
    weights_out, grad_bias = sum_parts(part_sums)
    weights_out, back_in, own = lax.optimization_barrier((weights_out, back_in, own))
    weights_in = lax.all_to_all(weights_out, "dom", 0, 0, tiled=True)
    grad_feats = finish(listed, send_count, hub_ids, back_in, own)
    grad_self, grad_neigh = place_weights(me_s, weights_in.reshape(-1, width))
    return (output, grad_feats, grad_self, grad_neigh, grad_bias[0])


def solution(mesh):
    in_specs = (
        P("dom", "feat"),
        P("dom", None, None),
        P("dom"),
        P("dom"),
        P("dom"),
        P("dom", None, None),
        P("dom", None),
        P(None, "feat"),
        P(None, "feat"),
        P("feat"),
        P("dom", "feat"),
    )
    out_specs = (P("dom", "feat"), P("dom", "feat"), P(None, "feat"), P(None, "feat"), P("feat"))
    n_feat = mesh.shape["feat"]

    def run(*args):
        return body(*args, n_feat=n_feat)

    return jax.shard_map(run, mesh=mesh, in_specs=in_specs, out_specs=out_specs, check_vma=False)
```

```python
import functools

import jax
import jax.numpy as jnp
from jax import lax
from jax.experimental import pallas as pl
from jax.experimental.pallas import tpu as pltpu
from jax.sharding import PartitionSpec as P

F32 = jnp.float32
BF16 = jnp.bfloat16
VMEM = pl.BlockSpec(memory_space=pltpu.VMEM)
SMEM = pl.BlockSpec(memory_space=pltpu.SMEM)
HBM = pl.BlockSpec(memory_space=pltpu.HBM)
ANY = pl.BlockSpec(memory_space=pl.ANY)
UNROLL = 8
T_BITS, S_BITS = 10, 10


def params(mib=24):
    return pltpu.CompilerParams(vmem_limit_bytes=mib << 20)


def hbm(x):
    return pltpu.with_memory_space_constraint(x, pltpu.HBM)


def cost(flops, nbytes):
    return pl.CostEstimate(flops=flops, bytes_accessed=nbytes, transcendentals=0)


def start_copies(sems, *pairs):
    copies = [pltpu.make_async_copy(a, b, sems.at[i]) for i, (a, b) in enumerate(pairs)]
    for copy in copies:
        copy.start()
    return copies


def wait_copies(copies):
    for copy in copies:
        copy.wait()


def pick_kernel(rows_h, count_h, hub_h, x_h, out_h, rows_s, count_s, hub_s, x, x32, stage, out, sems, out_sems):
    copies = start_copies(sems, (x_h, x), (rows_h, rows_s), (count_h, count_s), (hub_h, hub_s))
    n_dom, capacity = rows_s.shape
    hub_dev = hub_s.shape[0]
    step = 16
    wait_copies(copies)
    x32[...] = x[...].astype(F32)
    for j in range(hub_dev):
        stage[capacity + j : capacity + j + 1, :] = x32[pl.ds(hub_s[j], 1), :]
    hub = stage[capacity:, :].astype(BF16)
    slot = lax.broadcasted_iota(jnp.int32, (capacity, x.shape[1]), 0)

    def peer(q, carry):
        def some(g, carry):
            for u in range(step):
                c = g * step + u
                stage[pl.ds(c, 1), :] = x32[pl.ds(rows_s[q, c], 1), :]
            return carry

        lax.fori_loop(0, capacity // step, some, 0)
        kept = jnp.where(slot < count_s[0, q], stage[:capacity, :], 0.0)
        out[q, :capacity, :] = kept.astype(BF16)
        out[q, capacity:, :] = hub
        pltpu.make_async_copy(out.at[q], out_h.at[q], out_sems.at[q]).start()
        return carry

    lax.fori_loop(0, n_dom, peer, 0)
    for q in range(n_dom):
        pltpu.make_async_copy(out.at[q], out_h.at[q], out_sems.at[q]).wait()


def pick(send_rows, send_count, hub_ids, x):
    n_dom, capacity = send_rows.shape
    rows = capacity + hub_ids.shape[0]
    shape = (n_dom, rows, x.shape[1])
    return pl.pallas_call(
        pick_kernel,
        out_shape=pltpu.HBM(shape, BF16),
        in_specs=[HBM] * 4,
        out_specs=HBM,
        scratch_shapes=[
            pltpu.SMEM(send_rows.shape, jnp.int32),
            pltpu.SMEM(send_count.shape, jnp.int32),
            pltpu.SMEM(hub_ids.shape, jnp.int32),
            pltpu.VMEM(x.shape, BF16),
            pltpu.VMEM(x.shape, F32),
            pltpu.VMEM((rows, x.shape[1]), F32),
            pltpu.VMEM(shape, BF16),
            pltpu.SemaphoreType.DMA((4,)),
            pltpu.SemaphoreType.DMA((n_dom,)),
        ],
        compiler_params=params(),
        cost_estimate=cost(0, 1 << 21),
        name="pick_rows",
    )(hbm(send_rows), hbm(send_count), hbm(hub_ids), hbm(x))


def unpack(entry):
    t = entry & ((1 << T_BITS) - 1)
    s = (entry >> T_BITS) & ((1 << S_BITS) - 1)
    return t, s, entry >> (T_BITS + S_BITS)


def make_lists(dst_s, src_s, lists, own_blocks, far_blocks):
    length = lists.shape[1] - 1

    def step(t, n):
        s = src_s[t]
        d = dst_s[t]
        far = (s >= own_blocks).astype(jnp.int32)
        lists[0, n[0]] = t + (s << T_BITS) + (d << (T_BITS + S_BITS))
        lists[1, n[1]] = t + ((s - own_blocks) << T_BITS) + (d << (T_BITS + S_BITS))
        return n[0] + 1 - far, n[1] + far

    n = lax.fori_loop(0, dst_s.shape[0], step, (jnp.int32(0), jnp.int32(0)))
    for which, blocks in ((0, own_blocks), (1, far_blocks)):
        spare = (blocks << T_BITS) + (own_blocks << (T_BITS + S_BITS))
        for u in range(UNROLL - 1):
            lists[which, n[which] + u] = jnp.int32(spare)
        lists[which, length] = n[which]


def add_tiles(lists, which, tiles, source, acc, spare):
    n = lists[which, lists.shape[1] - 1]

    def group(g, carry):
        done = []
        for u in range(UNROLL):
            t, s, d = unpack(lists[which, g * UNROLL + u])
            s = jnp.where(d == spare, 0, s)
            done.append((d, jnp.dot(tiles[t], source[s], preferred_element_type=F32)))
        for d, product in done:
            acc[d] += product
        return carry

    lax.fori_loop(0, (n + UNROLL - 1) // UNROLL, group, 0)


def add_tiles_t(lists, which, tiles, source, acc, spare):
    n = lists[which, lists.shape[1] - 1]

    def group(g, carry):
        done = []
        for u in range(UNROLL):
            t, s, d = unpack(lists[which, g * UNROLL + u])
            d = jnp.where(d == spare, 0, d)
            product = lax.dot_general(
                tiles[t], source[d], (((0,), (0,)), ((), ())), preferred_element_type=F32
            )
            done.append((s, product))
        for s, product in done:
            acc[s] += product
        return carry

    lax.fori_loop(0, (n + UNROLL - 1) // UNROLL, group, 0)


def own_kernel(
    dst_h, src_h, tiles_h, x_h, out_h, lists, dst_s, src_s, x, tiles, acc, sems, *, far_blocks
):
    own_blocks = x.shape[0]
    copies = start_copies(sems, (dst_h, dst_s), (src_h, src_s), (x_h, x), (tiles_h, tiles))
    acc[...] = jnp.zeros_like(acc)
    wait_copies(copies[:2])
    make_lists(dst_s, src_s, lists, own_blocks, far_blocks)
    wait_copies(copies[2:])
    add_tiles(lists, 0, tiles, x, acc, own_blocks)
    wait_copies(start_copies(sems, (acc.at[pl.ds(0, own_blocks)], out_h)))


def own_tiles(tile_dst, tile_src, tiles, x, far_blocks):
    n = tiles.shape[0]
    return pl.pallas_call(
        functools.partial(own_kernel, far_blocks=far_blocks),
        out_shape=(
            pltpu.HBM(x.shape, F32),
            jax.ShapeDtypeStruct((2, n + UNROLL), jnp.int32),
        ),
        in_specs=[HBM, HBM, HBM, HBM],
        out_specs=(HBM, SMEM),
        scratch_shapes=[
            pltpu.SMEM((n,), jnp.int32),
            pltpu.SMEM((n,), jnp.int32),
            pltpu.VMEM(x.shape, BF16),
            pltpu.VMEM(tiles.shape, BF16),
            pltpu.VMEM((x.shape[0] + 1,) + x.shape[1:], F32),
            pltpu.SemaphoreType.DMA((4,)),
        ],
        compiler_params=params(),
        cost_estimate=cost(2 * n * 128**3, 1 << 23),
        name="own_tiles",
    )(hbm(tile_dst), hbm(tile_src), hbm(tiles), hbm(x))


def far_kernel(lists, tiles, incoming_h, base_h, out_h, source, acc, out, sems):
    n_dom, rows, _ = incoming_h.shape
    own_blocks, tile, _ = base_h.shape
    hub_dev = rows - tile
    hub_blocks = n_dom * hub_dev // tile
    pairs = [(incoming_h.at[:, pl.ds(0, tile), :], source.at[pl.ds(hub_blocks, n_dom)])]
    pairs.append((base_h, acc.at[pl.ds(0, own_blocks)]))
    for q in range(n_dom):
        block, row = divmod(q * hub_dev, tile)
        pairs.append(
            (incoming_h.at[q, pl.ds(tile, hub_dev), :], source.at[block, pl.ds(row, hub_dev), :])
        )
    wait_copies(start_copies(sems, *pairs))
    add_tiles(lists, 1, tiles, source, acc, own_blocks)
    out[...] = acc[:own_blocks].astype(BF16)
    wait_copies(start_copies(sems, (out, out_h)))


def far_tiles(lists, tiles, incoming, base, far_blocks):
    own_blocks, tile, width = base.shape
    return pl.pallas_call(
        far_kernel,
        out_shape=pltpu.HBM(base.shape, BF16),
        in_specs=[SMEM, VMEM, HBM, HBM],
        out_specs=HBM,
        scratch_shapes=[
            pltpu.VMEM((far_blocks, tile, width), BF16),
            pltpu.VMEM((own_blocks + 1, tile, width), F32),
            pltpu.VMEM(base.shape, BF16),
            pltpu.SemaphoreType.DMA((incoming.shape[0] + 2,)),
        ],
        compiler_params=params(),
        cost_estimate=cost(tiles.shape[0] * 128**3, 1 << 22),
        name="far_tiles",
    )(lists, tiles, hbm(incoming), hbm(base))


def by_shards(me, shards, w):
    width = shards[0].shape[1]
    rows = [
        w[pl.ds(pl.multiple_of((me ^ k) * width, width), width), :] for k in range(len(shards))
    ]
    return jnp.dot(
        jnp.concatenate([s[...] for s in shards], axis=1),
        jnp.concatenate(rows, axis=0),
        preferred_element_type=F32,
    )


def stream(step, ins_h, ins, outs_h, outs, sems, block):
    rows = ins[0].shape[0]
    n_in = len(ins)
    pending = []
    for i in range(rows // block):
        at = pl.ds(i * block, block)
        pairs = [(a.at[at], b.at[at]) for a, b in zip(ins_h, ins)]
        pending.append(start_copies(sems.at[i], *pairs))
    leaving = []
    for i in range(rows // block):
        at = pl.ds(i * block, block)
        wait_copies(pending[i])
        step(at, [r.at[at] for r in ins], [r.at[at] for r in outs])
        pairs = [(a.at[at], b.at[at]) for a, b in zip(outs, outs_h)]
        leaving.append(start_copies(sems.at[i, pl.ds(n_in, len(outs))], *pairs))
    for copies in leaving:
        wait_copies(copies)


def stream_call(kernel, me, streamed, whole, outs, flops, name, block=512):
    rows = streamed[0].shape[0]
    n_in, n_whole, n_out = len(streamed), len(whole), len(outs)

    def run(me_s, *refs):
        ins_h, refs = refs[:n_in], refs[n_in:]
        held, refs = refs[:n_whole], refs[n_whole:]
        outs_h, refs = refs[:n_out], refs[n_out:]
        ins, refs = refs[:n_in], refs[n_in:]
        out, sems = refs[:n_out], refs[n_out]
        stream(
            lambda at, i, o: kernel(me_s[0], i, held, o), ins_h, ins, outs_h, out, sems, block
        )

    return pl.pallas_call(
        run,
        out_shape=tuple(pltpu.HBM(shape, t) for shape, t in outs),
        in_specs=[SMEM] + [ANY] * n_in + [VMEM] * n_whole,
        out_specs=(HBM,) * n_out,
        scratch_shapes=[pltpu.VMEM(x.shape, x.dtype) for x in streamed]
        + [pltpu.VMEM(shape, t) for shape, t in outs]
        + [pltpu.SemaphoreType.DMA((rows // block, n_in + n_out))],
        compiler_params=params(),
        cost_estimate=cost(flops, 1 << 22),
        name=name,
    )(me, *streamed, *[hbm(x) for x in whole])


def self_step(me, ins, held, outs):
    w, bias = held
    outs[0][...] = by_shards(me, ins, w) + bias[...]


def forward_step(me, ins, held, outs):
    *shards, own_part, grad_out = ins
    output, grad_pre = outs
    pre_act = own_part[...] + by_shards(me, shards, held[0])
    gate = jax.nn.sigmoid(pre_act)
    output[...] = (pre_act * gate).astype(BF16)
    grad = grad_out[...].astype(F32) * gate * (1.0 + pre_act * (1.0 - gate))
    grad_pre[...] = grad.astype(BF16)


def weights_kernel(*refs, n_feat):
    shards, grad, out_h, out, sems = refs[: 2 * n_feat], *refs[2 * n_feat :]
    n_dom, chunk = out.shape[0], out.shape[1] - 8
    width = grad.shape[1]
    flipped = grad[...].T
    bias = jnp.sum(grad[...].astype(F32), axis=0, keepdims=True)
    for i, shard in enumerate(shards):
        block = jnp.dot(flipped, shard[...], preferred_element_type=F32).T
        for row in range(0, width, min(chunk, width)):
            q, start = divmod(i * width + row, chunk)
            n = min(chunk, width)
            out[q, start : start + n, :] = block[row : row + n, :]
    for q in range(n_dom):
        out[q, chunk:, :] = jnp.broadcast_to(bias, (8, width))
    wait_copies(start_copies(sems, (out, out_h)))


def weight_parts(shards, grad, n_dom):
    n_feat = len(shards) // 2
    width = grad.shape[1]
    chunk = 2 * n_feat * width // n_dom
    return pl.pallas_call(
        functools.partial(weights_kernel, n_feat=n_feat),
        out_shape=pltpu.HBM((n_dom, chunk + 8, width), F32),
        in_specs=[VMEM] * (2 * n_feat + 1),
        out_specs=HBM,
        scratch_shapes=[
            pltpu.VMEM((n_dom, chunk + 8, width), F32),
            pltpu.SemaphoreType.DMA((1,)),
        ],
        compiler_params=params(),
        cost_estimate=cost(4 * n_feat * width * width * grad.shape[0], 1 << 22),
        name="weight_parts",
    )(*shards, grad)


def split_copies(sems, pairs, block):
    rows = pairs[0][0].shape[0]
    return [
        start_copies(
            sems.at[i], *[(a.at[pl.ds(i * block, block)], b.at[pl.ds(i * block, block)]) for a, b in pairs]
        )
        for i in range(rows // block)
    ]


def back_far_kernel(*refs, n_feat):
    lists, tiles = refs[:2]
    grads_h, w = refs[2 : 2 + n_feat], refs[2 + n_feat : 2 + 2 * n_feat]
    out_h, back_h, direct_h = refs[2 + 2 * n_feat : 5 + 2 * n_feat]
    grads = refs[5 + 2 * n_feat : 5 + 3 * n_feat]
    back, direct, acc, out, sems, out_sems = refs[5 + 3 * n_feat :]
    n_dom = out.shape[0]
    own_blocks, tile, width = back.shape
    hub_dev = out.shape[1] - tile
    hub_blocks = n_dom * hub_dev // tile
    block = 4 * tile
    pending = split_copies(sems, list(zip(grads_h, grads)), block)
    acc[...] = jnp.zeros_like(acc)
    own_w, near_w, far_w, both_w = w
    rows = [r.reshape(2 * width, -1) for r in (own_w[...], near_w[...], far_w[0], both_w[1])]
    rows = jnp.concatenate(rows, axis=1)
    for i, copies in enumerate(pending):
        wait_copies(copies)
        whole = jnp.concatenate([g[i * block : (i + 1) * block, :] for g in grads], axis=1)
        both = lax.dot_general(whole, rows, (((1,), (1,)), ((), ())), preferred_element_type=F32)
        direct[4 * i : 4 * (i + 1)] = both[:, :width].reshape(4, tile, width)
        back[4 * i : 4 * (i + 1)] = both[:, width:].astype(BF16).reshape(4, tile, width)
    leaving = start_copies(out_sems, (direct, direct_h), (back, back_h))
    add_tiles_t(lists, 1, tiles, back, acc, own_blocks)
    for q in range(n_dom):
        out[q, :tile, :] = acc[hub_blocks + q].astype(BF16)
        at, row = divmod(q * hub_dev, tile)
        out[q, tile:, :] = acc[at, row : row + hub_dev, :].astype(BF16)
    leaving += start_copies(out_sems.at[pl.ds(2, 1)], (out, out_h))
    wait_copies(leaving)


def back_far(lists, tiles, grads, w, n_dom, hub_dev, tile):
    n_feat = len(grads)
    rows, width = grads[0].shape
    far_blocks = n_dom * hub_dev // tile + n_dom
    shape = (n_dom, tile + hub_dev, width)
    back_shape = (rows // tile, tile, width)
    return pl.pallas_call(
        functools.partial(back_far_kernel, n_feat=n_feat),
        out_shape=(pltpu.HBM(shape, BF16), pltpu.HBM(back_shape, BF16), pltpu.HBM(back_shape, F32)),
        in_specs=[SMEM, VMEM] + [ANY] * n_feat + [VMEM] * n_feat,
        out_specs=(HBM, HBM, HBM),
        scratch_shapes=[pltpu.VMEM((rows, width), BF16)] * n_feat
        + [
            pltpu.VMEM(back_shape, BF16),
            pltpu.VMEM(back_shape, F32),
            pltpu.VMEM((far_blocks + 1, tile, width), F32),
            pltpu.VMEM(shape, BF16),
            pltpu.SemaphoreType.DMA((rows // (4 * tile), n_feat)),
            pltpu.SemaphoreType.DMA((3,)),
        ],
        compiler_params=params(),
        cost_estimate=cost(4 * rows * width * width * n_feat, 1 << 22),
        name="back_far",
    )(lists, tiles, *grads, *[hbm(r) for r in w])


def back_own_kernel(lists, tiles, back_h, direct_h, out_h, back, acc, sems):
    own_blocks = back.shape[0]
    own = acc.at[pl.ds(0, own_blocks)]
    wait_copies(start_copies(sems, (back_h, back), (direct_h, own)))
    add_tiles_t(lists, 0, tiles, back, acc, own_blocks)
    wait_copies(start_copies(sems, (own, out_h)))


def back_own(lists, tiles, back, direct):
    return pl.pallas_call(
        back_own_kernel,
        out_shape=pltpu.HBM(direct.shape, F32),
        in_specs=[SMEM, VMEM, HBM, HBM],
        out_specs=HBM,
        scratch_shapes=[
            pltpu.VMEM(back.shape, BF16),
            pltpu.VMEM((direct.shape[0] + 1,) + direct.shape[1:], F32),
            pltpu.SemaphoreType.DMA((2,)),
        ],
        compiler_params=params(),
        cost_estimate=cost(2 * tiles.shape[0] * 128**3, 1 << 23),
        name="back_own",
    )(lists, tiles, hbm(back), hbm(direct))


def finish_kernel(rows_s, count_h, hub_h, incoming_h, base_h, out_h, count_s, hub_s, sent, hubs, base, sems, out_sems):
    n_dom, capacity = rows_s.shape
    hub_dev = hub_s.shape[0]
    own_count, width = base.shape
    block, peers = 256, min(8, n_dom)
    copies = start_copies(
        sems,
        (count_h, count_s),
        (hub_h, hub_s),
        (incoming_h.at[:, pl.ds(0, capacity), :], sent),
        (incoming_h.at[:, pl.ds(capacity, hub_dev), :], hubs),
        (base_h, base),
    )
    wait_copies(copies)
    hub = hubs[0].astype(F32)
    for q in range(1, n_dom):
        hub += hubs[q].astype(F32)
    for j in range(hub_dev):
        base[pl.ds(hub_s[j], 1), :] += hub[j : j + 1, :]
    lane = lax.broadcasted_iota(jnp.int32, (1, capacity), 1)
    leaving = []
    for start in range(0, own_count, block):
        vertex = lax.broadcasted_iota(jnp.int32, (block, capacity), 0) + start
        total = base[start : start + block, :]
        for first in range(0, n_dom, peers):
            hot, rows = [], []
            for q in range(first, first + peers):
                wanted = jnp.where(lane < count_s[0, q], rows_s[q : q + 1, :], -1)
                hot.append((vertex == wanted).astype(F32).astype(BF16))
                rows.append(sent[q])
            total += jnp.dot(
                jnp.concatenate(hot, axis=1),
                jnp.concatenate(rows, axis=0),
                preferred_element_type=F32,
            )
        base[start : start + block, :] = total
        at = pl.ds(start, block)
        leaving.append(start_copies(out_sems.at[pl.ds(start // block, 1)], (base.at[at], out_h.at[at])))
    for copies in leaving:
        wait_copies(copies)


def finish(send_rows, send_count, hub_ids, incoming, base):
    n_dom, capacity = send_rows.shape
    hub_dev = hub_ids.shape[0]
    own_count, width = base.shape
    return pl.pallas_call(
        finish_kernel,
        out_shape=pltpu.HBM(base.shape, F32),
        in_specs=[VMEM, HBM, HBM, ANY, HBM],
        out_specs=HBM,
        scratch_shapes=[
            pltpu.SMEM(send_count.shape, jnp.int32),
            pltpu.SMEM(hub_ids.shape, jnp.int32),
            pltpu.VMEM((n_dom, capacity, width), BF16),
            pltpu.VMEM((n_dom, hub_dev, width), BF16),
            pltpu.VMEM(base.shape, F32),
            pltpu.SemaphoreType.DMA((5,)),
            pltpu.SemaphoreType.DMA((own_count // 256,)),
        ],
        compiler_params=params(),
        cost_estimate=cost(2 * base.size * send_rows.size, 1 << 22),
        name="finish",
    )(hbm(send_rows), hbm(send_count), hbm(hub_ids), incoming, hbm(base))


def cut_kernel(me_s, w_self, w_neigh, *outs):
    width = w_self.shape[1]
    own, near, far = outs
    for k, out in enumerate((own, near, far.at[0], far.at[1])):
        at = pl.ds(pl.multiple_of((me_s[0] ^ k) * width, width), width)
        out[0] = w_self[at, :]
        out[1] = w_neigh[at, :]


def cut_weights(me, w_self, w_neigh):
    width = w_self.shape[1]
    one = (2, width, width)
    return pl.pallas_call(
        cut_kernel,
        out_shape=tuple(pltpu.HBM(shape, BF16) for shape in (one, one, (2,) + one)),
        in_specs=[SMEM, VMEM, VMEM],
        out_specs=(VMEM,) * 3,
        compiler_params=params(),
        cost_estimate=cost(0, 1 << 20),
        name="cut_weights",
    )(me, hbm(w_self), hbm(w_neigh))


def sum_kernel(parts, out, bias):
    n_dom, chunk, _ = out.shape
    total = parts[0]
    for q in range(1, n_dom):
        total += parts[q]
    bias[...] = total[chunk : chunk + 1, :]
    rows = total[:chunk, :].astype(BF16)
    for q in range(n_dom):
        out[q] = rows


def sum_parts(parts):
    n_dom, rows, width = parts.shape
    return pl.pallas_call(
        sum_kernel,
        out_shape=(pltpu.HBM((n_dom, rows - 8, width), BF16), pltpu.HBM((1, width), F32)),
        in_specs=[VMEM],
        out_specs=(VMEM, VMEM),
        compiler_params=params(),
        cost_estimate=cost(0, 1 << 20),
        name="sum_parts",
    )(hbm(parts))


def place_kernel(me_s, sums, self_out, neigh_out):
    rows, width = self_out.shape
    for i in range(2 * rows // width):
        which, k = divmod(i, rows // width)
        target = (self_out, neigh_out)[which]
        at = pl.ds(pl.multiple_of((me_s[0] ^ k) * width, width), width)
        target[at, :] = sums[i * width : (i + 1) * width, :].astype(F32)


def place_weights(me, sums):
    rows, width = sums.shape[0] // 2, sums.shape[1]
    return pl.pallas_call(
        place_kernel,
        out_shape=(pltpu.HBM((rows, width), F32),) * 2,
        in_specs=[SMEM, VMEM],
        out_specs=(VMEM, VMEM),
        compiler_params=params(),
        cost_estimate=cost(0, 1 << 20),
        name="place_weights",
    )(me, sums)


def body(
    node_feats,
    edge_tiles,
    tile_dst,
    tile_src,
    hub_ids,
    send_rows,
    send_count,
    w_self,
    w_neigh,
    out_bias,
    grad_out,
    *,
    n_feat,
):
    own_count, width = node_feats.shape
    tile_size = edge_tiles.shape[1]
    listed = send_rows[0]
    n_dom, capacity = listed.shape
    hub_dev = hub_ids.shape[0]
    me = lax.axis_index("feat").astype(jnp.int32)
    me_s = me.reshape(1)
    far, near = 2, 1
    assert n_feat == 4
    far_blocks = n_dom * hub_dev // tile_size + n_dom

    def swap(x, k):
        return lax.ppermute(x, "feat", [(j, j ^ k) for j in range(n_feat)])

    feat_far = swap(node_feats, far)

    outgoing = pick(listed, send_count, hub_ids, node_feats)
    incoming = lax.all_to_all(outgoing, "dom", 0, 0, tiled=True)
    cut = cut_weights(me_s, w_self, w_neigh)
    own_feats, *cut = lax.optimization_barrier((node_feats.reshape(-1, tile_size, width), *cut))
    far_w = swap(cut[2], far)
    base, lists = own_tiles(tile_dst, tile_src, edge_tiles, own_feats, far_blocks)
    aggregated = far_tiles(lists, edge_tiles, incoming, base, far_blocks).reshape(own_count, width)

    aggregated, far_w = lax.optimization_barrier((aggregated, far_w))
    w_rows = [cut[0], swap(cut[1], near), far_w, swap(far_w, near)]
    agg_far = swap(aggregated, far)
    feat_far, aggregated = lax.optimization_barrier((feat_far, aggregated))
    feats = [hbm(node_feats), swap(node_feats, near), feat_far, swap(feat_far, near)]
    flops = 2 * own_count * n_feat * width * width
    rows_out = ((own_count, width), BF16)
    (own_part,) = stream_call(
        self_step,
        me_s,
        feats,
        [w_self, out_bias[None, :]],
        [((own_count, width), F32)],
        flops,
        "self_dense",
    )
    agg_far, own_part, *w_rows = lax.optimization_barrier((agg_far, own_part, *w_rows))
    aggs = [hbm(aggregated), swap(aggregated, near), agg_far, swap(agg_far, near)]
    output, grad_pre = stream_call(
        forward_step,
        me_s,
        [*aggs, hbm(own_part), hbm(grad_out)],
        [w_neigh],
        [rows_out, rows_out],
        flops,
        "forward_dense",
    )

    grad_far = swap(grad_pre, far)
    parts = weight_parts(feats + aggs, hbm(grad_pre), n_dom)
    part_sums = lax.all_to_all(parts, "dom", 0, 0, tiled=True)
    grads = [hbm(grad_pre), swap(grad_pre, near), grad_far, swap(grad_far, near)]

    back_out, back_agg, direct = back_far(
        lists, edge_tiles, grads, w_rows, n_dom, hub_dev, tile_size
    )
    back_in = lax.all_to_all(back_out, "dom", 0, 0, tiled=True)
    own = back_own(lists, edge_tiles, back_agg, direct).reshape(own_count, width)
    weights_out, grad_bias = sum_parts(part_sums)
    weights_out, back_in, own = lax.optimization_barrier((weights_out, back_in, own))
    weights_in = lax.all_to_all(weights_out, "dom", 0, 0, tiled=True)
    grad_feats = finish(listed, send_count, hub_ids, back_in, own)
    grad_self, grad_neigh = place_weights(me_s, weights_in.reshape(-1, width))
    return (output, grad_feats, grad_self, grad_neigh, grad_bias[0])


def solution(mesh):
    in_specs = (
        P("dom", "feat"),
        P("dom", None, None),
        P("dom"),
        P("dom"),
        P("dom"),
        P("dom", None, None),
        P("dom", None),
        P(None, "feat"),
        P(None, "feat"),
        P("feat"),
        P("dom", "feat"),
    )
    out_specs = (P("dom", "feat"), P("dom", "feat"), P(None, "feat"), P(None, "feat"), P("feat"))
    n_feat = mesh.shape["feat"]

    def run(*args):
        return body(*args, n_feat=n_feat)

    return jax.shard_map(run, mesh=mesh, in_specs=in_specs, out_specs=out_specs, check_vma=False)
```

```python
import functools

import jax
import jax.numpy as jnp
from jax import lax
from jax.experimental import pallas as pl
from jax.experimental.pallas import tpu as pltpu
from jax.sharding import PartitionSpec as P

F32 = jnp.float32
BF16 = jnp.bfloat16
VMEM = pl.BlockSpec(memory_space=pltpu.VMEM)
SMEM = pl.BlockSpec(memory_space=pltpu.SMEM)
HBM = pl.BlockSpec(memory_space=pltpu.HBM)
ANY = pl.BlockSpec(memory_space=pl.ANY)
UNROLL = 16
T_BITS, S_BITS = 10, 10


def params(mib=24):
    return pltpu.CompilerParams(vmem_limit_bytes=mib << 20)


def hbm(x):
    return pltpu.with_memory_space_constraint(x, pltpu.HBM)


def cost(flops, nbytes):
    return pl.CostEstimate(flops=flops, bytes_accessed=nbytes, transcendentals=0)


def start_copies(sems, *pairs):
    copies = [pltpu.make_async_copy(a, b, sems.at[i]) for i, (a, b) in enumerate(pairs)]
    for copy in copies:
        copy.start()
    return copies


def wait_copies(copies):
    for copy in copies:
        copy.wait()


def pick_kernel(rows_h, count_h, hub_h, x_h, out_h, rows_s, count_s, hub_s, x, x32, stage, out, sems, out_sems):
    copies = start_copies(sems, (x_h, x), (rows_h, rows_s), (count_h, count_s), (hub_h, hub_s))
    n_dom, capacity = rows_s.shape
    hub_dev = hub_s.shape[0]
    step = 32
    wait_copies(copies)
    x32[...] = x[...].astype(F32)
    for j in range(hub_dev):
        stage[capacity + j : capacity + j + 1, :] = x32[pl.ds(hub_s[j], 1), :]
    hub = stage[capacity:, :].astype(BF16)
    slot = lax.broadcasted_iota(jnp.int32, (capacity, x.shape[1]), 0)

    def peer(q, carry):
        def some(g, carry):
            for u in range(step):
                c = g * step + u
                stage[pl.ds(c, 1), :] = x32[pl.ds(rows_s[q, c], 1), :]
            return carry

        lax.fori_loop(0, capacity // step, some, 0)
        kept = jnp.where(slot < count_s[0, q], stage[:capacity, :], 0.0)
        out[q, :capacity, :] = kept.astype(BF16)
        out[q, capacity:, :] = hub
        pltpu.make_async_copy(out.at[q], out_h.at[q], out_sems.at[q]).start()
        return carry

    lax.fori_loop(0, n_dom, peer, 0)
    for q in range(n_dom):
        pltpu.make_async_copy(out.at[q], out_h.at[q], out_sems.at[q]).wait()


def pick(send_rows, send_count, hub_ids, x):
    n_dom, capacity = send_rows.shape
    rows = capacity + hub_ids.shape[0]
    shape = (n_dom, rows, x.shape[1])
    return pl.pallas_call(
        pick_kernel,
        out_shape=pltpu.HBM(shape, BF16),
        in_specs=[HBM] * 4,
        out_specs=HBM,
        scratch_shapes=[
            pltpu.SMEM(send_rows.shape, jnp.int32),
            pltpu.SMEM(send_count.shape, jnp.int32),
            pltpu.SMEM(hub_ids.shape, jnp.int32),
            pltpu.VMEM(x.shape, BF16),
            pltpu.VMEM(x.shape, F32),
            pltpu.VMEM((rows, x.shape[1]), F32),
            pltpu.VMEM(shape, BF16),
            pltpu.SemaphoreType.DMA((4,)),
            pltpu.SemaphoreType.DMA((n_dom,)),
        ],
        compiler_params=params(),
        cost_estimate=cost(0, 1 << 21),
        name="pick_rows",
    )(hbm(send_rows), hbm(send_count), hbm(hub_ids), hbm(x))


def unpack(entry):
    t = entry & ((1 << T_BITS) - 1)
    s = (entry >> T_BITS) & ((1 << S_BITS) - 1)
    return t, s, entry >> (T_BITS + S_BITS)


def make_lists(dst_s, src_s, lists, own_blocks, far_blocks):
    length = lists.shape[1] - 1

    def step(t, n):
        s = src_s[t]
        d = dst_s[t]
        far = (s >= own_blocks).astype(jnp.int32)
        lists[0, n[0]] = t + (s << T_BITS) + (d << (T_BITS + S_BITS))
        lists[1, n[1]] = t + ((s - own_blocks) << T_BITS) + (d << (T_BITS + S_BITS))
        return n[0] + 1 - far, n[1] + far

    n = lax.fori_loop(0, dst_s.shape[0], step, (jnp.int32(0), jnp.int32(0)))
    for which, blocks in ((0, own_blocks), (1, far_blocks)):
        spare = (blocks << T_BITS) + (own_blocks << (T_BITS + S_BITS))
        for u in range(UNROLL - 1):
            lists[which, n[which] + u] = jnp.int32(spare)
        lists[which, length] = n[which]


def add_tiles(lists, which, tiles, source, acc, spare):
    n = lists[which, lists.shape[1] - 1]

    def group(g, carry):
        done = []
        for u in range(UNROLL):
            t, s, d = unpack(lists[which, g * UNROLL + u])
            s = jnp.where(d == spare, 0, s)
            done.append((d, jnp.dot(tiles[t], source[s], preferred_element_type=F32)))
        for d, product in done:
            acc[d] += product
        return carry

    lax.fori_loop(0, (n + UNROLL - 1) // UNROLL, group, 0)


def add_tiles_t(lists, which, tiles, source, acc, spare):
    n = lists[which, lists.shape[1] - 1]

    def group(g, carry):
        done = []
        for u in range(UNROLL):
            t, s, d = unpack(lists[which, g * UNROLL + u])
            d = jnp.where(d == spare, 0, d)
            product = lax.dot_general(
                tiles[t], source[d], (((0,), (0,)), ((), ())), preferred_element_type=F32
            )
            done.append((s, product))
        for s, product in done:
            acc[s] += product
        return carry

    lax.fori_loop(0, (n + UNROLL - 1) // UNROLL, group, 0)


def own_kernel(
    dst_h, src_h, tiles_h, x_h, out_h, lists, dst_s, src_s, x, tiles, acc, sems, *, far_blocks
):
    own_blocks = x.shape[0]
    copies = start_copies(sems, (dst_h, dst_s), (src_h, src_s), (x_h, x), (tiles_h, tiles))
    acc[...] = jnp.zeros_like(acc)
    wait_copies(copies[:2])
    make_lists(dst_s, src_s, lists, own_blocks, far_blocks)
    wait_copies(copies[2:])
    add_tiles(lists, 0, tiles, x, acc, own_blocks)
    wait_copies(start_copies(sems, (acc.at[pl.ds(0, own_blocks)], out_h)))


def own_tiles(tile_dst, tile_src, tiles, x, far_blocks):
    n = tiles.shape[0]
    return pl.pallas_call(
        functools.partial(own_kernel, far_blocks=far_blocks),
        out_shape=(
            pltpu.HBM(x.shape, F32),
            jax.ShapeDtypeStruct((2, n + UNROLL), jnp.int32),
        ),
        in_specs=[HBM, HBM, HBM, HBM],
        out_specs=(HBM, SMEM),
        scratch_shapes=[
            pltpu.SMEM((n,), jnp.int32),
            pltpu.SMEM((n,), jnp.int32),
            pltpu.VMEM(x.shape, BF16),
            pltpu.VMEM(tiles.shape, BF16),
            pltpu.VMEM((x.shape[0] + 1,) + x.shape[1:], F32),
            pltpu.SemaphoreType.DMA((4,)),
        ],
        compiler_params=params(),
        cost_estimate=cost(2 * n * 128**3, 1 << 23),
        name="own_tiles",
    )(hbm(tile_dst), hbm(tile_src), hbm(tiles), hbm(x))


def far_kernel(lists, tiles, incoming_h, base_h, out_h, source, acc, out, sems):
    n_dom, rows, _ = incoming_h.shape
    own_blocks, tile, _ = base_h.shape
    hub_dev = rows - tile
    hub_blocks = n_dom * hub_dev // tile
    pairs = [(incoming_h.at[:, pl.ds(0, tile), :], source.at[pl.ds(hub_blocks, n_dom)])]
    pairs.append((base_h, acc.at[pl.ds(0, own_blocks)]))
    for q in range(n_dom):
        block, row = divmod(q * hub_dev, tile)
        pairs.append(
            (incoming_h.at[q, pl.ds(tile, hub_dev), :], source.at[block, pl.ds(row, hub_dev), :])
        )
    wait_copies(start_copies(sems, *pairs))
    add_tiles(lists, 1, tiles, source, acc, own_blocks)
    out[...] = acc[:own_blocks].astype(BF16)
    wait_copies(start_copies(sems, (out, out_h)))


def far_tiles(lists, tiles, incoming, base, far_blocks):
    own_blocks, tile, width = base.shape
    return pl.pallas_call(
        far_kernel,
        out_shape=pltpu.HBM(base.shape, BF16),
        in_specs=[SMEM, VMEM, HBM, HBM],
        out_specs=HBM,
        scratch_shapes=[
            pltpu.VMEM((far_blocks, tile, width), BF16),
            pltpu.VMEM((own_blocks + 1, tile, width), F32),
            pltpu.VMEM(base.shape, BF16),
            pltpu.SemaphoreType.DMA((incoming.shape[0] + 2,)),
        ],
        compiler_params=params(),
        cost_estimate=cost(tiles.shape[0] * 128**3, 1 << 22),
        name="far_tiles",
    )(lists, tiles, hbm(incoming), hbm(base))


def by_shards(me, shards, w):
    width = shards[0].shape[1]
    rows = [
        w[pl.ds(pl.multiple_of((me ^ k) * width, width), width), :] for k in range(len(shards))
    ]
    return jnp.dot(
        jnp.concatenate([s[...] for s in shards], axis=1),
        jnp.concatenate(rows, axis=0),
        preferred_element_type=F32,
    )


def stream(step, ins_h, ins, outs_h, outs, sems, block):
    rows = ins[0].shape[0]
    n_in = len(ins)
    pending = []
    for i in range(rows // block):
        at = pl.ds(i * block, block)
        pairs = [(a.at[at], b.at[at]) for a, b in zip(ins_h, ins)]
        pending.append(start_copies(sems.at[i], *pairs))
    leaving = []
    for i in range(rows // block):
        at = pl.ds(i * block, block)
        wait_copies(pending[i])
        step(at, [r.at[at] for r in ins], [r.at[at] for r in outs])
        pairs = [(a.at[at], b.at[at]) for a, b in zip(outs, outs_h)]
        leaving.append(start_copies(sems.at[i, pl.ds(n_in, len(outs))], *pairs))
    for copies in leaving:
        wait_copies(copies)


def stream_call(kernel, me, streamed, whole, outs, flops, name, block=1024):
    rows = streamed[0].shape[0]
    n_in, n_whole, n_out = len(streamed), len(whole), len(outs)

    def run(me_s, *refs):
        ins_h, refs = refs[:n_in], refs[n_in:]
        held, refs = refs[:n_whole], refs[n_whole:]
        outs_h, refs = refs[:n_out], refs[n_out:]
        ins, refs = refs[:n_in], refs[n_in:]
        out, sems = refs[:n_out], refs[n_out]
        stream(
            lambda at, i, o: kernel(me_s[0], i, held, o), ins_h, ins, outs_h, out, sems, block
        )

    return pl.pallas_call(
        run,
        out_shape=tuple(pltpu.HBM(shape, t) for shape, t in outs),
        in_specs=[SMEM] + [ANY] * n_in + [VMEM] * n_whole,
        out_specs=(HBM,) * n_out,
        scratch_shapes=[pltpu.VMEM(x.shape, x.dtype) for x in streamed]
        + [pltpu.VMEM(shape, t) for shape, t in outs]
        + [pltpu.SemaphoreType.DMA((rows // block, n_in + n_out))],
        compiler_params=params(),
        cost_estimate=cost(flops, 1 << 22),
        name=name,
    )(me, *streamed, *[hbm(x) for x in whole])


def self_step(me, ins, held, outs):
    w, bias = held
    outs[0][...] = by_shards(me, ins, w) + bias[...]


def forward_step(me, ins, held, outs):
    *shards, own_part, grad_out = ins
    output, grad_pre = outs
    pre_act = own_part[...] + by_shards(me, shards, held[0])
    gate = jax.nn.sigmoid(pre_act)
    output[...] = (pre_act * gate).astype(BF16)
    grad = grad_out[...].astype(F32) * gate * (1.0 + pre_act * (1.0 - gate))
    grad_pre[...] = grad.astype(BF16)


def weights_kernel(*refs, n_feat):
    shards, grad, out_h, out, sems = refs[: 2 * n_feat], *refs[2 * n_feat :]
    n_dom, chunk = out.shape[0], out.shape[1] - 8
    width = grad.shape[1]
    flipped = grad[...].T
    bias = jnp.sum(grad[...].astype(F32), axis=0, keepdims=True)
    for i, shard in enumerate(shards):
        block = jnp.dot(flipped, shard[...], preferred_element_type=F32).T
        for row in range(0, width, min(chunk, width)):
            q, start = divmod(i * width + row, chunk)
            n = min(chunk, width)
            out[q, start : start + n, :] = block[row : row + n, :]
    for q in range(n_dom):
        out[q, chunk:, :] = jnp.broadcast_to(bias, (8, width))
    wait_copies(start_copies(sems, (out, out_h)))


def weight_parts(shards, grad, n_dom):
    n_feat = len(shards) // 2
    width = grad.shape[1]
    chunk = 2 * n_feat * width // n_dom
    return pl.pallas_call(
        functools.partial(weights_kernel, n_feat=n_feat),
        out_shape=pltpu.HBM((n_dom, chunk + 8, width), F32),
        in_specs=[VMEM] * (2 * n_feat + 1),
        out_specs=HBM,
        scratch_shapes=[
            pltpu.VMEM((n_dom, chunk + 8, width), F32),
            pltpu.SemaphoreType.DMA((1,)),
        ],
        compiler_params=params(),
        cost_estimate=cost(4 * n_feat * width * width * grad.shape[0], 1 << 22),
        name="weight_parts",
    )(*shards, grad)


def split_copies(sems, pairs, block):
    rows = pairs[0][0].shape[0]
    return [
        start_copies(
            sems.at[i], *[(a.at[pl.ds(i * block, block)], b.at[pl.ds(i * block, block)]) for a, b in pairs]
        )
        for i in range(rows // block)
    ]


def back_far_kernel(*refs, n_feat):
    lists, tiles = refs[:2]
    grads_h, w = refs[2 : 2 + n_feat], refs[2 + n_feat : 2 + 2 * n_feat]
    out_h, back_h, direct_h = refs[2 + 2 * n_feat : 5 + 2 * n_feat]
    grads = refs[5 + 2 * n_feat : 5 + 3 * n_feat]
    back, direct, acc, out, sems, out_sems = refs[5 + 3 * n_feat :]
    n_dom = out.shape[0]
    own_blocks, tile, width = back.shape
    hub_dev = out.shape[1] - tile
    hub_blocks = n_dom * hub_dev // tile
    block = 4 * tile
    pending = split_copies(sems, list(zip(grads_h, grads)), block)
    acc[...] = jnp.zeros_like(acc)
    own_w, near_w, far_w, both_w = w
    rows = [r.reshape(2 * width, -1) for r in (own_w[...], near_w[...], far_w[0], both_w[1])]
    rows = jnp.concatenate(rows, axis=1)
    for i, copies in enumerate(pending):
        wait_copies(copies)
        whole = jnp.concatenate([g[i * block : (i + 1) * block, :] for g in grads], axis=1)
        both = lax.dot_general(whole, rows, (((1,), (1,)), ((), ())), preferred_element_type=F32)
        direct[4 * i : 4 * (i + 1)] = both[:, :width].reshape(4, tile, width)
        back[4 * i : 4 * (i + 1)] = both[:, width:].astype(BF16).reshape(4, tile, width)
    leaving = start_copies(out_sems, (direct, direct_h), (back, back_h))
    add_tiles_t(lists, 1, tiles, back, acc, own_blocks)
    for q in range(n_dom):
        out[q, :tile, :] = acc[hub_blocks + q].astype(BF16)
        at, row = divmod(q * hub_dev, tile)
        out[q, tile:, :] = acc[at, row : row + hub_dev, :].astype(BF16)
    leaving += start_copies(out_sems.at[pl.ds(2, 1)], (out, out_h))
    wait_copies(leaving)


def back_far(lists, tiles, grads, w, n_dom, hub_dev, tile):
    n_feat = len(grads)
    rows, width = grads[0].shape
    far_blocks = n_dom * hub_dev // tile + n_dom
    shape = (n_dom, tile + hub_dev, width)
    back_shape = (rows // tile, tile, width)
    return pl.pallas_call(
        functools.partial(back_far_kernel, n_feat=n_feat),
        out_shape=(pltpu.HBM(shape, BF16), pltpu.HBM(back_shape, BF16), pltpu.HBM(back_shape, F32)),
        in_specs=[SMEM, VMEM] + [ANY] * n_feat + [VMEM] * n_feat,
        out_specs=(HBM, HBM, HBM),
        scratch_shapes=[pltpu.VMEM((rows, width), BF16)] * n_feat
        + [
            pltpu.VMEM(back_shape, BF16),
            pltpu.VMEM(back_shape, F32),
            pltpu.VMEM((far_blocks + 1, tile, width), F32),
            pltpu.VMEM(shape, BF16),
            pltpu.SemaphoreType.DMA((rows // (4 * tile), n_feat)),
            pltpu.SemaphoreType.DMA((3,)),
        ],
        compiler_params=params(),
        cost_estimate=cost(4 * rows * width * width * n_feat, 1 << 22),
        name="back_far",
    )(lists, tiles, *grads, *[hbm(r) for r in w])


def back_own_kernel(lists, tiles, back_h, direct_h, out_h, back, acc, sems):
    own_blocks = back.shape[0]
    own = acc.at[pl.ds(0, own_blocks)]
    wait_copies(start_copies(sems, (back_h, back), (direct_h, own)))
    add_tiles_t(lists, 0, tiles, back, acc, own_blocks)
    wait_copies(start_copies(sems, (own, out_h)))


def back_own(lists, tiles, back, direct):
    return pl.pallas_call(
        back_own_kernel,
        out_shape=pltpu.HBM(direct.shape, F32),
        in_specs=[SMEM, VMEM, HBM, HBM],
        out_specs=HBM,
        scratch_shapes=[
            pltpu.VMEM(back.shape, BF16),
            pltpu.VMEM((direct.shape[0] + 1,) + direct.shape[1:], F32),
            pltpu.SemaphoreType.DMA((2,)),
        ],
        compiler_params=params(),
        cost_estimate=cost(2 * tiles.shape[0] * 128**3, 1 << 23),
        name="back_own",
    )(lists, tiles, hbm(back), hbm(direct))


def finish_kernel(rows_s, count_h, hub_h, incoming_h, base_h, out_h, count_s, hub_s, sent, hubs, base, sems, out_sems):
    n_dom, capacity = rows_s.shape
    hub_dev = hub_s.shape[0]
    own_count, width = base.shape
    block, peers = 256, min(8, n_dom)
    copies = start_copies(
        sems,
        (count_h, count_s),
        (hub_h, hub_s),
        (incoming_h.at[:, pl.ds(0, capacity), :], sent),
        (incoming_h.at[:, pl.ds(capacity, hub_dev), :], hubs),
        (base_h, base),
    )
    wait_copies(copies)
    hub = hubs[0].astype(F32)
    for q in range(1, n_dom):
        hub += hubs[q].astype(F32)
    for j in range(hub_dev):
        base[pl.ds(hub_s[j], 1), :] += hub[j : j + 1, :]
    lane = lax.broadcasted_iota(jnp.int32, (1, capacity), 1)
    leaving = []
    for start in range(0, own_count, block):
        vertex = lax.broadcasted_iota(jnp.int32, (block, capacity), 0) + start
        total = base[start : start + block, :]
        for first in range(0, n_dom, peers):
            hot, rows = [], []
            for q in range(first, first + peers):
                wanted = jnp.where(lane < count_s[0, q], rows_s[q : q + 1, :], -1)
                hot.append((vertex == wanted).astype(F32).astype(BF16))
                rows.append(sent[q])
            total += jnp.dot(
                jnp.concatenate(hot, axis=1),
                jnp.concatenate(rows, axis=0),
                preferred_element_type=F32,
            )
        base[start : start + block, :] = total
        at = pl.ds(start, block)
        leaving.append(start_copies(out_sems.at[pl.ds(start // block, 1)], (base.at[at], out_h.at[at])))
    for copies in leaving:
        wait_copies(copies)


def finish(send_rows, send_count, hub_ids, incoming, base):
    n_dom, capacity = send_rows.shape
    hub_dev = hub_ids.shape[0]
    own_count, width = base.shape
    return pl.pallas_call(
        finish_kernel,
        out_shape=pltpu.HBM(base.shape, F32),
        in_specs=[VMEM, HBM, HBM, ANY, HBM],
        out_specs=HBM,
        scratch_shapes=[
            pltpu.SMEM(send_count.shape, jnp.int32),
            pltpu.SMEM(hub_ids.shape, jnp.int32),
            pltpu.VMEM((n_dom, capacity, width), BF16),
            pltpu.VMEM((n_dom, hub_dev, width), BF16),
            pltpu.VMEM(base.shape, F32),
            pltpu.SemaphoreType.DMA((5,)),
            pltpu.SemaphoreType.DMA((own_count // 256,)),
        ],
        compiler_params=params(),
        cost_estimate=cost(2 * base.size * send_rows.size, 1 << 22),
        name="finish",
    )(hbm(send_rows), hbm(send_count), hbm(hub_ids), incoming, hbm(base))


def cut_kernel(me_s, w_self, w_neigh, *outs):
    width = w_self.shape[1]
    own, near, far = outs
    for k, out in enumerate((own, near, far.at[0], far.at[1])):
        at = pl.ds(pl.multiple_of((me_s[0] ^ k) * width, width), width)
        out[0] = w_self[at, :]
        out[1] = w_neigh[at, :]


def cut_weights(me, w_self, w_neigh):
    width = w_self.shape[1]
    one = (2, width, width)
    return pl.pallas_call(
        cut_kernel,
        out_shape=tuple(pltpu.HBM(shape, BF16) for shape in (one, one, (2,) + one)),
        in_specs=[SMEM, VMEM, VMEM],
        out_specs=(VMEM,) * 3,
        compiler_params=params(),
        cost_estimate=cost(0, 1 << 20),
        name="cut_weights",
    )(me, hbm(w_self), hbm(w_neigh))


def sum_kernel(parts, out, bias):
    n_dom, chunk, _ = out.shape
    total = parts[0]
    for q in range(1, n_dom):
        total += parts[q]
    bias[...] = total[chunk : chunk + 1, :]
    rows = total[:chunk, :].astype(BF16)
    for q in range(n_dom):
        out[q] = rows


def sum_parts(parts):
    n_dom, rows, width = parts.shape
    return pl.pallas_call(
        sum_kernel,
        out_shape=(pltpu.HBM((n_dom, rows - 8, width), BF16), pltpu.HBM((1, width), F32)),
        in_specs=[VMEM],
        out_specs=(VMEM, VMEM),
        compiler_params=params(),
        cost_estimate=cost(0, 1 << 20),
        name="sum_parts",
    )(hbm(parts))


def place_kernel(me_s, sums, self_out, neigh_out):
    rows, width = self_out.shape
    for i in range(2 * rows // width):
        which, k = divmod(i, rows // width)
        target = (self_out, neigh_out)[which]
        at = pl.ds(pl.multiple_of((me_s[0] ^ k) * width, width), width)
        target[at, :] = sums[i * width : (i + 1) * width, :].astype(F32)


def place_weights(me, sums):
    rows, width = sums.shape[0] // 2, sums.shape[1]
    return pl.pallas_call(
        place_kernel,
        out_shape=(pltpu.HBM((rows, width), F32),) * 2,
        in_specs=[SMEM, VMEM],
        out_specs=(VMEM, VMEM),
        compiler_params=params(),
        cost_estimate=cost(0, 1 << 20),
        name="place_weights",
    )(me, sums)


def body(
    node_feats,
    edge_tiles,
    tile_dst,
    tile_src,
    hub_ids,
    send_rows,
    send_count,
    w_self,
    w_neigh,
    out_bias,
    grad_out,
    *,
    n_feat,
):
    own_count, width = node_feats.shape
    tile_size = edge_tiles.shape[1]
    listed = send_rows[0]
    n_dom, capacity = listed.shape
    hub_dev = hub_ids.shape[0]
    me = lax.axis_index("feat").astype(jnp.int32)
    me_s = me.reshape(1)
    far, near = 2, 1
    assert n_feat == 4
    far_blocks = n_dom * hub_dev // tile_size + n_dom

    def swap(x, k):
        return lax.ppermute(x, "feat", [(j, j ^ k) for j in range(n_feat)])

    feat_far = swap(node_feats, far)

    outgoing = pick(listed, send_count, hub_ids, node_feats)
    incoming = lax.all_to_all(outgoing, "dom", 0, 0, tiled=True)
    cut = cut_weights(me_s, w_self, w_neigh)
    own_feats, *cut = lax.optimization_barrier((node_feats.reshape(-1, tile_size, width), *cut))
    far_w = swap(cut[2], far)
    base, lists = own_tiles(tile_dst, tile_src, edge_tiles, own_feats, far_blocks)
    aggregated = far_tiles(lists, edge_tiles, incoming, base, far_blocks).reshape(own_count, width)

    aggregated, far_w = lax.optimization_barrier((aggregated, far_w))
    w_rows = [cut[0], swap(cut[1], near), far_w, swap(far_w, near)]
    agg_far = swap(aggregated, far)
    feat_far, aggregated = lax.optimization_barrier((feat_far, aggregated))
    feats = [hbm(node_feats), swap(node_feats, near), feat_far, swap(feat_far, near)]
    flops = 2 * own_count * n_feat * width * width
    rows_out = ((own_count, width), BF16)
    (own_part,) = stream_call(
        self_step,
        me_s,
        feats,
        [w_self, out_bias[None, :]],
        [((own_count, width), F32)],
        flops,
        "self_dense",
    )
    agg_far, own_part, *w_rows = lax.optimization_barrier((agg_far, own_part, *w_rows))
    aggs = [hbm(aggregated), swap(aggregated, near), agg_far, swap(agg_far, near)]
    output, grad_pre = stream_call(
        forward_step,
        me_s,
        [*aggs, hbm(own_part), hbm(grad_out)],
        [w_neigh],
        [rows_out, rows_out],
        flops,
        "forward_dense",
    )

    grad_far = swap(grad_pre, far)
    parts = weight_parts(feats + aggs, hbm(grad_pre), n_dom)
    part_sums = lax.all_to_all(parts, "dom", 0, 0, tiled=True)
    grads = [hbm(grad_pre), swap(grad_pre, near), grad_far, swap(grad_far, near)]

    back_out, back_agg, direct = back_far(
        lists, edge_tiles, grads, w_rows, n_dom, hub_dev, tile_size
    )
    back_in = lax.all_to_all(back_out, "dom", 0, 0, tiled=True)
    own = back_own(lists, edge_tiles, back_agg, direct).reshape(own_count, width)
    weights_out, grad_bias = sum_parts(part_sums)
    weights_out, back_in, own = lax.optimization_barrier((weights_out, back_in, own))
    weights_in = lax.all_to_all(weights_out, "dom", 0, 0, tiled=True)
    grad_feats = finish(listed, send_count, hub_ids, back_in, own)
    grad_self, grad_neigh = place_weights(me_s, weights_in.reshape(-1, width))
    return (output, grad_feats, grad_self, grad_neigh, grad_bias[0])


def solution(mesh):
    in_specs = (
        P("dom", "feat"),
        P("dom", None, None),
        P("dom"),
        P("dom"),
        P("dom"),
        P("dom", None, None),
        P("dom", None),
        P(None, "feat"),
        P(None, "feat"),
        P("feat"),
        P("dom", "feat"),
    )
    out_specs = (P("dom", "feat"), P("dom", "feat"), P(None, "feat"), P(None, "feat"), P("feat"))
    n_feat = mesh.shape["feat"]

    def run(*args):
        return body(*args, n_feat=n_feat)

    return jax.shard_map(run, mesh=mesh, in_specs=in_specs, out_specs=out_specs, check_vma=False)
```

```python
import functools

import jax
import jax.numpy as jnp
from jax import lax
from jax.experimental import pallas as pl
from jax.experimental.pallas import tpu as pltpu
from jax.sharding import PartitionSpec as P

F32 = jnp.float32
BF16 = jnp.bfloat16
VMEM = pl.BlockSpec(memory_space=pltpu.VMEM)
SMEM = pl.BlockSpec(memory_space=pltpu.SMEM)
HBM = pl.BlockSpec(memory_space=pltpu.HBM)
ANY = pl.BlockSpec(memory_space=pl.ANY)
UNROLL = 16
T_BITS, S_BITS = 10, 10


def params(mib=24):
    return pltpu.CompilerParams(vmem_limit_bytes=mib << 20)


def hbm(x):
    return pltpu.with_memory_space_constraint(x, pltpu.HBM)


def cost(flops, nbytes):
    return pl.CostEstimate(flops=flops, bytes_accessed=nbytes, transcendentals=0)


def start_copies(sems, *pairs):
    copies = [pltpu.make_async_copy(a, b, sems.at[i]) for i, (a, b) in enumerate(pairs)]
    for copy in copies:
        copy.start()
    return copies


def wait_copies(copies):
    for copy in copies:
        copy.wait()


def pick_kernel(rows_h, count_h, hub_h, x_h, out_h, rows_s, count_s, hub_s, x, x32, stage, out, sems, out_sems):
    copies = start_copies(sems, (x_h, x), (rows_h, rows_s), (count_h, count_s), (hub_h, hub_s))
    n_dom, capacity = rows_s.shape
    hub_dev = hub_s.shape[0]
    step = 32
    wait_copies(copies)
    x32[...] = x[...].astype(F32)
    for j in range(hub_dev):
        stage[capacity + j : capacity + j + 1, :] = x32[pl.ds(hub_s[j], 1), :]
    hub = stage[capacity:, :].astype(BF16)
    slot = lax.broadcasted_iota(jnp.int32, (capacity, x.shape[1]), 0)

    def peer(q, carry):
        def some(g, carry):
            for u in range(step):
                c = g * step + u
                stage[pl.ds(c, 1), :] = x32[pl.ds(rows_s[q, c], 1), :]
            return carry

        lax.fori_loop(0, capacity // step, some, 0)
        kept = jnp.where(slot < count_s[0, q], stage[:capacity, :], 0.0)
        out[q, :capacity, :] = kept.astype(BF16)
        out[q, capacity:, :] = hub
        pltpu.make_async_copy(out.at[q], out_h.at[q], out_sems.at[q]).start()
        return carry

    lax.fori_loop(0, n_dom, peer, 0)
    for q in range(n_dom):
        pltpu.make_async_copy(out.at[q], out_h.at[q], out_sems.at[q]).wait()


def pick(send_rows, send_count, hub_ids, x):
    n_dom, capacity = send_rows.shape
    rows = capacity + hub_ids.shape[0]
    shape = (n_dom, rows, x.shape[1])
    return pl.pallas_call(
        pick_kernel,
        out_shape=pltpu.HBM(shape, BF16),
        in_specs=[HBM] * 4,
        out_specs=HBM,
        scratch_shapes=[
            pltpu.SMEM(send_rows.shape, jnp.int32),
            pltpu.SMEM(send_count.shape, jnp.int32),
            pltpu.SMEM(hub_ids.shape, jnp.int32),
            pltpu.VMEM(x.shape, BF16),
            pltpu.VMEM(x.shape, F32),
            pltpu.VMEM((rows, x.shape[1]), F32),
            pltpu.VMEM(shape, BF16),
            pltpu.SemaphoreType.DMA((4,)),
            pltpu.SemaphoreType.DMA((n_dom,)),
        ],
        compiler_params=params(),
        cost_estimate=cost(0, 1 << 21),
        name="pick_rows",
    )(hbm(send_rows), hbm(send_count), hbm(hub_ids), hbm(x))


def unpack(entry):
    t = entry & ((1 << T_BITS) - 1)
    s = (entry >> T_BITS) & ((1 << S_BITS) - 1)
    return t, s, entry >> (T_BITS + S_BITS)


def make_lists(dst_s, src_s, lists, own_blocks, far_blocks):
    length = lists.shape[1] - 1

    def step(t, n):
        s = src_s[t]
        d = dst_s[t]
        far = (s >= own_blocks).astype(jnp.int32)
        lists[0, n[0]] = t + (s << T_BITS) + (d << (T_BITS + S_BITS))
        lists[1, n[1]] = t + ((s - own_blocks) << T_BITS) + (d << (T_BITS + S_BITS))
        return n[0] + 1 - far, n[1] + far

    n = lax.fori_loop(0, dst_s.shape[0], step, (jnp.int32(0), jnp.int32(0)))
    for which, blocks in ((0, own_blocks), (1, far_blocks)):
        spare = (blocks << T_BITS) + (own_blocks << (T_BITS + S_BITS))
        for u in range(UNROLL - 1):
            lists[which, n[which] + u] = jnp.int32(spare)
        lists[which, length] = n[which]


def add_tiles(lists, which, tiles, source, acc, spare):
    n = lists[which, lists.shape[1] - 1]

    def group(g, carry):
        done = []
        for u in range(UNROLL):
            t, s, d = unpack(lists[which, g * UNROLL + u])
            s = jnp.where(d == spare, 0, s)
            done.append((d, jnp.dot(tiles[t], source[s], preferred_element_type=F32)))
        for d, product in done:
            acc[d] += product
        return carry

    lax.fori_loop(0, (n + UNROLL - 1) // UNROLL, group, 0)


def add_tiles_t(lists, which, tiles, source, acc, spare):
    n = lists[which, lists.shape[1] - 1]

    def group(g, carry):
        done = []
        for u in range(UNROLL):
            t, s, d = unpack(lists[which, g * UNROLL + u])
            d = jnp.where(d == spare, 0, d)
            product = lax.dot_general(
                tiles[t], source[d], (((0,), (0,)), ((), ())), preferred_element_type=F32
            )
            done.append((s, product))
        for s, product in done:
            acc[s] += product
        return carry

    lax.fori_loop(0, (n + UNROLL - 1) // UNROLL, group, 0)


def own_kernel(
    dst_h, src_h, tiles_h, x_h, out_h, lists, dst_s, src_s, x, tiles, acc, sems, *, far_blocks
):
    own_blocks = x.shape[0]
    copies = start_copies(sems, (dst_h, dst_s), (src_h, src_s), (x_h, x), (tiles_h, tiles))
    acc[...] = jnp.zeros_like(acc)
    wait_copies(copies[:2])
    make_lists(dst_s, src_s, lists, own_blocks, far_blocks)
    wait_copies(copies[2:])
    add_tiles(lists, 0, tiles, x, acc, own_blocks)
    wait_copies(start_copies(sems, (acc.at[pl.ds(0, own_blocks)], out_h)))


def own_tiles(tile_dst, tile_src, tiles, x, far_blocks):
    n = tiles.shape[0]
    return pl.pallas_call(
        functools.partial(own_kernel, far_blocks=far_blocks),
        out_shape=(
            pltpu.HBM(x.shape, F32),
            jax.ShapeDtypeStruct((2, n + UNROLL), jnp.int32),
        ),
        in_specs=[HBM, HBM, HBM, HBM],
        out_specs=(HBM, SMEM),
        scratch_shapes=[
            pltpu.SMEM((n,), jnp.int32),
            pltpu.SMEM((n,), jnp.int32),
            pltpu.VMEM(x.shape, BF16),
            pltpu.VMEM(tiles.shape, BF16),
            pltpu.VMEM((x.shape[0] + 1,) + x.shape[1:], F32),
            pltpu.SemaphoreType.DMA((4,)),
        ],
        compiler_params=params(),
        cost_estimate=cost(2 * n * 128**3, 1 << 23),
        name="own_tiles",
    )(hbm(tile_dst), hbm(tile_src), hbm(tiles), hbm(x))


def far_kernel(lists, tiles, incoming_h, base_h, out_h, source, acc, out, sems):
    n_dom, rows, _ = incoming_h.shape
    own_blocks, tile, _ = base_h.shape
    hub_dev = rows - tile
    hub_blocks = n_dom * hub_dev // tile
    pairs = [(incoming_h.at[:, pl.ds(0, tile), :], source.at[pl.ds(hub_blocks, n_dom)])]
    pairs.append((base_h, acc.at[pl.ds(0, own_blocks)]))
    for q in range(n_dom):
        block, row = divmod(q * hub_dev, tile)
        pairs.append(
            (incoming_h.at[q, pl.ds(tile, hub_dev), :], source.at[block, pl.ds(row, hub_dev), :])
        )
    wait_copies(start_copies(sems, *pairs))
    add_tiles(lists, 1, tiles, source, acc, own_blocks)
    out[...] = acc[:own_blocks].astype(BF16)
    wait_copies(start_copies(sems, (out, out_h)))


def far_tiles(lists, tiles, incoming, base, far_blocks):
    own_blocks, tile, width = base.shape
    return pl.pallas_call(
        far_kernel,
        out_shape=pltpu.HBM(base.shape, BF16),
        in_specs=[SMEM, VMEM, HBM, HBM],
        out_specs=HBM,
        scratch_shapes=[
            pltpu.VMEM((far_blocks, tile, width), BF16),
            pltpu.VMEM((own_blocks + 1, tile, width), F32),
            pltpu.VMEM(base.shape, BF16),
            pltpu.SemaphoreType.DMA((incoming.shape[0] + 2,)),
        ],
        compiler_params=params(),
        cost_estimate=cost(tiles.shape[0] * 128**3, 1 << 22),
        name="far_tiles",
    )(lists, tiles, hbm(incoming), hbm(base))


def by_shards(me, shards, w):
    width = shards[0].shape[1]
    rows = [
        w[pl.ds(pl.multiple_of((me ^ k) * width, width), width), :] for k in range(len(shards))
    ]
    return jnp.dot(
        jnp.concatenate([s[...] for s in shards], axis=1),
        jnp.concatenate(rows, axis=0),
        preferred_element_type=F32,
    )


def stream(step, ins_h, ins, outs_h, outs, sems, block):
    rows = ins[0].shape[0]
    n_in = len(ins)
    pending = []
    for i in range(rows // block):
        at = pl.ds(i * block, block)
        pairs = [(a.at[at], b.at[at]) for a, b in zip(ins_h, ins)]
        pending.append(start_copies(sems.at[i], *pairs))
    leaving = []
    for i in range(rows // block):
        at = pl.ds(i * block, block)
        wait_copies(pending[i])
        step(at, [r.at[at] for r in ins], [r.at[at] for r in outs])
        pairs = [(a.at[at], b.at[at]) for a, b in zip(outs, outs_h)]
        leaving.append(start_copies(sems.at[i, pl.ds(n_in, len(outs))], *pairs))
    for copies in leaving:
        wait_copies(copies)


def stream_call(kernel, me, streamed, whole, outs, flops, name, block=1024):
    rows = streamed[0].shape[0]
    n_in, n_whole, n_out = len(streamed), len(whole), len(outs)

    def run(me_s, *refs):
        ins_h, refs = refs[:n_in], refs[n_in:]
        held, refs = refs[:n_whole], refs[n_whole:]
        outs_h, refs = refs[:n_out], refs[n_out:]
        ins, refs = refs[:n_in], refs[n_in:]
        out, sems = refs[:n_out], refs[n_out]
        stream(
            lambda at, i, o: kernel(me_s[0], i, held, o), ins_h, ins, outs_h, out, sems, block
        )

    return pl.pallas_call(
        run,
        out_shape=tuple(pltpu.HBM(shape, t) for shape, t in outs),
        in_specs=[SMEM] + [ANY] * n_in + [VMEM] * n_whole,
        out_specs=(HBM,) * n_out,
        scratch_shapes=[pltpu.VMEM(x.shape, x.dtype) for x in streamed]
        + [pltpu.VMEM(shape, t) for shape, t in outs]
        + [pltpu.SemaphoreType.DMA((rows // block, n_in + n_out))],
        compiler_params=params(),
        cost_estimate=cost(flops, 1 << 22),
        name=name,
    )(me, *streamed, *[hbm(x) for x in whole])


def self_step(me, ins, held, outs):
    w, bias = held
    outs[0][...] = by_shards(me, ins, w) + bias[...]


def forward_step(me, ins, held, outs):
    *shards, own_part, grad_out = ins
    output, grad_pre = outs
    pre_act = own_part[...] + by_shards(me, shards, held[0])
    gate = jax.nn.sigmoid(pre_act)
    output[...] = (pre_act * gate).astype(BF16)
    grad = grad_out[...].astype(F32) * gate * (1.0 + pre_act * (1.0 - gate))
    grad_pre[...] = grad.astype(BF16)


def weights_kernel(*refs, n_feat):
    n = 2 * n_feat
    shards_h, grad_h, out_h, refs = refs[:n], refs[n], refs[n + 1], refs[n + 2 :]
    shards, (grad, out, sems, in_sems) = refs[:n], refs[n:]
    first = start_copies(sems, (grad_h, grad))
    pending = start_copies(in_sems, *zip(shards_h, shards))
    n_dom, chunk = out.shape[0], out.shape[1] - 8
    width = grad.shape[1]
    wait_copies(first)
    flipped = grad[...].T
    bias = jnp.sum(grad[...].astype(F32), axis=0, keepdims=True)
    for i, shard in enumerate(shards):
        pending[i].wait()
        block = jnp.dot(flipped, shard[...], preferred_element_type=F32).T
        for row in range(0, width, min(chunk, width)):
            q, start = divmod(i * width + row, chunk)
            n = min(chunk, width)
            out[q, start : start + n, :] = block[row : row + n, :]
    for q in range(n_dom):
        out[q, chunk:, :] = jnp.broadcast_to(bias, (8, width))
    wait_copies(start_copies(sems, (out, out_h)))


def weight_parts(shards, grad, n_dom):
    n_feat = len(shards) // 2
    width = grad.shape[1]
    chunk = 2 * n_feat * width // n_dom
    return pl.pallas_call(
        functools.partial(weights_kernel, n_feat=n_feat),
        out_shape=pltpu.HBM((n_dom, chunk + 8, width), F32),
        in_specs=[ANY] * (2 * n_feat + 1),
        out_specs=HBM,
        scratch_shapes=[pltpu.VMEM(grad.shape, BF16)] * (2 * n_feat + 1)
        + [
            pltpu.VMEM((n_dom, chunk + 8, width), F32),
            pltpu.SemaphoreType.DMA((1,)),
            pltpu.SemaphoreType.DMA((2 * n_feat,)),
        ],
        compiler_params=params(),
        cost_estimate=cost(4 * n_feat * width * width * grad.shape[0], 1 << 22),
        name="weight_parts",
    )(*shards, grad)


def split_copies(sems, pairs, block):
    rows = pairs[0][0].shape[0]
    return [
        start_copies(
            sems.at[i], *[(a.at[pl.ds(i * block, block)], b.at[pl.ds(i * block, block)]) for a, b in pairs]
        )
        for i in range(rows // block)
    ]


def back_far_kernel(*refs, n_feat):
    lists, tiles = refs[:2]
    grads_h, w = refs[2 : 2 + n_feat], refs[2 + n_feat : 2 + 2 * n_feat]
    out_h, back_h, direct_h = refs[2 + 2 * n_feat : 5 + 2 * n_feat]
    grads = refs[5 + 2 * n_feat : 5 + 3 * n_feat]
    back, direct, acc, out, sems, out_sems = refs[5 + 3 * n_feat :]
    n_dom = out.shape[0]
    own_blocks, tile, width = back.shape
    hub_dev = out.shape[1] - tile
    hub_blocks = n_dom * hub_dev // tile
    block = 4 * tile
    pending = split_copies(sems, list(zip(grads_h, grads)), block)
    acc[...] = jnp.zeros_like(acc)
    own_w, near_w, far_w, both_w = w
    rows = [r.reshape(2 * width, -1) for r in (own_w[...], near_w[...], far_w[0], both_w[1])]
    rows = jnp.concatenate(rows, axis=1)
    for i, copies in enumerate(pending):
        wait_copies(copies)
        whole = jnp.concatenate([g[i * block : (i + 1) * block, :] for g in grads], axis=1)
        both = lax.dot_general(whole, rows, (((1,), (1,)), ((), ())), preferred_element_type=F32)
        direct[4 * i : 4 * (i + 1)] = both[:, :width].reshape(4, tile, width)
        back[4 * i : 4 * (i + 1)] = both[:, width:].astype(BF16).reshape(4, tile, width)
    leaving = start_copies(out_sems, (direct, direct_h), (back, back_h))
    add_tiles_t(lists, 1, tiles, back, acc, own_blocks)
    for q in range(n_dom):
        out[q, :tile, :] = acc[hub_blocks + q].astype(BF16)
        at, row = divmod(q * hub_dev, tile)
        out[q, tile:, :] = acc[at, row : row + hub_dev, :].astype(BF16)
    leaving += start_copies(out_sems.at[pl.ds(2, 1)], (out, out_h))
    wait_copies(leaving)


def back_far(lists, tiles, grads, w, n_dom, hub_dev, tile):
    n_feat = len(grads)
    rows, width = grads[0].shape
    far_blocks = n_dom * hub_dev // tile + n_dom
    shape = (n_dom, tile + hub_dev, width)
    back_shape = (rows // tile, tile, width)
    return pl.pallas_call(
        functools.partial(back_far_kernel, n_feat=n_feat),
        out_shape=(pltpu.HBM(shape, BF16), pltpu.HBM(back_shape, BF16), pltpu.HBM(back_shape, F32)),
        in_specs=[SMEM, VMEM] + [ANY] * n_feat + [VMEM] * n_feat,
        out_specs=(HBM, HBM, HBM),
        scratch_shapes=[pltpu.VMEM((rows, width), BF16)] * n_feat
        + [
            pltpu.VMEM(back_shape, BF16),
            pltpu.VMEM(back_shape, F32),
            pltpu.VMEM((far_blocks + 1, tile, width), F32),
            pltpu.VMEM(shape, BF16),
            pltpu.SemaphoreType.DMA((rows // (4 * tile), n_feat)),
            pltpu.SemaphoreType.DMA((3,)),
        ],
        compiler_params=params(),
        cost_estimate=cost(4 * rows * width * width * n_feat, 1 << 22),
        name="back_far",
    )(lists, tiles, *grads, *[hbm(r) for r in w])


def back_own_kernel(lists, tiles, back_h, direct_h, out_h, back, acc, sems):
    own_blocks = back.shape[0]
    own = acc.at[pl.ds(0, own_blocks)]
    wait_copies(start_copies(sems, (back_h, back), (direct_h, own)))
    add_tiles_t(lists, 0, tiles, back, acc, own_blocks)
    wait_copies(start_copies(sems, (own, out_h)))


def back_own(lists, tiles, back, direct):
    return pl.pallas_call(
        back_own_kernel,
        out_shape=pltpu.HBM(direct.shape, F32),
        in_specs=[SMEM, VMEM, HBM, HBM],
        out_specs=HBM,
        scratch_shapes=[
            pltpu.VMEM(back.shape, BF16),
            pltpu.VMEM((direct.shape[0] + 1,) + direct.shape[1:], F32),
            pltpu.SemaphoreType.DMA((2,)),
        ],
        compiler_params=params(),
        cost_estimate=cost(2 * tiles.shape[0] * 128**3, 1 << 23),
        name="back_own",
    )(lists, tiles, hbm(back), hbm(direct))


def finish_kernel(rows_s, count_h, hub_h, incoming_h, base_h, out_h, count_s, hub_s, sent, hubs, base, sems, out_sems):
    n_dom, capacity = rows_s.shape
    hub_dev = hub_s.shape[0]
    own_count, width = base.shape
    block, peers = 256, min(8, n_dom)
    copies = start_copies(
        sems,
        (count_h, count_s),
        (hub_h, hub_s),
        (incoming_h.at[:, pl.ds(0, capacity), :], sent),
        (incoming_h.at[:, pl.ds(capacity, hub_dev), :], hubs),
        (base_h, base),
    )
    wait_copies(copies)
    hub = hubs[0].astype(F32)
    for q in range(1, n_dom):
        hub += hubs[q].astype(F32)
    for j in range(hub_dev):
        base[pl.ds(hub_s[j], 1), :] += hub[j : j + 1, :]
    lane = lax.broadcasted_iota(jnp.int32, (1, capacity), 1)
    leaving = []
    for start in range(0, own_count, block):
        vertex = lax.broadcasted_iota(jnp.int32, (block, capacity), 0) + start
        total = base[start : start + block, :]
        for first in range(0, n_dom, peers):
            hot, rows = [], []
            for q in range(first, first + peers):
                wanted = jnp.where(lane < count_s[0, q], rows_s[q : q + 1, :], -1)
                hot.append((vertex == wanted).astype(F32).astype(BF16))
                rows.append(sent[q])
            total += jnp.dot(
                jnp.concatenate(hot, axis=1),
                jnp.concatenate(rows, axis=0),
                preferred_element_type=F32,
            )
        base[start : start + block, :] = total
        at = pl.ds(start, block)
        leaving.append(start_copies(out_sems.at[pl.ds(start // block, 1)], (base.at[at], out_h.at[at])))
    for copies in leaving:
        wait_copies(copies)


def finish(send_rows, send_count, hub_ids, incoming, base):
    n_dom, capacity = send_rows.shape
    hub_dev = hub_ids.shape[0]
    own_count, width = base.shape
    return pl.pallas_call(
        finish_kernel,
        out_shape=pltpu.HBM(base.shape, F32),
        in_specs=[VMEM, HBM, HBM, ANY, HBM],
        out_specs=HBM,
        scratch_shapes=[
            pltpu.SMEM(send_count.shape, jnp.int32),
            pltpu.SMEM(hub_ids.shape, jnp.int32),
            pltpu.VMEM((n_dom, capacity, width), BF16),
            pltpu.VMEM((n_dom, hub_dev, width), BF16),
            pltpu.VMEM(base.shape, F32),
            pltpu.SemaphoreType.DMA((5,)),
            pltpu.SemaphoreType.DMA((own_count // 256,)),
        ],
        compiler_params=params(),
        cost_estimate=cost(2 * base.size * send_rows.size, 1 << 22),
        name="finish",
    )(hbm(send_rows), hbm(send_count), hbm(hub_ids), incoming, hbm(base))


def cut_kernel(me_s, w_self, w_neigh, *outs):
    width = w_self.shape[1]
    own, near, far = outs
    for k, out in enumerate((own, near, far.at[0], far.at[1])):
        at = pl.ds(pl.multiple_of((me_s[0] ^ k) * width, width), width)
        out[0] = w_self[at, :]
        out[1] = w_neigh[at, :]


def cut_weights(me, w_self, w_neigh):
    width = w_self.shape[1]
    one = (2, width, width)
    return pl.pallas_call(
        cut_kernel,
        out_shape=tuple(pltpu.HBM(shape, BF16) for shape in (one, one, (2,) + one)),
        in_specs=[SMEM, VMEM, VMEM],
        out_specs=(VMEM,) * 3,
        compiler_params=params(),
        cost_estimate=cost(0, 1 << 20),
        name="cut_weights",
    )(me, hbm(w_self), hbm(w_neigh))


def sum_kernel(parts, out, bias):
    n_dom, chunk, _ = out.shape
    total = parts[0]
    for q in range(1, n_dom):
        total += parts[q]
    bias[...] = total[chunk : chunk + 1, :]
    rows = total[:chunk, :].astype(BF16)
    for q in range(n_dom):
        out[q] = rows


def sum_parts(parts):
    n_dom, rows, width = parts.shape
    return pl.pallas_call(
        sum_kernel,
        out_shape=(pltpu.HBM((n_dom, rows - 8, width), BF16), pltpu.HBM((1, width), F32)),
        in_specs=[VMEM],
        out_specs=(VMEM, VMEM),
        compiler_params=params(),
        cost_estimate=cost(0, 1 << 20),
        name="sum_parts",
    )(hbm(parts))


def place_kernel(me_s, sums, self_out, neigh_out):
    rows, width = self_out.shape
    for i in range(2 * rows // width):
        which, k = divmod(i, rows // width)
        target = (self_out, neigh_out)[which]
        at = pl.ds(pl.multiple_of((me_s[0] ^ k) * width, width), width)
        target[at, :] = sums[i * width : (i + 1) * width, :].astype(F32)


def place_weights(me, sums):
    rows, width = sums.shape[0] // 2, sums.shape[1]
    return pl.pallas_call(
        place_kernel,
        out_shape=(pltpu.HBM((rows, width), F32),) * 2,
        in_specs=[SMEM, VMEM],
        out_specs=(VMEM, VMEM),
        compiler_params=params(),
        cost_estimate=cost(0, 1 << 20),
        name="place_weights",
    )(me, sums)


def body(
    node_feats,
    edge_tiles,
    tile_dst,
    tile_src,
    hub_ids,
    send_rows,
    send_count,
    w_self,
    w_neigh,
    out_bias,
    grad_out,
    *,
    n_feat,
):
    own_count, width = node_feats.shape
    tile_size = edge_tiles.shape[1]
    listed = send_rows[0]
    n_dom, capacity = listed.shape
    hub_dev = hub_ids.shape[0]
    me = lax.axis_index("feat").astype(jnp.int32)
    me_s = me.reshape(1)
    far, near = 2, 1
    assert n_feat == 4
    far_blocks = n_dom * hub_dev // tile_size + n_dom

    def swap(x, k):
        return lax.ppermute(x, "feat", [(j, j ^ k) for j in range(n_feat)])

    feat_far = swap(node_feats, far)

    outgoing = pick(listed, send_count, hub_ids, node_feats)
    incoming = lax.all_to_all(outgoing, "dom", 0, 0, tiled=True)
    cut = cut_weights(me_s, w_self, w_neigh)
    own_feats, *cut = lax.optimization_barrier((node_feats.reshape(-1, tile_size, width), *cut))
    far_w = swap(cut[2], far)
    base, lists = own_tiles(tile_dst, tile_src, edge_tiles, own_feats, far_blocks)
    aggregated = far_tiles(lists, edge_tiles, incoming, base, far_blocks).reshape(own_count, width)

    aggregated, far_w = lax.optimization_barrier((aggregated, far_w))
    w_rows = [cut[0], swap(cut[1], near), far_w, swap(far_w, near)]
    agg_far = swap(aggregated, far)
    feat_far, aggregated = lax.optimization_barrier((feat_far, aggregated))
    feats = [hbm(node_feats), swap(node_feats, near), feat_far, swap(feat_far, near)]
    flops = 2 * own_count * n_feat * width * width
    rows_out = ((own_count, width), BF16)
    (own_part,) = stream_call(
        self_step,
        me_s,
        feats,
        [w_self, out_bias[None, :]],
        [((own_count, width), F32)],
        flops,
        "self_dense",
    )
    agg_far, own_part, *w_rows = lax.optimization_barrier((agg_far, own_part, *w_rows))
    aggs = [hbm(aggregated), swap(aggregated, near), agg_far, swap(agg_far, near)]
    output, grad_pre = stream_call(
        forward_step,
        me_s,
        [*aggs, hbm(own_part), hbm(grad_out)],
        [w_neigh],
        [rows_out, rows_out],
        flops,
        "forward_dense",
    )

    grad_far = swap(grad_pre, far)
    parts = weight_parts(feats + aggs, hbm(grad_pre), n_dom)
    part_sums = lax.all_to_all(parts, "dom", 0, 0, tiled=True)
    grads = [hbm(grad_pre), swap(grad_pre, near), grad_far, swap(grad_far, near)]

    back_out, back_agg, direct = back_far(
        lists, edge_tiles, grads, w_rows, n_dom, hub_dev, tile_size
    )
    back_in = lax.all_to_all(back_out, "dom", 0, 0, tiled=True)
    own = back_own(lists, edge_tiles, back_agg, direct).reshape(own_count, width)
    weights_out, grad_bias = sum_parts(part_sums)
    weights_out, back_in, own = lax.optimization_barrier((weights_out, back_in, own))
    weights_in = lax.all_to_all(weights_out, "dom", 0, 0, tiled=True)
    grad_feats = finish(listed, send_count, hub_ids, back_in, own)
    grad_self, grad_neigh = place_weights(me_s, weights_in.reshape(-1, width))
    return (output, grad_feats, grad_self, grad_neigh, grad_bias[0])


def solution(mesh):
    in_specs = (
        P("dom", "feat"),
        P("dom", None, None),
        P("dom"),
        P("dom"),
        P("dom"),
        P("dom", None, None),
        P("dom", None),
        P(None, "feat"),
        P(None, "feat"),
        P("feat"),
        P("dom", "feat"),
    )
    out_specs = (P("dom", "feat"), P("dom", "feat"), P(None, "feat"), P(None, "feat"), P("feat"))
    n_feat = mesh.shape["feat"]

    def run(*args):
        return body(*args, n_feat=n_feat)

    return jax.shard_map(run, mesh=mesh, in_specs=in_specs, out_specs=out_specs, check_vma=False)
```

```python
import functools

import jax
import jax.numpy as jnp
from jax import lax
from jax.experimental import pallas as pl
from jax.experimental.pallas import tpu as pltpu
from jax.sharding import PartitionSpec as P

F32 = jnp.float32
BF16 = jnp.bfloat16
VMEM = pl.BlockSpec(memory_space=pltpu.VMEM)
SMEM = pl.BlockSpec(memory_space=pltpu.SMEM)
HBM = pl.BlockSpec(memory_space=pltpu.HBM)
ANY = pl.BlockSpec(memory_space=pl.ANY)
UNROLL = 16
T_BITS, S_BITS = 10, 10


def params(mib=24):
    return pltpu.CompilerParams(vmem_limit_bytes=mib << 20)


def hbm(x):
    return pltpu.with_memory_space_constraint(x, pltpu.HBM)


def cost(flops, nbytes):
    return pl.CostEstimate(flops=flops, bytes_accessed=nbytes, transcendentals=0)


def start_copies(sems, *pairs):
    copies = [pltpu.make_async_copy(a, b, sems.at[i]) for i, (a, b) in enumerate(pairs)]
    for copy in copies:
        copy.start()
    return copies


def wait_copies(copies):
    for copy in copies:
        copy.wait()


def pick_kernel(rows_h, count_h, hub_h, x_h, out_h, rows_s, count_s, hub_s, x, x32, stage, out, sems, out_sems):
    copies = start_copies(sems, (x_h, x), (rows_h, rows_s), (count_h, count_s), (hub_h, hub_s))
    n_dom, capacity = rows_s.shape
    hub_dev = hub_s.shape[0]
    step = 64
    wait_copies(copies)
    x32[...] = x[...].astype(F32)
    for j in range(hub_dev):
        stage[capacity + j : capacity + j + 1, :] = x32[pl.ds(hub_s[j], 1), :]
    hub = stage[capacity:, :].astype(BF16)
    slot = lax.broadcasted_iota(jnp.int32, (capacity, x.shape[1]), 0)

    def peer(q, carry):
        def some(g, carry):
            for u in range(step):
                c = g * step + u
                stage[pl.ds(c, 1), :] = x32[pl.ds(rows_s[q, c], 1), :]
            return carry

        lax.fori_loop(0, capacity // step, some, 0)
        kept = jnp.where(slot < count_s[0, q], stage[:capacity, :], 0.0)
        out[q, :capacity, :] = kept.astype(BF16)
        out[q, capacity:, :] = hub
        pltpu.make_async_copy(out.at[q], out_h.at[q], out_sems.at[q]).start()
        return carry

    lax.fori_loop(0, n_dom, peer, 0)
    for q in range(n_dom):
        pltpu.make_async_copy(out.at[q], out_h.at[q], out_sems.at[q]).wait()


def pick(send_rows, send_count, hub_ids, x):
    n_dom, capacity = send_rows.shape
    rows = capacity + hub_ids.shape[0]
    shape = (n_dom, rows, x.shape[1])
    return pl.pallas_call(
        pick_kernel,
        out_shape=pltpu.HBM(shape, BF16),
        in_specs=[HBM] * 4,
        out_specs=HBM,
        scratch_shapes=[
            pltpu.SMEM(send_rows.shape, jnp.int32),
            pltpu.SMEM(send_count.shape, jnp.int32),
            pltpu.SMEM(hub_ids.shape, jnp.int32),
            pltpu.VMEM(x.shape, BF16),
            pltpu.VMEM(x.shape, F32),
            pltpu.VMEM((rows, x.shape[1]), F32),
            pltpu.VMEM(shape, BF16),
            pltpu.SemaphoreType.DMA((4,)),
            pltpu.SemaphoreType.DMA((n_dom,)),
        ],
        compiler_params=params(),
        cost_estimate=cost(0, 1 << 21),
        name="pick_rows",
    )(hbm(send_rows), hbm(send_count), hbm(hub_ids), hbm(x))


def unpack(entry):
    t = entry & ((1 << T_BITS) - 1)
    s = (entry >> T_BITS) & ((1 << S_BITS) - 1)
    return t, s, entry >> (T_BITS + S_BITS)


def make_lists(dst_s, src_s, lists, own_blocks, far_blocks):
    length = lists.shape[1] - 1

    def step(t, n):
        s = src_s[t]
        d = dst_s[t]
        far = (s >= own_blocks).astype(jnp.int32)
        lists[0, n[0]] = t + (s << T_BITS) + (d << (T_BITS + S_BITS))
        lists[1, n[1]] = t + ((s - own_blocks) << T_BITS) + (d << (T_BITS + S_BITS))
        return n[0] + 1 - far, n[1] + far

    n = lax.fori_loop(0, dst_s.shape[0], step, (jnp.int32(0), jnp.int32(0)))
    for which, blocks in ((0, own_blocks), (1, far_blocks)):
        spare = (blocks << T_BITS) + (own_blocks << (T_BITS + S_BITS))
        for u in range(UNROLL - 1):
            lists[which, n[which] + u] = jnp.int32(spare)
        lists[which, length] = n[which]


def add_tiles(lists, which, tiles, source, acc, spare):
    n = lists[which, lists.shape[1] - 1]

    def group(g, carry):
        done = []
        for u in range(UNROLL):
            t, s, d = unpack(lists[which, g * UNROLL + u])
            s = jnp.where(d == spare, 0, s)
            done.append((d, jnp.dot(tiles[t], source[s], preferred_element_type=F32)))
        for d, product in done:
            acc[d] += product
        return carry

    lax.fori_loop(0, (n + UNROLL - 1) // UNROLL, group, 0)


def add_tiles_t(lists, which, tiles, source, acc, spare):
    n = lists[which, lists.shape[1] - 1]

    def group(g, carry):
        done = []
        for u in range(UNROLL):
            t, s, d = unpack(lists[which, g * UNROLL + u])
            d = jnp.where(d == spare, 0, d)
            product = lax.dot_general(
                tiles[t], source[d], (((0,), (0,)), ((), ())), preferred_element_type=F32
            )
            done.append((s, product))
        for s, product in done:
            acc[s] += product
        return carry

    lax.fori_loop(0, (n + UNROLL - 1) // UNROLL, group, 0)


def own_kernel(
    dst_h, src_h, tiles_h, x_h, out_h, lists, dst_s, src_s, x, tiles, acc, sems, *, far_blocks
):
    own_blocks = x.shape[0]
    copies = start_copies(sems, (dst_h, dst_s), (src_h, src_s), (x_h, x), (tiles_h, tiles))
    acc[...] = jnp.zeros_like(acc)
    wait_copies(copies[:2])
    make_lists(dst_s, src_s, lists, own_blocks, far_blocks)
    wait_copies(copies[2:])
    add_tiles(lists, 0, tiles, x, acc, own_blocks)
    wait_copies(start_copies(sems, (acc.at[pl.ds(0, own_blocks)], out_h)))


def own_tiles(tile_dst, tile_src, tiles, x, far_blocks):
    n = tiles.shape[0]
    return pl.pallas_call(
        functools.partial(own_kernel, far_blocks=far_blocks),
        out_shape=(
            pltpu.HBM(x.shape, F32),
            jax.ShapeDtypeStruct((2, n + UNROLL), jnp.int32),
        ),
        in_specs=[HBM, HBM, HBM, HBM],
        out_specs=(HBM, SMEM),
        scratch_shapes=[
            pltpu.SMEM((n,), jnp.int32),
            pltpu.SMEM((n,), jnp.int32),
            pltpu.VMEM(x.shape, BF16),
            pltpu.VMEM(tiles.shape, BF16),
            pltpu.VMEM((x.shape[0] + 1,) + x.shape[1:], F32),
            pltpu.SemaphoreType.DMA((4,)),
        ],
        compiler_params=params(),
        cost_estimate=cost(2 * n * 128**3, 1 << 23),
        name="own_tiles",
    )(hbm(tile_dst), hbm(tile_src), hbm(tiles), hbm(x))


def far_kernel(lists, tiles, incoming_h, base_h, out_h, source, acc, out, sems):
    n_dom, rows, _ = incoming_h.shape
    own_blocks, tile, _ = base_h.shape
    hub_dev = rows - tile
    hub_blocks = n_dom * hub_dev // tile
    pairs = [(incoming_h.at[:, pl.ds(0, tile), :], source.at[pl.ds(hub_blocks, n_dom)])]
    pairs.append((base_h, acc.at[pl.ds(0, own_blocks)]))
    for q in range(n_dom):
        block, row = divmod(q * hub_dev, tile)
        pairs.append(
            (incoming_h.at[q, pl.ds(tile, hub_dev), :], source.at[block, pl.ds(row, hub_dev), :])
        )
    wait_copies(start_copies(sems, *pairs))
    add_tiles(lists, 1, tiles, source, acc, own_blocks)
    out[...] = acc[:own_blocks].astype(BF16)
    wait_copies(start_copies(sems, (out, out_h)))


def far_tiles(lists, tiles, incoming, base, far_blocks):
    own_blocks, tile, width = base.shape
    return pl.pallas_call(
        far_kernel,
        out_shape=pltpu.HBM(base.shape, BF16),
        in_specs=[SMEM, VMEM, HBM, HBM],
        out_specs=HBM,
        scratch_shapes=[
            pltpu.VMEM((far_blocks, tile, width), BF16),
            pltpu.VMEM((own_blocks + 1, tile, width), F32),
            pltpu.VMEM(base.shape, BF16),
            pltpu.SemaphoreType.DMA((incoming.shape[0] + 2,)),
        ],
        compiler_params=params(),
        cost_estimate=cost(tiles.shape[0] * 128**3, 1 << 22),
        name="far_tiles",
    )(lists, tiles, hbm(incoming), hbm(base))


def by_shards(me, shards, w):
    width = shards[0].shape[1]
    rows = [
        w[pl.ds(pl.multiple_of((me ^ k) * width, width), width), :] for k in range(len(shards))
    ]
    return jnp.dot(
        jnp.concatenate([s[...] for s in shards], axis=1),
        jnp.concatenate(rows, axis=0),
        preferred_element_type=F32,
    )


def stream(step, ins_h, ins, outs_h, outs, sems, block):
    rows = ins[0].shape[0]
    n_in = len(ins)
    pending = []
    for i in range(rows // block):
        at = pl.ds(i * block, block)
        pairs = [(a.at[at], b.at[at]) for a, b in zip(ins_h, ins)]
        pending.append(start_copies(sems.at[i], *pairs))
    leaving = []
    for i in range(rows // block):
        at = pl.ds(i * block, block)
        wait_copies(pending[i])
        step(at, [r.at[at] for r in ins], [r.at[at] for r in outs])
        pairs = [(a.at[at], b.at[at]) for a, b in zip(outs, outs_h)]
        leaving.append(start_copies(sems.at[i, pl.ds(n_in, len(outs))], *pairs))
    for copies in leaving:
        wait_copies(copies)


def stream_call(kernel, me, streamed, whole, outs, flops, name, block=2048):
    rows = streamed[0].shape[0]
    n_in, n_whole, n_out = len(streamed), len(whole), len(outs)

    def run(me_s, *refs):
        ins_h, refs = refs[:n_in], refs[n_in:]
        held, refs = refs[:n_whole], refs[n_whole:]
        outs_h, refs = refs[:n_out], refs[n_out:]
        ins, refs = refs[:n_in], refs[n_in:]
        out, sems = refs[:n_out], refs[n_out]
        stream(
            lambda at, i, o: kernel(me_s[0], i, held, o), ins_h, ins, outs_h, out, sems, block
        )

    return pl.pallas_call(
        run,
        out_shape=tuple(pltpu.HBM(shape, t) for shape, t in outs),
        in_specs=[SMEM] + [ANY] * n_in + [VMEM] * n_whole,
        out_specs=(HBM,) * n_out,
        scratch_shapes=[pltpu.VMEM(x.shape, x.dtype) for x in streamed]
        + [pltpu.VMEM(shape, t) for shape, t in outs]
        + [pltpu.SemaphoreType.DMA((rows // block, n_in + n_out))],
        compiler_params=params(),
        cost_estimate=cost(flops, 1 << 22),
        name=name,
    )(me, *streamed, *[hbm(x) for x in whole])


def self_step(me, ins, held, outs):
    w, bias = held
    outs[0][...] = by_shards(me, ins, w) + bias[...]


def forward_step(me, ins, held, outs):
    *shards, own_part, grad_out = ins
    output, grad_pre = outs
    pre_act = own_part[...] + by_shards(me, shards, held[0])
    gate = jax.nn.sigmoid(pre_act)
    output[...] = (pre_act * gate).astype(BF16)
    grad = grad_out[...].astype(F32) * gate * (1.0 + pre_act * (1.0 - gate))
    grad_pre[...] = grad.astype(BF16)


def weights_kernel(*refs, n_feat):
    shards, grad, out_h, out, sems = refs[: 2 * n_feat], *refs[2 * n_feat :]
    n_dom, chunk = out.shape[0], out.shape[1] - 8
    width = grad.shape[1]
    flipped = grad[...].T
    bias = jnp.sum(grad[...].astype(F32), axis=0, keepdims=True)
    for i, shard in enumerate(shards):
        block = jnp.dot(flipped, shard[...], preferred_element_type=F32).T
        for row in range(0, width, min(chunk, width)):
            q, start = divmod(i * width + row, chunk)
            n = min(chunk, width)
            out[q, start : start + n, :] = block[row : row + n, :]
    for q in range(n_dom):
        out[q, chunk:, :] = jnp.broadcast_to(bias, (8, width))
    wait_copies(start_copies(sems, (out, out_h)))


def weight_parts(shards, grad, n_dom):
    n_feat = len(shards) // 2
    width = grad.shape[1]
    chunk = 2 * n_feat * width // n_dom
    return pl.pallas_call(
        functools.partial(weights_kernel, n_feat=n_feat),
        out_shape=pltpu.HBM((n_dom, chunk + 8, width), F32),
        in_specs=[VMEM] * (2 * n_feat + 1),
        out_specs=HBM,
        scratch_shapes=[
            pltpu.VMEM((n_dom, chunk + 8, width), F32),
            pltpu.SemaphoreType.DMA((1,)),
        ],
        compiler_params=params(),
        cost_estimate=cost(4 * n_feat * width * width * grad.shape[0], 1 << 22),
        name="weight_parts",
    )(*shards, grad)


def split_copies(sems, pairs, block):
    rows = pairs[0][0].shape[0]
    return [
        start_copies(
            sems.at[i], *[(a.at[pl.ds(i * block, block)], b.at[pl.ds(i * block, block)]) for a, b in pairs]
        )
        for i in range(rows // block)
    ]


def back_far_kernel(*refs, n_feat):
    lists, tiles = refs[:2]
    grads_h, w = refs[2 : 2 + n_feat], refs[2 + n_feat : 2 + 2 * n_feat]
    out_h, back_h, direct_h = refs[2 + 2 * n_feat : 5 + 2 * n_feat]
    grads = refs[5 + 2 * n_feat : 5 + 3 * n_feat]
    back, direct, acc, out, sems, out_sems = refs[5 + 3 * n_feat :]
    n_dom = out.shape[0]
    own_blocks, tile, width = back.shape
    hub_dev = out.shape[1] - tile
    hub_blocks = n_dom * hub_dev // tile
    block = 4 * tile
    pending = split_copies(sems, list(zip(grads_h, grads)), block)
    acc[...] = jnp.zeros_like(acc)
    own_w, near_w, far_w, both_w = w
    rows = [r.reshape(2 * width, -1) for r in (own_w[...], near_w[...], far_w[0], both_w[1])]
    rows = jnp.concatenate(rows, axis=1)
    for i, copies in enumerate(pending):
        wait_copies(copies)
        whole = jnp.concatenate([g[i * block : (i + 1) * block, :] for g in grads], axis=1)
        both = lax.dot_general(whole, rows, (((1,), (1,)), ((), ())), preferred_element_type=F32)
        direct[4 * i : 4 * (i + 1)] = both[:, :width].reshape(4, tile, width)
        back[4 * i : 4 * (i + 1)] = both[:, width:].astype(BF16).reshape(4, tile, width)
    leaving = start_copies(out_sems, (direct, direct_h), (back, back_h))
    add_tiles_t(lists, 1, tiles, back, acc, own_blocks)
    for q in range(n_dom):
        out[q, :tile, :] = acc[hub_blocks + q].astype(BF16)
        at, row = divmod(q * hub_dev, tile)
        out[q, tile:, :] = acc[at, row : row + hub_dev, :].astype(BF16)
    leaving += start_copies(out_sems.at[pl.ds(2, 1)], (out, out_h))
    wait_copies(leaving)


def back_far(lists, tiles, grads, w, n_dom, hub_dev, tile):
    n_feat = len(grads)
    rows, width = grads[0].shape
    far_blocks = n_dom * hub_dev // tile + n_dom
    shape = (n_dom, tile + hub_dev, width)
    back_shape = (rows // tile, tile, width)
    return pl.pallas_call(
        functools.partial(back_far_kernel, n_feat=n_feat),
        out_shape=(pltpu.HBM(shape, BF16), pltpu.HBM(back_shape, BF16), pltpu.HBM(back_shape, F32)),
        in_specs=[SMEM, VMEM] + [ANY] * n_feat + [VMEM] * n_feat,
        out_specs=(HBM, HBM, HBM),
        scratch_shapes=[pltpu.VMEM((rows, width), BF16)] * n_feat
        + [
            pltpu.VMEM(back_shape, BF16),
            pltpu.VMEM(back_shape, F32),
            pltpu.VMEM((far_blocks + 1, tile, width), F32),
            pltpu.VMEM(shape, BF16),
            pltpu.SemaphoreType.DMA((rows // (4 * tile), n_feat)),
            pltpu.SemaphoreType.DMA((3,)),
        ],
        compiler_params=params(),
        cost_estimate=cost(4 * rows * width * width * n_feat, 1 << 22),
        name="back_far",
    )(lists, tiles, *grads, *[hbm(r) for r in w])


def back_own_kernel(lists, tiles, back_h, direct_h, out_h, back, acc, sems):
    own_blocks = back.shape[0]
    own = acc.at[pl.ds(0, own_blocks)]
    wait_copies(start_copies(sems, (back_h, back), (direct_h, own)))
    add_tiles_t(lists, 0, tiles, back, acc, own_blocks)
    wait_copies(start_copies(sems, (own, out_h)))


def back_own(lists, tiles, back, direct):
    return pl.pallas_call(
        back_own_kernel,
        out_shape=pltpu.HBM(direct.shape, F32),
        in_specs=[SMEM, VMEM, HBM, HBM],
        out_specs=HBM,
        scratch_shapes=[
            pltpu.VMEM(back.shape, BF16),
            pltpu.VMEM((direct.shape[0] + 1,) + direct.shape[1:], F32),
            pltpu.SemaphoreType.DMA((2,)),
        ],
        compiler_params=params(),
        cost_estimate=cost(2 * tiles.shape[0] * 128**3, 1 << 23),
        name="back_own",
    )(lists, tiles, hbm(back), hbm(direct))


def finish_kernel(rows_s, count_h, hub_h, incoming_h, base_h, out_h, count_s, hub_s, sent, hubs, base, sems, out_sems):
    n_dom, capacity = rows_s.shape
    hub_dev = hub_s.shape[0]
    own_count, width = base.shape
    block, peers = 256, min(8, n_dom)
    copies = start_copies(
        sems,
        (count_h, count_s),
        (hub_h, hub_s),
        (incoming_h.at[:, pl.ds(0, capacity), :], sent),
        (incoming_h.at[:, pl.ds(capacity, hub_dev), :], hubs),
        (base_h, base),
    )
    wait_copies(copies)
    hub = hubs[0].astype(F32)
    for q in range(1, n_dom):
        hub += hubs[q].astype(F32)
    for j in range(hub_dev):
        base[pl.ds(hub_s[j], 1), :] += hub[j : j + 1, :]
    lane = lax.broadcasted_iota(jnp.int32, (1, capacity), 1)
    leaving = []
    for start in range(0, own_count, block):
        vertex = lax.broadcasted_iota(jnp.int32, (block, capacity), 0) + start
        total = base[start : start + block, :]
        for first in range(0, n_dom, peers):
            hot, rows = [], []
            for q in range(first, first + peers):
                wanted = jnp.where(lane < count_s[0, q], rows_s[q : q + 1, :], -1)
                hot.append((vertex == wanted).astype(F32).astype(BF16))
                rows.append(sent[q])
            total += jnp.dot(
                jnp.concatenate(hot, axis=1),
                jnp.concatenate(rows, axis=0),
                preferred_element_type=F32,
            )
        base[start : start + block, :] = total
        at = pl.ds(start, block)
        leaving.append(start_copies(out_sems.at[pl.ds(start // block, 1)], (base.at[at], out_h.at[at])))
    for copies in leaving:
        wait_copies(copies)


def finish(send_rows, send_count, hub_ids, incoming, base):
    n_dom, capacity = send_rows.shape
    hub_dev = hub_ids.shape[0]
    own_count, width = base.shape
    return pl.pallas_call(
        finish_kernel,
        out_shape=pltpu.HBM(base.shape, F32),
        in_specs=[VMEM, HBM, HBM, ANY, HBM],
        out_specs=HBM,
        scratch_shapes=[
            pltpu.SMEM(send_count.shape, jnp.int32),
            pltpu.SMEM(hub_ids.shape, jnp.int32),
            pltpu.VMEM((n_dom, capacity, width), BF16),
            pltpu.VMEM((n_dom, hub_dev, width), BF16),
            pltpu.VMEM(base.shape, F32),
            pltpu.SemaphoreType.DMA((5,)),
            pltpu.SemaphoreType.DMA((own_count // 256,)),
        ],
        compiler_params=params(),
        cost_estimate=cost(2 * base.size * send_rows.size, 1 << 22),
        name="finish",
    )(hbm(send_rows), hbm(send_count), hbm(hub_ids), incoming, hbm(base))


def cut_kernel(me_s, w_self, w_neigh, *outs):
    width = w_self.shape[1]
    own, near, far = outs
    for k, out in enumerate((own, near, far.at[0], far.at[1])):
        at = pl.ds(pl.multiple_of((me_s[0] ^ k) * width, width), width)
        out[0] = w_self[at, :]
        out[1] = w_neigh[at, :]


def cut_weights(me, w_self, w_neigh):
    width = w_self.shape[1]
    one = (2, width, width)
    return pl.pallas_call(
        cut_kernel,
        out_shape=tuple(pltpu.HBM(shape, BF16) for shape in (one, one, (2,) + one)),
        in_specs=[SMEM, VMEM, VMEM],
        out_specs=(VMEM,) * 3,
        compiler_params=params(),
        cost_estimate=cost(0, 1 << 20),
        name="cut_weights",
    )(me, hbm(w_self), hbm(w_neigh))


def sum_kernel(parts, out, bias):
    n_dom, chunk, _ = out.shape
    total = parts[0]
    for q in range(1, n_dom):
        total += parts[q]
    bias[...] = total[chunk : chunk + 1, :]
    rows = total[:chunk, :].astype(BF16)
    for q in range(n_dom):
        out[q] = rows


def sum_parts(parts):
    n_dom, rows, width = parts.shape
    return pl.pallas_call(
        sum_kernel,
        out_shape=(pltpu.HBM((n_dom, rows - 8, width), BF16), pltpu.HBM((1, width), F32)),
        in_specs=[VMEM],
        out_specs=(VMEM, VMEM),
        compiler_params=params(),
        cost_estimate=cost(0, 1 << 20),
        name="sum_parts",
    )(hbm(parts))


def place_kernel(me_s, sums, self_out, neigh_out):
    rows, width = self_out.shape
    for i in range(2 * rows // width):
        which, k = divmod(i, rows // width)
        target = (self_out, neigh_out)[which]
        at = pl.ds(pl.multiple_of((me_s[0] ^ k) * width, width), width)
        target[at, :] = sums[i * width : (i + 1) * width, :].astype(F32)


def place_weights(me, sums):
    rows, width = sums.shape[0] // 2, sums.shape[1]
    return pl.pallas_call(
        place_kernel,
        out_shape=(pltpu.HBM((rows, width), F32),) * 2,
        in_specs=[SMEM, VMEM],
        out_specs=(VMEM, VMEM),
        compiler_params=params(),
        cost_estimate=cost(0, 1 << 20),
        name="place_weights",
    )(me, sums)


def body(
    node_feats,
    edge_tiles,
    tile_dst,
    tile_src,
    hub_ids,
    send_rows,
    send_count,
    w_self,
    w_neigh,
    out_bias,
    grad_out,
    *,
    n_feat,
):
    own_count, width = node_feats.shape
    tile_size = edge_tiles.shape[1]
    listed = send_rows[0]
    n_dom, capacity = listed.shape
    hub_dev = hub_ids.shape[0]
    me = lax.axis_index("feat").astype(jnp.int32)
    me_s = me.reshape(1)
    far, near = 2, 1
    assert n_feat == 4
    far_blocks = n_dom * hub_dev // tile_size + n_dom

    def swap(x, k):
        return lax.ppermute(x, "feat", [(j, j ^ k) for j in range(n_feat)])

    feat_far = swap(node_feats, far)

    outgoing = pick(listed, send_count, hub_ids, node_feats)
    incoming = lax.all_to_all(outgoing, "dom", 0, 0, tiled=True)
    cut = cut_weights(me_s, w_self, w_neigh)
    own_feats, *cut = lax.optimization_barrier((node_feats.reshape(-1, tile_size, width), *cut))
    far_w = swap(cut[2], far)
    base, lists = own_tiles(tile_dst, tile_src, edge_tiles, own_feats, far_blocks)
    aggregated = far_tiles(lists, edge_tiles, incoming, base, far_blocks).reshape(own_count, width)

    aggregated, far_w = lax.optimization_barrier((aggregated, far_w))
    w_rows = [cut[0], swap(cut[1], near), far_w, swap(far_w, near)]
    agg_far = swap(aggregated, far)
    feat_far, aggregated = lax.optimization_barrier((feat_far, aggregated))
    feats = [hbm(node_feats), swap(node_feats, near), feat_far, swap(feat_far, near)]
    flops = 2 * own_count * n_feat * width * width
    rows_out = ((own_count, width), BF16)
    (own_part,) = stream_call(
        self_step,
        me_s,
        feats,
        [w_self, out_bias[None, :]],
        [((own_count, width), F32)],
        flops,
        "self_dense",
    )
    agg_far, own_part, *w_rows = lax.optimization_barrier((agg_far, own_part, *w_rows))
    aggs = [hbm(aggregated), swap(aggregated, near), agg_far, swap(agg_far, near)]
    output, grad_pre = stream_call(
        forward_step,
        me_s,
        [*aggs, hbm(own_part), hbm(grad_out)],
        [w_neigh],
        [rows_out, rows_out],
        flops,
        "forward_dense",
    )

    grad_far = swap(grad_pre, far)
    parts = weight_parts(feats + aggs, hbm(grad_pre), n_dom)
    part_sums = lax.all_to_all(parts, "dom", 0, 0, tiled=True)
    grads = [hbm(grad_pre), swap(grad_pre, near), grad_far, swap(grad_far, near)]

    back_out, back_agg, direct = back_far(
        lists, edge_tiles, grads, w_rows, n_dom, hub_dev, tile_size
    )
    back_in = lax.all_to_all(back_out, "dom", 0, 0, tiled=True)
    own = back_own(lists, edge_tiles, back_agg, direct).reshape(own_count, width)
    weights_out, grad_bias = sum_parts(part_sums)
    weights_out, back_in, own = lax.optimization_barrier((weights_out, back_in, own))
    weights_in = lax.all_to_all(weights_out, "dom", 0, 0, tiled=True)
    grad_feats = finish(listed, send_count, hub_ids, back_in, own)
    grad_self, grad_neigh = place_weights(me_s, weights_in.reshape(-1, width))
    return (output, grad_feats, grad_self, grad_neigh, grad_bias[0])


def solution(mesh):
    in_specs = (
        P("dom", "feat"),
        P("dom", None, None),
        P("dom"),
        P("dom"),
        P("dom"),
        P("dom", None, None),
        P("dom", None),
        P(None, "feat"),
        P(None, "feat"),
        P("feat"),
        P("dom", "feat"),
    )
    out_specs = (P("dom", "feat"), P("dom", "feat"), P(None, "feat"), P(None, "feat"), P("feat"))
    n_feat = mesh.shape["feat"]

    def run(*args):
        return body(*args, n_feat=n_feat)

    return jax.shard_map(run, mesh=mesh, in_specs=in_specs, out_specs=out_specs, check_vma=False)
```

```python
import functools

import jax
import jax.numpy as jnp
from jax import lax
from jax.experimental import pallas as pl
from jax.experimental.pallas import tpu as pltpu
from jax.sharding import PartitionSpec as P

F32 = jnp.float32
BF16 = jnp.bfloat16
VMEM = pl.BlockSpec(memory_space=pltpu.VMEM)
SMEM = pl.BlockSpec(memory_space=pltpu.SMEM)
HBM = pl.BlockSpec(memory_space=pltpu.HBM)
ANY = pl.BlockSpec(memory_space=pl.ANY)
UNROLL = 16
T_BITS, S_BITS = 10, 10


def params(mib=24):
    return pltpu.CompilerParams(vmem_limit_bytes=mib << 20)


def hbm(x):
    return pltpu.with_memory_space_constraint(x, pltpu.HBM)


def cost(flops, nbytes):
    return pl.CostEstimate(flops=flops, bytes_accessed=nbytes, transcendentals=0)


def start_copies(sems, *pairs):
    copies = [pltpu.make_async_copy(a, b, sems.at[i]) for i, (a, b) in enumerate(pairs)]
    for copy in copies:
        copy.start()
    return copies


def wait_copies(copies):
    for copy in copies:
        copy.wait()


def pick_kernel(rows_h, count_h, hub_h, x_h, out_h, rows_s, count_s, hub_s, x, x32, stage, out, sems, out_sems):
    copies = start_copies(sems, (x_h, x), (rows_h, rows_s), (count_h, count_s), (hub_h, hub_s))
    n_dom, capacity = rows_s.shape
    hub_dev = hub_s.shape[0]
    step = 64
    wait_copies(copies)
    x32[...] = x[...].astype(F32)
    for j in range(hub_dev):
        stage[capacity + j : capacity + j + 1, :] = x32[pl.ds(hub_s[j], 1), :]
    hub = stage[capacity:, :].astype(BF16)
    slot = lax.broadcasted_iota(jnp.int32, (capacity, x.shape[1]), 0)

    def peer(q, carry):
        def some(g, carry):
            for u in range(step):
                c = g * step + u
                stage[pl.ds(c, 1), :] = x32[pl.ds(rows_s[q, c], 1), :]
            return carry

        lax.fori_loop(0, capacity // step, some, 0)
        kept = jnp.where(slot < count_s[0, q], stage[:capacity, :], 0.0)
        out[q, :capacity, :] = kept.astype(BF16)
        out[q, capacity:, :] = hub
        pltpu.make_async_copy(out.at[q], out_h.at[q], out_sems.at[q]).start()
        return carry

    lax.fori_loop(0, n_dom, peer, 0)
    for q in range(n_dom):
        pltpu.make_async_copy(out.at[q], out_h.at[q], out_sems.at[q]).wait()


def pick(send_rows, send_count, hub_ids, x):
    n_dom, capacity = send_rows.shape
    rows = capacity + hub_ids.shape[0]
    shape = (n_dom, rows, x.shape[1])
    return pl.pallas_call(
        pick_kernel,
        out_shape=pltpu.HBM(shape, BF16),
        in_specs=[HBM] * 4,
        out_specs=HBM,
        scratch_shapes=[
            pltpu.SMEM(send_rows.shape, jnp.int32),
            pltpu.SMEM(send_count.shape, jnp.int32),
            pltpu.SMEM(hub_ids.shape, jnp.int32),
            pltpu.VMEM(x.shape, BF16),
            pltpu.VMEM(x.shape, F32),
            pltpu.VMEM((rows, x.shape[1]), F32),
            pltpu.VMEM(shape, BF16),
            pltpu.SemaphoreType.DMA((4,)),
            pltpu.SemaphoreType.DMA((n_dom,)),
        ],
        compiler_params=params(),
        cost_estimate=cost(0, 1 << 21),
        name="pick_rows",
    )(hbm(send_rows), hbm(send_count), hbm(hub_ids), hbm(x))


def unpack(entry):
    t = entry & ((1 << T_BITS) - 1)
    s = (entry >> T_BITS) & ((1 << S_BITS) - 1)
    return t, s, entry >> (T_BITS + S_BITS)


def make_lists(dst_s, src_s, lists, own_blocks, far_blocks):
    length = lists.shape[1] - 1

    def step(t, n):
        s = src_s[t]
        d = dst_s[t]
        far = (s >= own_blocks).astype(jnp.int32)
        lists[0, n[0]] = t + (s << T_BITS) + (d << (T_BITS + S_BITS))
        lists[1, n[1]] = t + ((s - own_blocks) << T_BITS) + (d << (T_BITS + S_BITS))
        return n[0] + 1 - far, n[1] + far

    n = lax.fori_loop(0, dst_s.shape[0], step, (jnp.int32(0), jnp.int32(0)))
    for which, blocks in ((0, own_blocks), (1, far_blocks)):
        spare = (blocks << T_BITS) + (own_blocks << (T_BITS + S_BITS))
        for u in range(UNROLL - 1):
            lists[which, n[which] + u] = jnp.int32(spare)
        lists[which, length] = n[which]


def add_tiles(lists, which, tiles, source, acc, spare):
    n = lists[which, lists.shape[1] - 1]

    def group(g, carry):
        done = []
        for u in range(UNROLL):
            t, s, d = unpack(lists[which, g * UNROLL + u])
            s = jnp.where(d == spare, 0, s)
            done.append((d, jnp.dot(tiles[t], source[s], preferred_element_type=F32)))
        for d, product in done:
            acc[d] += product
        return carry

    lax.fori_loop(0, (n + UNROLL - 1) // UNROLL, group, 0)


def add_tiles_t(lists, which, tiles, source, acc, spare):
    n = lists[which, lists.shape[1] - 1]

    def group(g, carry):
        done = []
        for u in range(UNROLL):
            t, s, d = unpack(lists[which, g * UNROLL + u])
            d = jnp.where(d == spare, 0, d)
            product = lax.dot_general(
                tiles[t], source[d], (((0,), (0,)), ((), ())), preferred_element_type=F32
            )
            done.append((s, product))
        for s, product in done:
            acc[s] += product
        return carry

    lax.fori_loop(0, (n + UNROLL - 1) // UNROLL, group, 0)


def own_kernel(
    dst_h, src_h, tiles_h, x_h, out_h, lists, dst_s, src_s, x, tiles, acc, sems, *, far_blocks
):
    own_blocks = x.shape[0]
    copies = start_copies(sems, (dst_h, dst_s), (src_h, src_s), (x_h, x), (tiles_h, tiles))
    acc[...] = jnp.zeros_like(acc)
    wait_copies(copies[:2])
    make_lists(dst_s, src_s, lists, own_blocks, far_blocks)
    wait_copies(copies[2:])
    add_tiles(lists, 0, tiles, x, acc, own_blocks)
    wait_copies(start_copies(sems, (acc.at[pl.ds(0, own_blocks)], out_h)))


def own_tiles(tile_dst, tile_src, tiles, x, far_blocks):
    n = tiles.shape[0]
    return pl.pallas_call(
        functools.partial(own_kernel, far_blocks=far_blocks),
        out_shape=(
            pltpu.HBM(x.shape, F32),
            jax.ShapeDtypeStruct((2, n + UNROLL), jnp.int32),
        ),
        in_specs=[HBM, HBM, HBM, HBM],
        out_specs=(HBM, SMEM),
        scratch_shapes=[
            pltpu.SMEM((n,), jnp.int32),
            pltpu.SMEM((n,), jnp.int32),
            pltpu.VMEM(x.shape, BF16),
            pltpu.VMEM(tiles.shape, BF16),
            pltpu.VMEM((x.shape[0] + 1,) + x.shape[1:], F32),
            pltpu.SemaphoreType.DMA((4,)),
        ],
        compiler_params=params(),
        cost_estimate=cost(2 * n * 128**3, 1 << 23),
        name="own_tiles",
    )(hbm(tile_dst), hbm(tile_src), hbm(tiles), hbm(x))


def far_kernel(lists, tiles, incoming_h, base_h, out_h, source, acc, out, sems):
    n_dom, rows, _ = incoming_h.shape
    own_blocks, tile, _ = base_h.shape
    hub_dev = rows - tile
    hub_blocks = n_dom * hub_dev // tile
    pairs = [(incoming_h.at[:, pl.ds(0, tile), :], source.at[pl.ds(hub_blocks, n_dom)])]
    pairs.append((base_h, acc.at[pl.ds(0, own_blocks)]))
    for q in range(n_dom):
        block, row = divmod(q * hub_dev, tile)
        pairs.append(
            (incoming_h.at[q, pl.ds(tile, hub_dev), :], source.at[block, pl.ds(row, hub_dev), :])
        )
    wait_copies(start_copies(sems, *pairs))
    add_tiles(lists, 1, tiles, source, acc, own_blocks)
    out[...] = acc[:own_blocks].astype(BF16)
    wait_copies(start_copies(sems, (out, out_h)))


def far_tiles(lists, tiles, incoming, base, far_blocks):
    own_blocks, tile, width = base.shape
    return pl.pallas_call(
        far_kernel,
        out_shape=pltpu.HBM(base.shape, BF16),
        in_specs=[SMEM, VMEM, HBM, HBM],
        out_specs=HBM,
        scratch_shapes=[
            pltpu.VMEM((far_blocks, tile, width), BF16),
            pltpu.VMEM((own_blocks + 1, tile, width), F32),
            pltpu.VMEM(base.shape, BF16),
            pltpu.SemaphoreType.DMA((incoming.shape[0] + 2,)),
        ],
        compiler_params=params(),
        cost_estimate=cost(tiles.shape[0] * 128**3, 1 << 22),
        name="far_tiles",
    )(lists, tiles, hbm(incoming), hbm(base))


def by_shards(me, shards, w):
    width = shards[0].shape[1]
    rows = [
        w[pl.ds(pl.multiple_of((me ^ k) * width, width), width), :] for k in range(len(shards))
    ]
    return jnp.dot(
        jnp.concatenate([s[...] for s in shards], axis=1),
        jnp.concatenate(rows, axis=0),
        preferred_element_type=F32,
    )


def stream(step, ins_h, ins, outs_h, outs, sems, block):
    rows = ins[0].shape[0]
    n_in = len(ins)
    pending = []
    for i in range(rows // block):
        at = pl.ds(i * block, block)
        pairs = [(a.at[at], b.at[at]) for a, b in zip(ins_h, ins)]
        pending.append(start_copies(sems.at[i], *pairs))
    leaving = []
    for i in range(rows // block):
        at = pl.ds(i * block, block)
        wait_copies(pending[i])
        step(at, [r.at[at] for r in ins], [r.at[at] for r in outs])
        pairs = [(a.at[at], b.at[at]) for a, b in zip(outs, outs_h)]
        leaving.append(start_copies(sems.at[i, pl.ds(n_in, len(outs))], *pairs))
    for copies in leaving:
        wait_copies(copies)


def stream_call(kernel, me, streamed, whole, outs, flops, name, block=2048):
    rows = streamed[0].shape[0]
    n_in, n_whole, n_out = len(streamed), len(whole), len(outs)

    def run(me_s, *refs):
        ins_h, refs = refs[:n_in], refs[n_in:]
        held, refs = refs[:n_whole], refs[n_whole:]
        outs_h, refs = refs[:n_out], refs[n_out:]
        ins, refs = refs[:n_in], refs[n_in:]
        out, sems = refs[:n_out], refs[n_out]
        stream(
            lambda at, i, o: kernel(me_s[0], i, held, o), ins_h, ins, outs_h, out, sems, block
        )

    return pl.pallas_call(
        run,
        out_shape=tuple(pltpu.HBM(shape, t) for shape, t in outs),
        in_specs=[SMEM] + [ANY] * n_in + [VMEM] * n_whole,
        out_specs=(HBM,) * n_out,
        scratch_shapes=[pltpu.VMEM(x.shape, x.dtype) for x in streamed]
        + [pltpu.VMEM(shape, t) for shape, t in outs]
        + [pltpu.SemaphoreType.DMA((rows // block, n_in + n_out))],
        compiler_params=params(),
        cost_estimate=cost(flops, 1 << 22),
        name=name,
    )(me, *streamed, *[hbm(x) for x in whole])


def self_step(me, ins, held, outs):
    w, bias = held
    outs[0][...] = by_shards(me, ins, w) + bias[...]


def forward_step(me, ins, held, outs):
    *shards, own_part, grad_out = ins
    output, grad_pre = outs
    pre_act = own_part[...] + by_shards(me, shards, held[0])
    gate = jax.nn.sigmoid(pre_act)
    output[...] = (pre_act * gate).astype(BF16)
    grad = grad_out[...].astype(F32) * gate * (1.0 + pre_act * (1.0 - gate))
    grad_pre[...] = grad.astype(BF16)


def weights_kernel(*refs, n_feat):
    shards, grad, out_h, out, sems = refs[: 2 * n_feat], *refs[2 * n_feat :]
    n_dom, chunk = out.shape[0], out.shape[1] - 8
    width = grad.shape[1]
    flipped = grad[...].T
    bias = jnp.sum(grad[...].astype(F32), axis=0, keepdims=True)
    for i, shard in enumerate(shards):
        block = jnp.dot(flipped, shard[...], preferred_element_type=F32).T
        for row in range(0, width, min(chunk, width)):
            q, start = divmod(i * width + row, chunk)
            n = min(chunk, width)
            out[q, start : start + n, :] = block[row : row + n, :]
    for q in range(n_dom):
        out[q, chunk:, :] = jnp.broadcast_to(bias, (8, width))
    wait_copies(start_copies(sems, (out, out_h)))


def weight_parts(shards, grad, n_dom):
    n_feat = len(shards) // 2
    width = grad.shape[1]
    chunk = 2 * n_feat * width // n_dom
    return pl.pallas_call(
        functools.partial(weights_kernel, n_feat=n_feat),
        out_shape=pltpu.HBM((n_dom, chunk + 8, width), F32),
        in_specs=[VMEM] * (2 * n_feat + 1),
        out_specs=HBM,
        scratch_shapes=[
            pltpu.VMEM((n_dom, chunk + 8, width), F32),
            pltpu.SemaphoreType.DMA((1,)),
        ],
        compiler_params=params(),
        cost_estimate=cost(4 * n_feat * width * width * grad.shape[0], 1 << 22),
        name="weight_parts",
    )(*shards, grad)


def split_copies(sems, pairs, block):
    rows = pairs[0][0].shape[0]
    return [
        start_copies(
            sems.at[i], *[(a.at[pl.ds(i * block, block)], b.at[pl.ds(i * block, block)]) for a, b in pairs]
        )
        for i in range(rows // block)
    ]


def back_far_kernel(*refs, n_feat):
    lists, tiles = refs[:2]
    grads_h, w = refs[2 : 2 + n_feat], refs[2 + n_feat : 2 + 2 * n_feat]
    out_h, back_h, direct_h = refs[2 + 2 * n_feat : 5 + 2 * n_feat]
    grads = refs[5 + 2 * n_feat : 5 + 3 * n_feat]
    back, direct, acc, out, sems, out_sems = refs[5 + 3 * n_feat :]
    n_dom = out.shape[0]
    own_blocks, tile, width = back.shape
    hub_dev = out.shape[1] - tile
    hub_blocks = n_dom * hub_dev // tile
    block = 4 * tile
    pending = split_copies(sems, list(zip(grads_h, grads)), block)
    acc[...] = jnp.zeros_like(acc)
    own_w, near_w, far_w, both_w = w
    rows = [r.reshape(2 * width, -1) for r in (own_w[...], near_w[...], far_w[0], both_w[1])]
    rows = jnp.concatenate(rows, axis=1)
    for i, copies in enumerate(pending):
        wait_copies(copies)
        whole = jnp.concatenate([g[i * block : (i + 1) * block, :] for g in grads], axis=1)
        both = lax.dot_general(whole, rows, (((1,), (1,)), ((), ())), preferred_element_type=F32)
        direct[4 * i : 4 * (i + 1)] = both[:, :width].reshape(4, tile, width)
        back[4 * i : 4 * (i + 1)] = both[:, width:].astype(BF16).reshape(4, tile, width)
    leaving = start_copies(out_sems, (direct, direct_h), (back, back_h))
    add_tiles_t(lists, 1, tiles, back, acc, own_blocks)
    for q in range(n_dom):
        out[q, :tile, :] = acc[hub_blocks + q].astype(BF16)
        at, row = divmod(q * hub_dev, tile)
        out[q, tile:, :] = acc[at, row : row + hub_dev, :].astype(BF16)
    leaving += start_copies(out_sems.at[pl.ds(2, 1)], (out, out_h))
    wait_copies(leaving)


def back_far(lists, tiles, grads, w, n_dom, hub_dev, tile):
    n_feat = len(grads)
    rows, width = grads[0].shape
    far_blocks = n_dom * hub_dev // tile + n_dom
    shape = (n_dom, tile + hub_dev, width)
    back_shape = (rows // tile, tile, width)
    return pl.pallas_call(
        functools.partial(back_far_kernel, n_feat=n_feat),
        out_shape=(pltpu.HBM(shape, BF16), pltpu.HBM(back_shape, BF16), pltpu.HBM(back_shape, F32)),
        in_specs=[SMEM, VMEM] + [ANY] * n_feat + [VMEM] * n_feat,
        out_specs=(HBM, HBM, HBM),
        scratch_shapes=[pltpu.VMEM((rows, width), BF16)] * n_feat
        + [
            pltpu.VMEM(back_shape, BF16),
            pltpu.VMEM(back_shape, F32),
            pltpu.VMEM((far_blocks + 1, tile, width), F32),
            pltpu.VMEM(shape, BF16),
            pltpu.SemaphoreType.DMA((rows // (4 * tile), n_feat)),
            pltpu.SemaphoreType.DMA((3,)),
        ],
        compiler_params=params(),
        cost_estimate=cost(4 * rows * width * width * n_feat, 1 << 22),
        name="back_far",
    )(lists, tiles, *grads, *[hbm(r) for r in w])


def back_own_kernel(lists, tiles, back_h, direct_h, out_h, back, acc, sems):
    own_blocks = back.shape[0]
    own = acc.at[pl.ds(0, own_blocks)]
    wait_copies(start_copies(sems, (back_h, back), (direct_h, own)))
    add_tiles_t(lists, 0, tiles, back, acc, own_blocks)
    wait_copies(start_copies(sems, (own, out_h)))


def back_own(lists, tiles, back, direct):
    return pl.pallas_call(
        back_own_kernel,
        out_shape=pltpu.HBM(direct.shape, F32),
        in_specs=[SMEM, VMEM, HBM, HBM],
        out_specs=HBM,
        scratch_shapes=[
            pltpu.VMEM(back.shape, BF16),
            pltpu.VMEM((direct.shape[0] + 1,) + direct.shape[1:], F32),
            pltpu.SemaphoreType.DMA((2,)),
        ],
        compiler_params=params(),
        cost_estimate=cost(2 * tiles.shape[0] * 128**3, 1 << 23),
        name="back_own",
    )(lists, tiles, hbm(back), hbm(direct))


def finish_kernel(rows_s, count_h, hub_h, incoming_h, base_h, out_h, count_s, hub_s, sent, hubs, base, sems, out_sems):
    n_dom, capacity = rows_s.shape
    hub_dev = hub_s.shape[0]
    own_count, width = base.shape
    block, peers = 256, min(8, n_dom)
    copies = start_copies(
        sems,
        (count_h, count_s),
        (hub_h, hub_s),
        (incoming_h.at[:, pl.ds(0, capacity), :], sent),
        (incoming_h.at[:, pl.ds(capacity, hub_dev), :], hubs),
        (base_h, base),
    )
    wait_copies(copies)
    hub = hubs[0].astype(F32)
    for q in range(1, n_dom):
        hub += hubs[q].astype(F32)
    for j in range(hub_dev):
        base[pl.ds(hub_s[j], 1), :] += hub[j : j + 1, :]
    lane = lax.broadcasted_iota(jnp.int32, (1, capacity), 1)
    leaving = []
    for start in range(0, own_count, block):
        vertex = lax.broadcasted_iota(jnp.int32, (block, capacity), 0) + start
        total = base[start : start + block, :]
        for first in range(0, n_dom, peers):
            hot, rows = [], []
            for q in range(first, first + peers):
                wanted = jnp.where(lane < count_s[0, q], rows_s[q : q + 1, :], -1)
                hot.append((vertex == wanted).astype(F32).astype(BF16))
                rows.append(sent[q])
            total += jnp.dot(
                jnp.concatenate(hot, axis=1),
                jnp.concatenate(rows, axis=0),
                preferred_element_type=F32,
            )
        base[start : start + block, :] = total
        at = pl.ds(start, block)
        leaving.append(start_copies(out_sems.at[pl.ds(start // block, 1)], (base.at[at], out_h.at[at])))
    for copies in leaving:
        wait_copies(copies)


def finish(send_rows, send_count, hub_ids, incoming, base):
    n_dom, capacity = send_rows.shape
    hub_dev = hub_ids.shape[0]
    own_count, width = base.shape
    return pl.pallas_call(
        finish_kernel,
        out_shape=pltpu.HBM(base.shape, F32),
        in_specs=[VMEM, HBM, HBM, ANY, HBM],
        out_specs=HBM,
        scratch_shapes=[
            pltpu.SMEM(send_count.shape, jnp.int32),
            pltpu.SMEM(hub_ids.shape, jnp.int32),
            pltpu.VMEM((n_dom, capacity, width), BF16),
            pltpu.VMEM((n_dom, hub_dev, width), BF16),
            pltpu.VMEM(base.shape, F32),
            pltpu.SemaphoreType.DMA((5,)),
            pltpu.SemaphoreType.DMA((own_count // 256,)),
        ],
        compiler_params=params(),
        cost_estimate=cost(2 * base.size * send_rows.size, 1 << 22),
        name="finish",
    )(hbm(send_rows), hbm(send_count), hbm(hub_ids), incoming, hbm(base))


def cut_kernel(me_s, w_self, w_neigh, *outs):
    width = w_self.shape[1]
    own, near, far = outs
    for k, out in enumerate((own, near, far.at[0], far.at[1])):
        at = pl.ds(pl.multiple_of((me_s[0] ^ k) * width, width), width)
        out[0] = w_self[at, :]
        out[1] = w_neigh[at, :]


def cut_weights(me, w_self, w_neigh):
    width = w_self.shape[1]
    one = (2, width, width)
    return pl.pallas_call(
        cut_kernel,
        out_shape=tuple(pltpu.HBM(shape, BF16) for shape in (one, one, (2,) + one)),
        in_specs=[SMEM, VMEM, VMEM],
        out_specs=(VMEM,) * 3,
        compiler_params=params(),
        cost_estimate=cost(0, 1 << 20),
        name="cut_weights",
    )(me, hbm(w_self), hbm(w_neigh))


def sum_kernel(parts, out, bias):
    n_dom, chunk = parts.shape[0], out.shape[0]
    total = parts[0]
    for q in range(1, n_dom):
        total += parts[q]
    bias[...] = total[chunk : chunk + 1, :]
    out[...] = total[:chunk, :].astype(BF16)


def sum_parts(parts):
    _, rows, width = parts.shape
    return pl.pallas_call(
        sum_kernel,
        out_shape=(pltpu.HBM((rows - 8, width), BF16), pltpu.HBM((1, width), F32)),
        in_specs=[VMEM],
        out_specs=(VMEM, VMEM),
        compiler_params=params(),
        cost_estimate=cost(0, 1 << 20),
        name="sum_parts",
    )(hbm(parts))


def place_kernel(me_s, sums, self_out, neigh_out):
    rows, width = self_out.shape
    half, _, chunk, _ = sums.shape
    n = min(chunk, width)
    for j in range(half):
        for t in range(2):
            index = ((me_s[1] & half) ^ (t * half)) + j
            for part in range(0, chunk, n):
                row = index * chunk + part
                feat = me_s[0] ^ (row // width % (rows // width))
                at = pl.ds(pl.multiple_of(feat * width + row % width, n), n)
                piece = sums[j, t, part : part + n, :].astype(F32)

                @pl.when(row < rows)
                def _():
                    self_out[at, :] = piece

                @pl.when(row >= rows)
                def _():
                    neigh_out[at, :] = piece


def place_weights(both, sums, rows):
    width = sums.shape[-1]
    return pl.pallas_call(
        place_kernel,
        out_shape=(pltpu.HBM((rows, width), F32),) * 2,
        in_specs=[SMEM, VMEM],
        out_specs=(VMEM, VMEM),
        compiler_params=params(),
        cost_estimate=cost(0, 1 << 20),
        name="place_weights",
    )(both, sums)


def body(
    node_feats,
    edge_tiles,
    tile_dst,
    tile_src,
    hub_ids,
    send_rows,
    send_count,
    w_self,
    w_neigh,
    out_bias,
    grad_out,
    *,
    n_feat,
):
    own_count, width = node_feats.shape
    tile_size = edge_tiles.shape[1]
    listed = send_rows[0]
    n_dom, capacity = listed.shape
    hub_dev = hub_ids.shape[0]
    me = lax.axis_index("feat").astype(jnp.int32)
    me_s = me.reshape(1)
    far, near = 2, 1
    assert n_feat == 4
    far_blocks = n_dom * hub_dev // tile_size + n_dom

    def swap(x, k):
        return lax.ppermute(x, "feat", [(j, j ^ k) for j in range(n_feat)])

    feat_far = swap(node_feats, far)

    outgoing = pick(listed, send_count, hub_ids, node_feats)
    incoming = lax.all_to_all(outgoing, "dom", 0, 0, tiled=True)
    cut = cut_weights(me_s, w_self, w_neigh)
    own_feats, *cut = lax.optimization_barrier((node_feats.reshape(-1, tile_size, width), *cut))
    far_w = swap(cut[2], far)
    base, lists = own_tiles(tile_dst, tile_src, edge_tiles, own_feats, far_blocks)
    aggregated = far_tiles(lists, edge_tiles, incoming, base, far_blocks).reshape(own_count, width)

    aggregated, far_w = lax.optimization_barrier((aggregated, far_w))
    w_rows = [cut[0], swap(cut[1], near), far_w, swap(far_w, near)]
    agg_far = swap(aggregated, far)
    feat_far, aggregated = lax.optimization_barrier((feat_far, aggregated))
    feats = [hbm(node_feats), swap(node_feats, near), feat_far, swap(feat_far, near)]
    flops = 2 * own_count * n_feat * width * width
    rows_out = ((own_count, width), BF16)
    (own_part,) = stream_call(
        self_step,
        me_s,
        feats,
        [w_self, out_bias[None, :]],
        [((own_count, width), F32)],
        flops,
        "self_dense",
    )
    agg_far, own_part, *w_rows = lax.optimization_barrier((agg_far, own_part, *w_rows))
    aggs = [hbm(aggregated), swap(aggregated, near), agg_far, swap(agg_far, near)]
    output, grad_pre = stream_call(
        forward_step,
        me_s,
        [*aggs, hbm(own_part), hbm(grad_out)],
        [w_neigh],
        [rows_out, rows_out],
        flops,
        "forward_dense",
    )

    grad_far = swap(grad_pre, far)
    parts = weight_parts(feats + aggs, hbm(grad_pre), n_dom)
    part_sums = lax.all_to_all(parts, "dom", 0, 0, tiled=True)
    grads = [hbm(grad_pre), swap(grad_pre, near), grad_far, swap(grad_far, near)]

    back_out, back_agg, direct = back_far(
        lists, edge_tiles, grads, w_rows, n_dom, hub_dev, tile_size
    )
    back_in = lax.all_to_all(back_out, "dom", 0, 0, tiled=True)
    own = back_own(lists, edge_tiles, back_agg, direct).reshape(own_count, width)
    weights, grad_bias = sum_parts(part_sums)
    half = n_dom // 2
    other = lax.ppermute(weights, "dom", [(j, j ^ half) for j in range(n_dom)])
    other, own = lax.optimization_barrier((other, own))
    pair = jnp.stack([weights, other])
    weights_out = jnp.broadcast_to(pair[None], (half,) + pair.shape)
    weights_out, back_in, own = lax.optimization_barrier((weights_out, back_in, own))
    halves = [list(range(half)), list(range(half, n_dom))]
    weights_in = lax.all_to_all(weights_out, "dom", 0, 0, axis_index_groups=halves, tiled=True)
    grad_feats = finish(listed, send_count, hub_ids, back_in, own)
    both = jnp.stack([me, lax.axis_index("dom").astype(jnp.int32)])
    grad_self, grad_neigh = place_weights(both, weights_in, n_feat * width)
    return (output, grad_feats, grad_self, grad_neigh, grad_bias[0])


def solution(mesh):
    in_specs = (
        P("dom", "feat"),
        P("dom", None, None),
        P("dom"),
        P("dom"),
        P("dom"),
        P("dom", None, None),
        P("dom", None),
        P(None, "feat"),
        P(None, "feat"),
        P("feat"),
        P("dom", "feat"),
    )
    out_specs = (P("dom", "feat"), P("dom", "feat"), P(None, "feat"), P(None, "feat"), P("feat"))
    n_feat = mesh.shape["feat"]

    def run(*args):
        return body(*args, n_feat=n_feat)

    return jax.shard_map(run, mesh=mesh, in_specs=in_specs, out_specs=out_specs, check_vma=False)
```

```python
import functools

import jax
import jax.numpy as jnp
from jax import lax
from jax.experimental import pallas as pl
from jax.experimental.pallas import tpu as pltpu
from jax.sharding import PartitionSpec as P

F32 = jnp.float32
BF16 = jnp.bfloat16
VMEM = pl.BlockSpec(memory_space=pltpu.VMEM)
SMEM = pl.BlockSpec(memory_space=pltpu.SMEM)
HBM = pl.BlockSpec(memory_space=pltpu.HBM)
ANY = pl.BlockSpec(memory_space=pl.ANY)
UNROLL = 16
T_BITS, S_BITS = 10, 10


def params(mib=24):
    return pltpu.CompilerParams(vmem_limit_bytes=mib << 20)


def hbm(x):
    return pltpu.with_memory_space_constraint(x, pltpu.HBM)


def cost(flops, nbytes):
    return pl.CostEstimate(flops=flops, bytes_accessed=nbytes, transcendentals=0)


def start_copies(sems, *pairs):
    copies = [pltpu.make_async_copy(a, b, sems.at[i]) for i, (a, b) in enumerate(pairs)]
    for copy in copies:
        copy.start()
    return copies


def wait_copies(copies):
    for copy in copies:
        copy.wait()


def pick_kernel(rows_h, count_h, hub_h, x_h, out_h, rows_s, count_s, hub_s, x, x32, stage, out, sems, out_sems):
    copies = start_copies(sems, (x_h, x), (rows_h, rows_s), (count_h, count_s), (hub_h, hub_s))
    n_dom, capacity = rows_s.shape
    hub_dev = hub_s.shape[0]
    step = 64
    wait_copies(copies)
    x32[...] = x[...].astype(F32)
    for j in range(hub_dev):
        stage[capacity + j : capacity + j + 1, :] = x32[pl.ds(hub_s[j], 1), :]
    hub = stage[capacity:, :].astype(BF16)
    slot = lax.broadcasted_iota(jnp.int32, (capacity, x.shape[1]), 0)

    def peer(q, carry):
        def some(g, carry):
            for u in range(step):
                c = g * step + u
                stage[pl.ds(c, 1), :] = x32[pl.ds(rows_s[q, c], 1), :]
            return carry

        lax.fori_loop(0, capacity // step, some, 0)
        kept = jnp.where(slot < count_s[0, q], stage[:capacity, :], 0.0)
        out[q, :capacity, :] = kept.astype(BF16)
        out[q, capacity:, :] = hub
        pltpu.make_async_copy(out.at[q], out_h.at[q], out_sems.at[q]).start()
        return carry

    lax.fori_loop(0, n_dom, peer, 0)
    for q in range(n_dom):
        pltpu.make_async_copy(out.at[q], out_h.at[q], out_sems.at[q]).wait()


def pick(send_rows, send_count, hub_ids, x):
    n_dom, capacity = send_rows.shape
    rows = capacity + hub_ids.shape[0]
    shape = (n_dom, rows, x.shape[1])
    return pl.pallas_call(
        pick_kernel,
        out_shape=pltpu.HBM(shape, BF16),
        in_specs=[HBM] * 4,
        out_specs=HBM,
        scratch_shapes=[
            pltpu.SMEM(send_rows.shape, jnp.int32),
            pltpu.SMEM(send_count.shape, jnp.int32),
            pltpu.SMEM(hub_ids.shape, jnp.int32),
            pltpu.VMEM(x.shape, BF16),
            pltpu.VMEM(x.shape, F32),
            pltpu.VMEM((rows, x.shape[1]), F32),
            pltpu.VMEM(shape, BF16),
            pltpu.SemaphoreType.DMA((4,)),
            pltpu.SemaphoreType.DMA((n_dom,)),
        ],
        compiler_params=params(),
        cost_estimate=cost(0, 1 << 21),
        name="pick_rows",
    )(hbm(send_rows), hbm(send_count), hbm(hub_ids), hbm(x))


def unpack(entry):
    t = entry & ((1 << T_BITS) - 1)
    s = (entry >> T_BITS) & ((1 << S_BITS) - 1)
    return t, s, entry >> (T_BITS + S_BITS)


def make_lists(dst_s, src_s, lists, own_blocks, far_blocks):
    length = lists.shape[1] - 1

    def step(t, n):
        s = src_s[t]
        d = dst_s[t]
        far = (s >= own_blocks).astype(jnp.int32)
        lists[0, n[0]] = t + (s << T_BITS) + (d << (T_BITS + S_BITS))
        lists[1, n[1]] = t + ((s - own_blocks) << T_BITS) + (d << (T_BITS + S_BITS))
        return n[0] + 1 - far, n[1] + far

    n = lax.fori_loop(0, dst_s.shape[0], step, (jnp.int32(0), jnp.int32(0)))
    for which, blocks in ((0, own_blocks), (1, far_blocks)):
        spare = (blocks << T_BITS) + (own_blocks << (T_BITS + S_BITS))
        for u in range(UNROLL - 1):
            lists[which, n[which] + u] = jnp.int32(spare)
        lists[which, length] = n[which]


def add_tiles(lists, which, tiles, source, acc, spare):
    n = lists[which, lists.shape[1] - 1]

    def group(g, carry):
        done = []
        for u in range(UNROLL):
            t, s, d = unpack(lists[which, g * UNROLL + u])
            s = jnp.where(d == spare, 0, s)
            done.append((d, jnp.dot(tiles[t], source[s], preferred_element_type=F32)))
        for d, product in done:
            acc[d] += product
        return carry

    lax.fori_loop(0, (n + UNROLL - 1) // UNROLL, group, 0)


def add_tiles_t(lists, which, tiles, source, acc, spare):
    n = lists[which, lists.shape[1] - 1]

    def group(g, carry):
        done = []
        for u in range(UNROLL):
            t, s, d = unpack(lists[which, g * UNROLL + u])
            d = jnp.where(d == spare, 0, d)
            product = lax.dot_general(
                tiles[t], source[d], (((0,), (0,)), ((), ())), preferred_element_type=F32
            )
            done.append((s, product))
        for s, product in done:
            acc[s] += product
        return carry

    lax.fori_loop(0, (n + UNROLL - 1) // UNROLL, group, 0)


def own_kernel(
    dst_h, src_h, tiles_h, x_h, out_h, lists, dst_s, src_s, x, tiles, acc, sems, *, far_blocks
):
    own_blocks = x.shape[0]
    copies = start_copies(sems, (dst_h, dst_s), (src_h, src_s), (x_h, x), (tiles_h, tiles))
    acc[...] = jnp.zeros_like(acc)
    wait_copies(copies[:2])
    make_lists(dst_s, src_s, lists, own_blocks, far_blocks)
    wait_copies(copies[2:])
    add_tiles(lists, 0, tiles, x, acc, own_blocks)
    wait_copies(start_copies(sems, (acc.at[pl.ds(0, own_blocks)], out_h)))


def own_tiles(tile_dst, tile_src, tiles, x, far_blocks):
    n = tiles.shape[0]
    return pl.pallas_call(
        functools.partial(own_kernel, far_blocks=far_blocks),
        out_shape=(
            pltpu.HBM(x.shape, F32),
            jax.ShapeDtypeStruct((2, n + UNROLL), jnp.int32),
        ),
        in_specs=[HBM, HBM, HBM, HBM],
        out_specs=(HBM, SMEM),
        scratch_shapes=[
            pltpu.SMEM((n,), jnp.int32),
            pltpu.SMEM((n,), jnp.int32),
            pltpu.VMEM(x.shape, BF16),
            pltpu.VMEM(tiles.shape, BF16),
            pltpu.VMEM((x.shape[0] + 1,) + x.shape[1:], F32),
            pltpu.SemaphoreType.DMA((4,)),
        ],
        compiler_params=params(),
        cost_estimate=cost(2 * n * 128**3, 1 << 23),
        name="own_tiles",
    )(hbm(tile_dst), hbm(tile_src), hbm(tiles), hbm(x))


def far_kernel(lists, tiles, incoming_h, base_h, out_h, source, acc, out, sems):
    n_dom, rows, _ = incoming_h.shape
    own_blocks, tile, _ = base_h.shape
    hub_dev = rows - tile
    hub_blocks = n_dom * hub_dev // tile
    pairs = [(incoming_h.at[:, pl.ds(0, tile), :], source.at[pl.ds(hub_blocks, n_dom)])]
    pairs.append((base_h, acc.at[pl.ds(0, own_blocks)]))
    for q in range(n_dom):
        block, row = divmod(q * hub_dev, tile)
        pairs.append(
            (incoming_h.at[q, pl.ds(tile, hub_dev), :], source.at[block, pl.ds(row, hub_dev), :])
        )
    wait_copies(start_copies(sems, *pairs))
    add_tiles(lists, 1, tiles, source, acc, own_blocks)
    out[...] = acc[:own_blocks].astype(BF16)
    wait_copies(start_copies(sems, (out, out_h)))


def far_tiles(lists, tiles, incoming, base, far_blocks):
    own_blocks, tile, width = base.shape
    return pl.pallas_call(
        far_kernel,
        out_shape=pltpu.HBM(base.shape, BF16),
        in_specs=[SMEM, VMEM, HBM, HBM],
        out_specs=HBM,
        scratch_shapes=[
            pltpu.VMEM((far_blocks, tile, width), BF16),
            pltpu.VMEM((own_blocks + 1, tile, width), F32),
            pltpu.VMEM(base.shape, BF16),
            pltpu.SemaphoreType.DMA((incoming.shape[0] + 2,)),
        ],
        compiler_params=params(),
        cost_estimate=cost(tiles.shape[0] * 128**3, 1 << 22),
        name="far_tiles",
    )(lists, tiles, hbm(incoming), hbm(base))


def by_shards(me, shards, w):
    width = shards[0].shape[1]
    rows = [
        w[pl.ds(pl.multiple_of((me ^ k) * width, width), width), :] for k in range(len(shards))
    ]
    return jnp.dot(
        jnp.concatenate([s[...] for s in shards], axis=1),
        jnp.concatenate(rows, axis=0),
        preferred_element_type=F32,
    )


def stream(step, ins_h, ins, outs_h, outs, sems, block):
    rows = ins[0].shape[0]
    n_in = len(ins)
    pending = []
    for i in range(rows // block):
        at = pl.ds(i * block, block)
        pairs = [(a.at[at], b.at[at]) for a, b in zip(ins_h, ins)]
        pending.append(start_copies(sems.at[i], *pairs))
    leaving = []
    for i in range(rows // block):
        at = pl.ds(i * block, block)
        wait_copies(pending[i])
        step(at, [r.at[at] for r in ins], [r.at[at] for r in outs])
        pairs = [(a.at[at], b.at[at]) for a, b in zip(outs, outs_h)]
        leaving.append(start_copies(sems.at[i, pl.ds(n_in, len(outs))], *pairs))
    for copies in leaving:
        wait_copies(copies)


def stream_call(kernel, me, streamed, whole, outs, flops, name, block=2048):
    rows = streamed[0].shape[0]
    n_in, n_whole, n_out = len(streamed), len(whole), len(outs)

    def run(me_s, *refs):
        ins_h, refs = refs[:n_in], refs[n_in:]
        held, refs = refs[:n_whole], refs[n_whole:]
        outs_h, refs = refs[:n_out], refs[n_out:]
        ins, refs = refs[:n_in], refs[n_in:]
        out, sems = refs[:n_out], refs[n_out]
        stream(
            lambda at, i, o: kernel(me_s[0], i, held, o), ins_h, ins, outs_h, out, sems, block
        )

    return pl.pallas_call(
        run,
        out_shape=tuple(pltpu.HBM(shape, t) for shape, t in outs),
        in_specs=[SMEM] + [ANY] * n_in + [VMEM] * n_whole,
        out_specs=(HBM,) * n_out,
        scratch_shapes=[pltpu.VMEM(x.shape, x.dtype) for x in streamed]
        + [pltpu.VMEM(shape, t) for shape, t in outs]
        + [pltpu.SemaphoreType.DMA((rows // block, n_in + n_out))],
        compiler_params=params(),
        cost_estimate=cost(flops, 1 << 22),
        name=name,
    )(me, *streamed, *[hbm(x) for x in whole])


def self_step(me, ins, held, outs):
    w, bias = held
    outs[0][...] = by_shards(me, ins, w) + bias[...]


def forward_step(me, ins, held, outs):
    *shards, own_part, grad_out = ins
    output, grad_pre = outs
    pre_act = own_part[...] + by_shards(me, shards, held[0])
    gate = jax.nn.sigmoid(pre_act)
    output[...] = (pre_act * gate).astype(BF16)
    grad = grad_out[...].astype(F32) * gate * (1.0 + pre_act * (1.0 - gate))
    grad_pre[...] = grad.astype(BF16)


def weights_kernel(*refs, n_feat):
    shards, grad, out_h, out, sems = refs[: 2 * n_feat], *refs[2 * n_feat :]
    n_dom, chunk = out.shape[0], out.shape[1] - 8
    width = grad.shape[1]
    flipped = grad[...].T
    bias = jnp.sum(grad[...].astype(F32), axis=0, keepdims=True)
    for i, shard in enumerate(shards):
        block = jnp.dot(flipped, shard[...], preferred_element_type=F32).T
        for row in range(0, width, min(chunk, width)):
            q, start = divmod(i * width + row, chunk)
            n = min(chunk, width)
            q = q % (n_dom // 2) * 2 + q // (n_dom // 2)
            out[q, start : start + n, :] = block[row : row + n, :]
    for q in range(n_dom):
        out[q, chunk:, :] = jnp.broadcast_to(bias, (8, width))
    wait_copies(start_copies(sems, (out, out_h)))


def weight_parts(shards, grad, n_dom):
    n_feat = len(shards) // 2
    width = grad.shape[1]
    chunk = 2 * n_feat * width // n_dom
    return pl.pallas_call(
        functools.partial(weights_kernel, n_feat=n_feat),
        out_shape=pltpu.HBM((n_dom, chunk + 8, width), F32),
        in_specs=[VMEM] * (2 * n_feat + 1),
        out_specs=HBM,
        scratch_shapes=[
            pltpu.VMEM((n_dom, chunk + 8, width), F32),
            pltpu.SemaphoreType.DMA((1,)),
        ],
        compiler_params=params(),
        cost_estimate=cost(4 * n_feat * width * width * grad.shape[0], 1 << 22),
        name="weight_parts",
    )(*shards, grad)


def split_copies(sems, pairs, block):
    rows = pairs[0][0].shape[0]
    return [
        start_copies(
            sems.at[i], *[(a.at[pl.ds(i * block, block)], b.at[pl.ds(i * block, block)]) for a, b in pairs]
        )
        for i in range(rows // block)
    ]


def back_far_kernel(*refs, n_feat):
    lists, tiles = refs[:2]
    grads_h, w = refs[2 : 2 + n_feat], refs[2 + n_feat : 2 + 2 * n_feat]
    out_h, back_h, direct_h = refs[2 + 2 * n_feat : 5 + 2 * n_feat]
    grads = refs[5 + 2 * n_feat : 5 + 3 * n_feat]
    back, direct, acc, out, sems, out_sems = refs[5 + 3 * n_feat :]
    n_dom = out.shape[0]
    own_blocks, tile, width = back.shape
    hub_dev = out.shape[1] - tile
    hub_blocks = n_dom * hub_dev // tile
    block = 4 * tile
    pending = split_copies(sems, list(zip(grads_h, grads)), block)
    acc[...] = jnp.zeros_like(acc)
    own_w, near_w, far_w, both_w = w
    rows = [r.reshape(2 * width, -1) for r in (own_w[...], near_w[...], far_w[0], both_w[1])]
    rows = jnp.concatenate(rows, axis=1)
    for i, copies in enumerate(pending):
        wait_copies(copies)
        whole = jnp.concatenate([g[i * block : (i + 1) * block, :] for g in grads], axis=1)
        both = lax.dot_general(whole, rows, (((1,), (1,)), ((), ())), preferred_element_type=F32)
        direct[4 * i : 4 * (i + 1)] = both[:, :width].reshape(4, tile, width)
        back[4 * i : 4 * (i + 1)] = both[:, width:].astype(BF16).reshape(4, tile, width)
    leaving = start_copies(out_sems, (direct, direct_h), (back, back_h))
    add_tiles_t(lists, 1, tiles, back, acc, own_blocks)
    for q in range(n_dom):
        out[q, :tile, :] = acc[hub_blocks + q].astype(BF16)
        at, row = divmod(q * hub_dev, tile)
        out[q, tile:, :] = acc[at, row : row + hub_dev, :].astype(BF16)
    leaving += start_copies(out_sems.at[pl.ds(2, 1)], (out, out_h))
    wait_copies(leaving)


def back_far(lists, tiles, grads, w, n_dom, hub_dev, tile):
    n_feat = len(grads)
    rows, width = grads[0].shape
    far_blocks = n_dom * hub_dev // tile + n_dom
    shape = (n_dom, tile + hub_dev, width)
    back_shape = (rows // tile, tile, width)
    return pl.pallas_call(
        functools.partial(back_far_kernel, n_feat=n_feat),
        out_shape=(pltpu.HBM(shape, BF16), pltpu.HBM(back_shape, BF16), pltpu.HBM(back_shape, F32)),
        in_specs=[SMEM, VMEM] + [ANY] * n_feat + [VMEM] * n_feat,
        out_specs=(HBM, HBM, HBM),
        scratch_shapes=[pltpu.VMEM((rows, width), BF16)] * n_feat
        + [
            pltpu.VMEM(back_shape, BF16),
            pltpu.VMEM(back_shape, F32),
            pltpu.VMEM((far_blocks + 1, tile, width), F32),
            pltpu.VMEM(shape, BF16),
            pltpu.SemaphoreType.DMA((rows // (4 * tile), n_feat)),
            pltpu.SemaphoreType.DMA((3,)),
        ],
        compiler_params=params(),
        cost_estimate=cost(4 * rows * width * width * n_feat, 1 << 22),
        name="back_far",
    )(lists, tiles, *grads, *[hbm(r) for r in w])


def back_own_kernel(lists, tiles, back_h, direct_h, out_h, back, acc, sems):
    own_blocks = back.shape[0]
    own = acc.at[pl.ds(0, own_blocks)]
    wait_copies(start_copies(sems, (back_h, back), (direct_h, own)))
    add_tiles_t(lists, 0, tiles, back, acc, own_blocks)
    wait_copies(start_copies(sems, (own, out_h)))


def back_own(lists, tiles, back, direct):
    return pl.pallas_call(
        back_own_kernel,
        out_shape=pltpu.HBM(direct.shape, F32),
        in_specs=[SMEM, VMEM, HBM, HBM],
        out_specs=HBM,
        scratch_shapes=[
            pltpu.VMEM(back.shape, BF16),
            pltpu.VMEM((direct.shape[0] + 1,) + direct.shape[1:], F32),
            pltpu.SemaphoreType.DMA((2,)),
        ],
        compiler_params=params(),
        cost_estimate=cost(2 * tiles.shape[0] * 128**3, 1 << 23),
        name="back_own",
    )(lists, tiles, hbm(back), hbm(direct))


def finish_kernel(rows_s, count_h, hub_h, incoming_h, base_h, out_h, count_s, hub_s, sent, hubs, base, sems, out_sems):
    n_dom, capacity = rows_s.shape
    hub_dev = hub_s.shape[0]
    own_count, width = base.shape
    block, peers = 256, min(8, n_dom)
    copies = start_copies(
        sems,
        (count_h, count_s),
        (hub_h, hub_s),
        (incoming_h.at[:, pl.ds(0, capacity), :], sent),
        (incoming_h.at[:, pl.ds(capacity, hub_dev), :], hubs),
        (base_h, base),
    )
    wait_copies(copies)
    hub = hubs[0].astype(F32)
    for q in range(1, n_dom):
        hub += hubs[q].astype(F32)
    for j in range(hub_dev):
        base[pl.ds(hub_s[j], 1), :] += hub[j : j + 1, :]
    lane = lax.broadcasted_iota(jnp.int32, (1, capacity), 1)
    leaving = []
    for start in range(0, own_count, block):
        vertex = lax.broadcasted_iota(jnp.int32, (block, capacity), 0) + start
        total = base[start : start + block, :]
        for first in range(0, n_dom, peers):
            hot, rows = [], []
            for q in range(first, first + peers):
                wanted = jnp.where(lane < count_s[0, q], rows_s[q : q + 1, :], -1)
                hot.append((vertex == wanted).astype(F32).astype(BF16))
                rows.append(sent[q])
            total += jnp.dot(
                jnp.concatenate(hot, axis=1),
                jnp.concatenate(rows, axis=0),
                preferred_element_type=F32,
            )
        base[start : start + block, :] = total
        at = pl.ds(start, block)
        leaving.append(start_copies(out_sems.at[pl.ds(start // block, 1)], (base.at[at], out_h.at[at])))
    for copies in leaving:
        wait_copies(copies)


def finish(send_rows, send_count, hub_ids, incoming, base):
    n_dom, capacity = send_rows.shape
    hub_dev = hub_ids.shape[0]
    own_count, width = base.shape
    return pl.pallas_call(
        finish_kernel,
        out_shape=pltpu.HBM(base.shape, F32),
        in_specs=[VMEM, HBM, HBM, ANY, HBM],
        out_specs=HBM,
        scratch_shapes=[
            pltpu.SMEM(send_count.shape, jnp.int32),
            pltpu.SMEM(hub_ids.shape, jnp.int32),
            pltpu.VMEM((n_dom, capacity, width), BF16),
            pltpu.VMEM((n_dom, hub_dev, width), BF16),
            pltpu.VMEM(base.shape, F32),
            pltpu.SemaphoreType.DMA((5,)),
            pltpu.SemaphoreType.DMA((own_count // 256,)),
        ],
        compiler_params=params(),
        cost_estimate=cost(2 * base.size * send_rows.size, 1 << 22),
        name="finish",
    )(hbm(send_rows), hbm(send_count), hbm(hub_ids), incoming, hbm(base))


def cut_kernel(me_s, w_self, w_neigh, *outs):
    width = w_self.shape[1]
    own, near, far = outs
    for k, out in enumerate((own, near, far.at[0], far.at[1])):
        at = pl.ds(pl.multiple_of((me_s[0] ^ k) * width, width), width)
        out[0] = w_self[at, :]
        out[1] = w_neigh[at, :]


def cut_weights(me, w_self, w_neigh):
    width = w_self.shape[1]
    one = (2, width, width)
    return pl.pallas_call(
        cut_kernel,
        out_shape=tuple(pltpu.HBM(shape, BF16) for shape in (one, one, (2,) + one)),
        in_specs=[SMEM, VMEM, VMEM],
        out_specs=(VMEM,) * 3,
        compiler_params=params(),
        cost_estimate=cost(0, 1 << 20),
        name="cut_weights",
    )(me, hbm(w_self), hbm(w_neigh))


def half_kernel(parts, out):
    total = parts[0]
    for q in range(1, parts.shape[0]):
        total += parts[q]
    out[...] = total


def half_sum(parts):
    return pl.pallas_call(
        half_kernel,
        out_shape=pltpu.HBM(parts.shape[1:], F32),
        in_specs=[VMEM],
        out_specs=VMEM,
        compiler_params=params(),
        cost_estimate=cost(0, 1 << 20),
        name="half_sum",
    )(hbm(parts))


def sum_kernel(mine, other, out, bias):
    half, _, chunk, _ = out.shape
    for t in range(2):
        first = t * (chunk + 8)
        total = mine[first : first + chunk + 8, :] + other[first : first + chunk + 8, :]
        if t == 0:
            bias[...] = total[chunk : chunk + 1, :]
        rows = total[:chunk, :].astype(BF16)
        for j in range(half):
            out[j, t] = rows


def sum_parts(mine, other, half):
    rows, width = mine.shape
    return pl.pallas_call(
        sum_kernel,
        out_shape=(pltpu.HBM((half, 2, rows // 2 - 8, width), BF16), pltpu.HBM((1, width), F32)),
        in_specs=[VMEM, VMEM],
        out_specs=(VMEM, VMEM),
        compiler_params=params(),
        cost_estimate=cost(0, 1 << 20),
        name="sum_parts",
    )(hbm(mine), other)


def place_kernel(me_s, sums, self_out, neigh_out):
    rows, width = self_out.shape
    half, _, chunk, _ = sums.shape
    n = min(chunk, width)
    for row in range(0, 2 * rows, n):
        index, part = divmod(row, chunk)
        t, j = divmod(index, half)
        which, k = divmod(row // width, rows // width)
        at = pl.ds(pl.multiple_of((me_s[0] ^ k) * width + row % width, n), n)
        (self_out, neigh_out)[which][at, :] = sums[j, t, part : part + n, :].astype(F32)


def place_weights(me, sums, rows):
    width = sums.shape[-1]
    return pl.pallas_call(
        place_kernel,
        out_shape=(pltpu.HBM((rows, width), F32),) * 2,
        in_specs=[SMEM, VMEM],
        out_specs=(VMEM, VMEM),
        compiler_params=params(),
        cost_estimate=cost(0, 1 << 20),
        name="place_weights",
    )(me, sums)


def body(
    node_feats,
    edge_tiles,
    tile_dst,
    tile_src,
    hub_ids,
    send_rows,
    send_count,
    w_self,
    w_neigh,
    out_bias,
    grad_out,
    *,
    n_feat,
):
    own_count, width = node_feats.shape
    tile_size = edge_tiles.shape[1]
    listed = send_rows[0]
    n_dom, capacity = listed.shape
    hub_dev = hub_ids.shape[0]
    me = lax.axis_index("feat").astype(jnp.int32)
    me_s = me.reshape(1)
    far, near = 2, 1
    assert n_feat == 4
    far_blocks = n_dom * hub_dev // tile_size + n_dom

    def swap(x, k):
        return lax.ppermute(x, "feat", [(j, j ^ k) for j in range(n_feat)])

    feat_far = swap(node_feats, far)

    outgoing = pick(listed, send_count, hub_ids, node_feats)
    incoming = lax.all_to_all(outgoing, "dom", 0, 0, tiled=True)
    cut = cut_weights(me_s, w_self, w_neigh)
    own_feats, *cut = lax.optimization_barrier((node_feats.reshape(-1, tile_size, width), *cut))
    far_w = swap(cut[2], far)
    base, lists = own_tiles(tile_dst, tile_src, edge_tiles, own_feats, far_blocks)
    aggregated = far_tiles(lists, edge_tiles, incoming, base, far_blocks).reshape(own_count, width)

    aggregated, far_w = lax.optimization_barrier((aggregated, far_w))
    w_rows = [cut[0], swap(cut[1], near), far_w, swap(far_w, near)]
    agg_far = swap(aggregated, far)
    feat_far, aggregated = lax.optimization_barrier((feat_far, aggregated))
    feats = [hbm(node_feats), swap(node_feats, near), feat_far, swap(feat_far, near)]
    flops = 2 * own_count * n_feat * width * width
    rows_out = ((own_count, width), BF16)
    (own_part,) = stream_call(
        self_step,
        me_s,
        feats,
        [w_self, out_bias[None, :]],
        [((own_count, width), F32)],
        flops,
        "self_dense",
    )
    agg_far, own_part, *w_rows = lax.optimization_barrier((agg_far, own_part, *w_rows))
    aggs = [hbm(aggregated), swap(aggregated, near), agg_far, swap(agg_far, near)]
    output, grad_pre = stream_call(
        forward_step,
        me_s,
        [*aggs, hbm(own_part), hbm(grad_out)],
        [w_neigh],
        [rows_out, rows_out],
        flops,
        "forward_dense",
    )

    grad_far = swap(grad_pre, far)
    parts = weight_parts(feats + aggs, hbm(grad_pre), n_dom)
    half = n_dom // 2
    halves = [list(range(half)), list(range(half, n_dom))]
    parts = parts.reshape(half, -1, width)
    part_sums = lax.all_to_all(parts, "dom", 0, 0, axis_index_groups=halves, tiled=True)
    grads = [hbm(grad_pre), swap(grad_pre, near), grad_far, swap(grad_far, near)]

    back_out, back_agg, direct = back_far(
        lists, edge_tiles, grads, w_rows, n_dom, hub_dev, tile_size
    )
    back_in = lax.all_to_all(back_out, "dom", 0, 0, tiled=True)
    own = back_own(lists, edge_tiles, back_agg, direct).reshape(own_count, width)
    mine = half_sum(part_sums)
    other = lax.ppermute(mine, "dom", [(j, j ^ half) for j in range(n_dom)])
    other, own = lax.optimization_barrier((other, own))
    weights_out, grad_bias = sum_parts(mine, other, half)
    weights_out, back_in, own = lax.optimization_barrier((weights_out, back_in, own))
    weights_in = lax.all_to_all(weights_out, "dom", 0, 0, axis_index_groups=halves, tiled=True)
    grad_feats = finish(listed, send_count, hub_ids, back_in, own)
    grad_self, grad_neigh = place_weights(me_s, weights_in, n_feat * width)
    return (output, grad_feats, grad_self, grad_neigh, grad_bias[0])


def solution(mesh):
    in_specs = (
        P("dom", "feat"),
        P("dom", None, None),
        P("dom"),
        P("dom"),
        P("dom"),
        P("dom", None, None),
        P("dom", None),
        P(None, "feat"),
        P(None, "feat"),
        P("feat"),
        P("dom", "feat"),
    )
    out_specs = (P("dom", "feat"), P("dom", "feat"), P(None, "feat"), P(None, "feat"), P("feat"))
    n_feat = mesh.shape["feat"]

    def run(*args):
        return body(*args, n_feat=n_feat)

    return jax.shard_map(run, mesh=mesh, in_specs=in_specs, out_specs=out_specs, check_vma=False)
```
